256 devices in a mesh: gx: 32 (over x, z_hi, core), sec: 8 (over z_lo, y).
Axes of the slice: x: 4, y: 4, z: 8 (z_hi: 4, z_lo: 2; z = z_hi * 2 + z_lo), core: 2. Of those that a mesh axis runs over, the one named last changes fastest.
Arguments:
- state_init: float32 [16, 256, 64, 128], P(None, 'gx', 'sec'), may hold values from -6 to 6
- rock_type: int32 [256, 4096], P('gx', 'sec'), may hold values from 0 to 15
- perm_table: float32 [3, 16], replicated, may hold values from 0.2 to 1
- well_cells: int32 [256], replicated, may hold values from 0 to 1048575
- well_rate: float32 [16, 256], replicated, may hold values from -12 to 12
- basis_in: bfloat16 [256, 64, 128, 256], P(('gx', 'sec')), may hold values from -4 to 4
- singular: float32 [256], replicated, may hold values from 0.5 to 2
Outputs:
- state_out: float32 [16, 256, 64, 128], P(None, 'gx', 'sec')
- basis_out: bfloat16 [256, 64, 128, 256], P(('gx', 'sec'))
- singular_out: float32 [256], replicated
The draws below stay inside these ranges and needn't reach their ends.
All inputs are finite; a program needn't handle non-finite values.
Results may differ from the reference program's by a relative error of at most 0.0059.
Values may be sent and summed in bfloat16 or wider, within the bound.
A program may use at most 128 MiB of HBM per device.

```python
import math
import jax
import jax.numpy as jnp
from jax import lax

NZ = 64
K = 256
MG = 8
STEPS = 4
GROUPS = 2
ROCKS = 16
WELLS = 256
NX = 256
NY = 64
FZ = 128
SNAPS = 32
MEMB = 16
ROWS = 2097152
CELLS = 1048576


def basis_table(key):
    values = jax.random.normal(jax.random.fold_in(key, 11), (NX, NY, 2 * NZ, K), jnp.float32)
    partner = jax.random.permutation(jax.random.fold_in(key, 14), K)
    scales = jnp.exp(jax.random.uniform(jax.random.fold_in(key, 15), (K,), jnp.float32, math.log(0.6), math.log(1.4)))
    mixed = (values + 0.4 * jnp.take(values, partner, axis=-1)) * scales
    return jnp.clip(mixed, -4.0, 4.0)


def draw_basis_in(key, part):
    return basis_table(key).astype(jnp.bfloat16)


def draw_state_init(key, part):
    table = basis_table(key)
    mixing = jax.random.normal(jax.random.fold_in(key, 12), (MG * GROUPS, K), jnp.float32) * (1.5 / math.sqrt(K))
    aligned = jnp.einsum('xyfk,mk->mxyf', table, mixing)
    noise_key = jax.random.fold_in(key, 13)
    position = jnp.arange(NX, dtype=jnp.float32) / max(NX - 1, 1)
    ramp = 0.5 * jnp.exp(math.log(3.0) * position)
    rough = jax.random.normal(noise_key, (MG * GROUPS, NX, NY, 2 * NZ), jnp.float32)
    rough = rough * ramp[None, :, None, None]
    return jnp.clip(aligned + rough, -6.0, 6.0)


def with_ends(result, stream_key, least, high):
    extent = result.shape
    index_at = [jax.random.randint(jax.random.fold_in(stream_key, axis), (), 0, extent[axis]) for axis in range(len(extent))]
    result = result.at[tuple(index_at)].set(least)
    longest = extent.index(max(extent))
    index_at[longest] = (index_at[longest] + 1) % extent[longest]
    return result.at[tuple(index_at)].set(high)


def bell_draw(key, dims, width, limit, held_as=jnp.bfloat16):
    array = width * jax.random.normal(key, dims, jnp.float32)
    return jnp.clip(array, min=-limit, max=limit).astype(held_as)


def setup_inputs(seed: int = 0) -> dict:
    splits = jax.random.split(jax.random.key(seed), 8)
    state_init = draw_state_init(jax.random.fold_in(splits[7], 71), 0)
    rock_type = with_ends(jax.random.randint(splits[1], (NX, NY * NZ), 0, ROCKS), jax.random.fold_in(splits[1], 1), 0, ROCKS - 1).astype(jnp.int32)
    perm_table = jnp.clip(jnp.exp(jax.random.uniform(splits[2], (3, ROCKS), jnp.float32, math.log(0.2), math.log(1.0))), 0.2, 1.0)
    well_cells = with_ends(jax.random.randint(splits[3], (WELLS,), 0, NX * NY * NZ), jax.random.fold_in(splits[3], 1), 0, (NX * NY * NZ) - 1).astype(jnp.int32)
    well_rate = bell_draw(splits[4], (MEMB, WELLS), 3.0, 12.0, jnp.float32)
    basis_in = draw_basis_in(jax.random.fold_in(splits[7], 71), 0)
    singular = jnp.clip(jnp.exp(jax.random.uniform(splits[6], (K,), jnp.float32, math.log(0.5), math.log(2.0))), 0.5, 2.0)
    return {"state_init": state_init, "rock_type": rock_type, "perm_table": perm_table, "well_cells": well_cells, "well_rate": well_rate, "basis_in": basis_in, "singular": singular}


DT_PRESSURE = 0.12
DT_SATURATION = 0.06
DT_ADVECT = 0.15

def harmonic(left, right):
    return 2.0 * left * right / (left + right)

def shift_layers(fields):
    blank = jnp.zeros_like(fields[..., :1])
    return (jnp.concatenate([fields[..., 1:], blank], -1), jnp.concatenate([blank, fields[..., :-1]], -1))

def advance(fields, besides, weights, inflow, layers):
    column = lax.broadcasted_iota(jnp.int32, (fields.shape[-1],), 0)
    step_sizes = jnp.where(column < layers, DT_PRESSURE, DT_SATURATION)
    is_sat = (column >= layers).astype(fields.dtype)
    press_both = jnp.concatenate([fields[..., :layers], fields[..., :layers]], -1)
    spread = jnp.zeros_like(fields)
    carried = jnp.zeros_like(fields)
    for beside, weight in zip(besides, weights):
        spread = spread + weight * (beside - fields)
        beside_press = jnp.concatenate([beside[..., :layers], beside[..., :layers]], -1)
        pushed = weight * (beside_press - press_both)
        carried = carried + jnp.maximum(pushed, 0.0) * beside + jnp.minimum(pushed, 0.0) * fields
    return fields + step_sizes * spread + DT_ADVECT * is_sat * carried + DT_PRESSURE * inflow

def small_rotation(coeffs, lower, sigma):
    count = sigma.shape[0]
    extra = lower.shape[0]
    top = jnp.concatenate([jnp.diag(sigma), coeffs.T], 1)
    bottom = jnp.concatenate([jnp.zeros((extra, count), sigma.dtype), lower.T], 1)
    core = jnp.concatenate([top, bottom], 0)
    leading = jnp.dot(core, top.T, precision=lax.Precision.HIGHEST)
    inner = jnp.dot(leading.T, leading, precision=lax.Precision.HIGHEST)
    factor = jnp.linalg.cholesky(inner)
    rotation = lax.linalg.triangular_solve(factor, leading.T, left_side=True, lower=True).T
    energy = jnp.dot(core.T, rotation, precision=lax.Precision.HIGHEST)
    return (rotation, jnp.sqrt(lax.optimization_barrier(jnp.sum(energy * energy, axis=0))))

def compress(snaps, basis_now, sigma):
    flat_basis = basis_now.reshape(ROWS, K)
    coeffs = jnp.dot(snaps.astype(jnp.float32), flat_basis.astype(jnp.float32), preferred_element_type=jnp.float32) / ROWS
    rounded = coeffs.astype(jnp.bfloat16)
    resid = snaps.astype(jnp.float32) - lax.dot_general(rounded.astype(jnp.float32), flat_basis.astype(jnp.float32), (((1,), (1,)), ((), ())), preferred_element_type=jnp.float32)
    gram = jnp.dot(resid, resid.T, precision=lax.Precision.HIGHEST) / ROWS
    lower = jnp.linalg.cholesky(gram)
    ortho = lax.linalg.triangular_solve(lower, resid, left_side=True, lower=True).astype(jnp.bfloat16)
    rotation, sigma_next = small_rotation(coeffs, lower, sigma)
    mixing = rotation.astype(jnp.bfloat16)
    basis_blocks = basis_now.reshape(NX, NY * FZ, K)
    ortho_blocks = jnp.moveaxis(ortho.reshape(SNAPS, NX, NY * FZ), 1, 0)

    def rotate_block(pair):
        basis_block, ortho_block = pair
        value = jnp.dot(basis_block.astype(jnp.float32), mixing[:K].astype(jnp.float32), preferred_element_type=jnp.float32)
        value = value + lax.dot_general(ortho_block.astype(jnp.float32), mixing[K:].astype(jnp.float32), (((0,), (0,)), ((), ())), preferred_element_type=jnp.float32)
        return value.astype(jnp.bfloat16)
    fresh = lax.map(rotate_block, (basis_blocks, ortho_blocks))
    return (fresh.reshape(NX, NY, FZ, K), sigma_next)

def reference(state_init, rock_type, perm_table, well_cells, well_rate, basis_in, singular):
    kinds = lax.broadcasted_iota(jnp.int32, (ROCKS, 1, 1), 0)
    picks = (rock_type[None] == kinds).astype(perm_table.dtype)
    perm = jnp.einsum('dr,rxc->dxc', perm_table, picks, precision=lax.Precision.HIGHEST).reshape(3, NX, NY, NZ)
    padded = jnp.pad(perm, ((0, 0), (1, 1), (1, 1), (1, 1)))
    x_up = harmonic(perm[0], padded[0, 2:, 1:-1, 1:-1])
    x_down = harmonic(padded[0, :-2, 1:-1, 1:-1], perm[0])
    y_up = harmonic(perm[1], padded[1, 1:-1, 2:, 1:-1])
    y_down = harmonic(padded[1, 1:-1, :-2, 1:-1], perm[1])
    z_up = harmonic(perm[2], padded[2, 1:-1, 1:-1, 2:])
    z_down = harmonic(padded[2, 1:-1, 1:-1, :-2], perm[2])
    weights = [jnp.concatenate([face, face], -1) for face in (x_up, x_down, y_up, y_down, z_up, z_down)]
    source = jax.ops.segment_sum(well_rate.T, well_cells, num_segments=CELLS).T.reshape(MEMB, NX, NY, NZ)
    source_full = jnp.concatenate([source, jnp.zeros_like(source)], -1)
    basis_now = basis_in
    sigma = singular
    finals = []
    for group in range(GROUPS):
        fields = state_init[group * MG:(group + 1) * MG]
        inflow = source_full[group * MG:(group + 1) * MG]
        saved = []
        for step_index in range(STEPS):
            bordered = jnp.pad(fields, ((0, 0), (1, 1), (1, 1), (0, 0)))
            up_layer, down_layer = shift_layers(fields)
            besides = [bordered[:, 2:, 1:-1], bordered[:, :-2, 1:-1], bordered[:, 1:-1, 2:], bordered[:, 1:-1, :-2], up_layer, down_layer]
            fields = advance(fields, besides, weights, inflow, NZ)
            saved.append(fields.astype(jnp.bfloat16))
        finals.append(fields)
        snaps = jnp.concatenate(saved, 0).reshape(SNAPS, ROWS)
        basis_now, sigma = compress(snaps, basis_now, sigma)
    return (jnp.concatenate(finals, 0), basis_now, sigma)
```

```python
import jax
import jax.numpy as jnp
from jax import lax
from jax.sharding import PartitionSpec as P

MG = 8
STEPS = 4
GROUPS = 2


DT_PRESSURE = 0.12
DT_SATURATION = 0.06
DT_ADVECT = 0.15


def with_halo(block, sides, width):
    for axis, dim in sides:
        count = lax.axis_size(axis)
        forward = [(i, i + 1) for i in range(count - 1)]
        backward = [(target, source) for source, target in forward]
        low = lax.ppermute(
            lax.slice_in_dim(block, block.shape[dim] - width, None, axis=dim), axis, forward
        )
        high = lax.ppermute(lax.slice_in_dim(block, 0, width, axis=dim), axis, backward)
        block = jnp.concatenate([low, block, high], axis=dim)
    return block


def harmonic(left, right):
    return 2.0 * left * right / (left + right)


def shift_layers(fields):
    blank = jnp.zeros_like(fields[..., :1])
    return (
        jnp.concatenate([fields[..., 1:], blank], -1),
        jnp.concatenate([blank, fields[..., :-1]], -1),
    )


def advance(fields, besides, weights, inflow, layers):
    column = lax.broadcasted_iota(jnp.int32, (fields.shape[-1],), 0)
    step_sizes = jnp.where(column < layers, DT_PRESSURE, DT_SATURATION)
    is_sat = (column >= layers).astype(fields.dtype)
    press_both = jnp.concatenate([fields[..., :layers], fields[..., :layers]], -1)
    spread = jnp.zeros_like(fields)
    carried = jnp.zeros_like(fields)
    for beside, weight in zip(besides, weights):
        spread = spread + weight * (beside - fields)
        beside_press = jnp.concatenate([beside[..., :layers], beside[..., :layers]], -1)
        pushed = weight * (beside_press - press_both)
        carried = carried + jnp.maximum(pushed, 0.0) * beside + jnp.minimum(pushed, 0.0) * fields
    return fields + step_sizes * spread + DT_ADVECT * is_sat * carried + DT_PRESSURE * inflow


HIGH = lax.Precision.HIGHEST


def hdot(a, b):
    return jnp.dot(a, b, precision=HIGH)


def batch_update(coeffs, gram_of, sigma):
    rounded = coeffs.astype(jnp.bfloat16).astype(jnp.float32)
    gram = gram_of(coeffs, rounded)
    square = jnp.diag(sigma * sigma)
    total = square + hdot(coeffs.T, coeffs)
    inner = hdot(total, total) + hdot(coeffs.T, hdot(gram, coeffs))
    factor = jnp.linalg.cholesky(inner)
    eye = jnp.eye(sigma.shape[0], dtype=jnp.float32)
    back = lax.linalg.triangular_solve(factor, eye, left_side=True, lower=True).T
    top = sigma[:, None] * hdot(total, back)
    bottom = hdot(hdot(coeffs, total) + hdot(gram, coeffs), back)
    sigma_next = jnp.sqrt(jnp.sum(top * top, axis=0) + jnp.sum(bottom * bottom, axis=0))
    on_basis = hdot(square + hdot((coeffs - rounded).T, coeffs), back)
    on_snaps = hdot(coeffs, back)
    return on_basis, on_snaps, sigma_next


def small_algebra(uu, su, ss, sigma):
    half = su.shape[0] // 2
    s00, s10, s11 = ss[:half, :half], ss[half:, :half], ss[half:, half:]

    def gram_first(c, r):
        cr = hdot(c, r.T)
        return s00 - cr - cr.T + hdot(r, hdot(uu, r.T))

    wu, ws, sigma1 = batch_update(su[:half], gram_first, sigma)
    coeffs1 = hdot(su[half:], wu) + hdot(s10, ws)

    def gram_second(c, r):
        cr = hdot(c, r.T)
        yu, ys = hdot(wu, r.T), hdot(ws, r.T)
        mixed = hdot(ys.T, hdot(su[:half], yu))
        own = hdot(yu.T, hdot(uu, yu)) + mixed + mixed.T + hdot(ys.T, hdot(s00, ys))
        return s11 - cr - cr.T + own

    wu1, ws1, sigma2 = batch_update(coeffs1, gram_second, sigma1)
    return hdot(wu, wu1), hdot(ws, wu1), ws1, sigma2


def body(state_init, rock_type, perm_table, well_cells, well_rate, basis_in, singular):
    across = state_init.shape[1]
    along = state_init.shape[2]
    layers = state_init.shape[3] // 2
    sec_count = lax.axis_size("sec")
    rock_count = perm_table.shape[1]
    kinds = lax.broadcasted_iota(jnp.int32, (rock_count, 1, 1), 0)
    picks = (rock_type[None] == kinds).astype(jnp.float32)
    perm = jnp.einsum("dr,rxc->dxc", perm_table, picks, precision=lax.Precision.HIGHEST).reshape(
        3, across, along, layers
    )
    paired = jnp.concatenate([perm[0], perm[1]], -1)
    bordered_perm = with_halo(paired.astype(jnp.bfloat16), (("gx", 0), ("sec", 1)), 1).astype(
        paired.dtype
    )
    perm_xh = bordered_perm[..., :layers]
    perm_yh = bordered_perm[..., layers:]
    x_up = harmonic(perm[0], perm_xh[2:, 1:-1])
    x_down = harmonic(perm_xh[:-2, 1:-1], perm[0])
    y_up = harmonic(perm[1], perm_yh[1:-1, 2:])
    y_down = harmonic(perm_yh[1:-1, :-2], perm[1])
    z_padded = jnp.pad(perm[2], ((0, 0), (0, 0), (1, 1)))
    z_up = harmonic(perm[2], z_padded[..., 2:])
    z_down = harmonic(z_padded[..., :-2], perm[2])
    weights = [
        jnp.concatenate([face, face], -1) for face in (x_up, x_down, y_up, y_down, z_up, z_down)
    ]
    x_start = lax.axis_index("gx") * across
    y_start = lax.axis_index("sec") * along
    total_y = along * sec_count
    x_pos = lax.broadcasted_iota(jnp.int32, (across, along, layers), 0)
    y_pos = lax.broadcasted_iota(jnp.int32, (across, along, layers), 1)
    z_pos = lax.broadcasted_iota(jnp.int32, (across, along, layers), 2)
    cell_ids = ((x_start + x_pos) * total_y + y_start + y_pos) * layers + z_pos
    hits = (well_cells[:, None] == cell_ids.reshape(1, -1)).astype(jnp.float32)
    source = jnp.dot(well_rate, hits, precision=lax.Precision.HIGHEST).reshape(
        state_init.shape[0], across, along, layers
    )
    source_full = jnp.concatenate([source, jnp.zeros_like(source)], -1)
    local_rows = basis_in.shape[0] * basis_in.shape[1] * basis_in.shape[2]
    rows_total = local_rows * lax.axis_size("gx") * sec_count
    finals = []
    snaps = []
    for group in range(GROUPS):
        fields = state_init[group * MG : (group + 1) * MG]
        inflow = source_full[group * MG : (group + 1) * MG]
        saved = []
        for step_index in range(STEPS):
            bordered = with_halo(fields.astype(jnp.bfloat16), (("gx", 1), ("sec", 2)), 1).astype(
                fields.dtype
            )
            up_layer, down_layer = shift_layers(fields)
            besides = [
                bordered[:, 2:, 1:-1],
                bordered[:, :-2, 1:-1],
                bordered[:, 1:-1, 2:],
                bordered[:, 1:-1, :-2],
                up_layer,
                down_layer,
            ]
            fields = advance(fields, besides, weights, inflow, layers)
            snapshot = fields.astype(jnp.bfloat16)
            saved.append(snapshot)
        finals.append(fields)
        stacked = jnp.concatenate(saved, 0)
        stacked = lax.all_to_all(stacked, "sec", split_axis=1, concat_axis=2, tiled=True)
        snaps.append(stacked.reshape(stacked.shape[0], -1))
    both = jnp.concatenate(snaps, 0)
    basis = basis_in.reshape(both.shape[1], basis_in.shape[-1])
    count = basis.shape[1]
    uu = lax.dot_general(basis, basis, (((0,), (0,)), ((), ())), preferred_element_type=jnp.float32)
    su = jnp.dot(both, basis, preferred_element_type=jnp.float32)
    ss = lax.dot_general(both, both, (((1,), (1,)), ((), ())), preferred_element_type=jnp.float32)
    local = jnp.concatenate([jnp.concatenate([uu, su], 0), jnp.pad(jnp.concatenate([jnp.zeros((count, both.shape[0]), jnp.float32), ss], 0), ((0, 0), (0, 64)))], 1)
    whole = lax.psum(local, ("gx", "sec")) / rows_total
    w0, w1, w2, sigma = small_algebra(
        whole[:count, :count], whole[count:, :count], whole[count:, count : count + both.shape[0]], singular
    )
    fresh = jnp.dot(basis, w0.astype(jnp.bfloat16), preferred_element_type=jnp.float32)
    fresh = fresh + lax.dot_general(
        both, jnp.concatenate([w1, w2], 0).astype(jnp.bfloat16), (((0,), (0,)), ((), ())), preferred_element_type=jnp.float32
    )
    basis_now = fresh.astype(jnp.bfloat16).reshape(basis_in.shape)
    return (jnp.concatenate(finals, 0), basis_now, sigma)


def solution(mesh):
    return jax.shard_map(
        body,
        mesh=mesh,
        in_specs=(
            P(None, "gx", "sec", None),
            P("gx", "sec"),
            P(),
            P(),
            P(),
            P(("gx", "sec"), None, None, None),
            P(),
        ),
        out_specs=(P(None, "gx", "sec", None), P(("gx", "sec"), None, None, None), P()),
        check_vma=False,
    )
```

```python
import jax
import jax.numpy as jnp
from jax import lax
from jax.experimental import pallas as pl
from jax.experimental.pallas import tpu as pltpu
from jax.sharding import PartitionSpec as P

MG = 8
STEPS = 4
GROUPS = 2
MEMB = MG * GROUPS

DT_PRESSURE = 0.12
DT_SATURATION = 0.06
DT_ADVECT = 0.15

MESH = pl.DeviceIdType.MESH
VMEM = pltpu.VMEM
F32 = jnp.float32
BF16 = jnp.bfloat16


def harmonic(left, right):
    return 2.0 * left * right / (left + right)


def remote(src, dst, send_sem, recv_sem, device):
    return pltpu.make_async_remote_copy(
        src_ref=src, dst_ref=dst, send_sem=send_sem, recv_sem=recv_sem, device_id=device, device_id_type=MESH
    )


def flux_kernel(
    table_ref, state_ref, rock_ref, inflow_ref, out_ref, snaps_ref,
    perm_send, perm_recv, x_send, x_recv, y_send, y_recv, y_wide, weights, turned, packed,
    ps_sem, pr_sem, hs_sem, hr_sem, ss_sem, sr_sem, own_sem,
):
    gx_count, sec_count = lax.axis_size("gx"), lax.axis_size("sec")
    gx, sec = lax.axis_index("gx"), lax.axis_index("sec")
    beside = (
        {"gx": lax.rem(gx + gx_count - 1, gx_count)},
        {"gx": lax.rem(gx + 1, gx_count)},
        {"sec": lax.rem(sec + sec_count - 1, sec_count)},
        {"sec": lax.rem(sec + 1, sec_count)},
    )
    barrier = pltpu.get_barrier_semaphore()
    for device in beside[:2]:
        pl.semaphore_signal(barrier, inc=1, device_id=device, device_id_type=MESH)
    for ahead in range(1, sec_count):
        pl.semaphore_signal(
            barrier, inc=1, device_id={"sec": lax.rem(sec + ahead, sec_count)}, device_id_type=MESH
        )

    lane = lax.broadcasted_iota(jnp.int32, (8, 128), 1)
    row = lax.broadcasted_iota(jnp.int32, (8, 128), 0)

    perm = [[], [], []]
    for x in range(8):
        kind = rock_ref[x]
        for d in range(3):
            value = jnp.full((8, 128), table_ref[d, 0], F32)
            for r in range(1, 16):
                value = jnp.where(kind == r, table_ref[d, r], value)
            perm[d].append(value)
    perm_send[0] = perm[0][0]
    perm_send[1] = perm[0][7]
    for x in range(8):
        perm_send[2, pl.ds(x, 1), :] = perm[1][x][0:1]
        perm_send[3, pl.ds(x, 1), :] = perm[1][x][7:8]

    def halo_copies(step):
        pairs = []
        for d in range(4):
            send = (x_send if d < 2 else y_send).at[step, d % 2]
            recv = (x_recv if d < 2 else y_recv).at[step, 1 - d % 2]
            pairs.append(remote(send, recv, hs_sem.at[step, d], hr_sem.at[step, d ^ 1], beside[d]))
        return pairs

    def stage_y(step):
        y_send[step, 0] = out_ref[pl.ds(0, 128, stride=8), :].astype(BF16)
        y_send[step, 1] = out_ref[pl.ds(7, 128, stride=8), :].astype(BF16)

    def first(m, carry):
        x_send[0, 0, m] = state_ref[m, 0].astype(BF16)
        x_send[0, 1, m] = state_ref[m, 7].astype(BF16)
        for x in range(8):
            out_ref[pl.ds(pl.multiple_of(m * 64 + x * 8, 8), 8), :] = state_ref[m, x]
        return carry

    lax.fori_loop(0, MEMB, first, 0)
    stage_y(0)
    pl.semaphore_wait(barrier, 1 + sec_count)
    perm_copies = [
        remote(perm_send.at[d], perm_recv.at[d ^ 1], ps_sem.at[d], pr_sem.at[d ^ 1], beside[d]) for d in range(4)
    ]
    for copy in perm_copies:
        copy.start()
    flying = halo_copies(0)
    for copy in flying:
        copy.start()

    z_up = jnp.where((lane & 63) == 63, 0.0, 1.0)
    z_down = jnp.where((lane & 63) == 0, 0.0, 1.0)
    for x in range(8):
        weights[4, x] = z_up * harmonic(perm[2][x], pltpu.roll(perm[2][x], 127, 1))
        weights[5, x] = z_down * harmonic(perm[2][x], pltpu.roll(perm[2][x], 1, 1))
    for copy in perm_copies:
        copy.wait()
    not_first_x = jnp.where(gx == 0, 0.0, 1.0)
    not_last_x = jnp.where(gx == gx_count - 1, 0.0, 1.0)
    not_first_y = jnp.where(sec == 0, 0.0, 1.0)
    not_last_y = jnp.where(sec == sec_count - 1, 0.0, 1.0)
    for x in range(8):
        above = perm[0][x + 1] if x < 7 else perm_recv[1] * not_last_x
        below = perm[0][x - 1] if x > 0 else perm_recv[0] * not_first_x
        weights[0, x] = harmonic(perm[0][x], above)
        weights[1, x] = harmonic(below, perm[0][x])
        right = jnp.broadcast_to(perm_recv[3, pl.ds(x, 1), :] * not_last_y, (8, 128))
        left = jnp.broadcast_to(perm_recv[2, pl.ds(x, 1), :] * not_first_y, (8, 128))
        weights[2, x] = harmonic(perm[1][x], jnp.where(row == 7, right, pltpu.roll(perm[1][x], 7, 0)))
        weights[3, x] = harmonic(jnp.where(row == 0, left, pltpu.roll(perm[1][x], 1, 0)), perm[1][x])

    step_sizes = jnp.where(lane < 64, DT_PRESSURE, DT_SATURATION)
    advect = jnp.where(lane < 64, 0.0, DT_ADVECT)
    sent = []
    for step in range(STEPS):
        for copy in flying:
            copy.wait()
        y_wide[0] = y_recv[step, 0].astype(F32)
        y_wide[1] = y_recv[step, 1].astype(F32)

        def member(m, carry):
            base = pl.multiple_of(m * 64, 64)
            old = [out_ref[pl.ds(base + x * 8, 8), :] for x in range(8)]
            old_below = x_recv[step, 0, m].astype(F32)
            old_above = x_recv[step, 1, m].astype(F32)
            for x in range(8):
                here = old[x]
                left = jnp.broadcast_to(y_wide[0, pl.ds(m * 8 + x, 1), :], (8, 128))
                right = jnp.broadcast_to(y_wide[1, pl.ds(m * 8 + x, 1), :], (8, 128))
                besides = (
                    old[x + 1] if x < 7 else old_above,
                    old[x - 1] if x > 0 else old_below,
                    jnp.where(row == 7, right, pltpu.roll(here, 7, 0)),
                    jnp.where(row == 0, left, pltpu.roll(here, 1, 0)),
                    pltpu.roll(here, 127, 1),
                    pltpu.roll(here, 1, 1),
                )
                spread = carried = None
                for d in range(6):
                    flow = weights[d, x] * (besides[d] - here)
                    pushed = pltpu.roll(flow, 64, 1)
                    moved = pushed * jnp.where(pushed > 0.0, besides[d], here)
                    spread = flow if spread is None else spread + flow
                    carried = moved if carried is None else carried + moved
                fresh = here + step_sizes * spread + advect * carried + DT_PRESSURE * inflow_ref[m, x]
                out_ref[pl.ds(base + x * 8, 8), :] = fresh
                turned[x, pl.ds(m, 8, stride=MEMB), :] = fresh
                if step + 1 < STEPS and x in (0, 7):
                    x_send[step + 1, x // 7, m] = fresh.astype(BF16)
            return carry

        lax.fori_loop(0, MEMB, member, 0)
        if step + 1 < STEPS:
            stage_y(step + 1)
            flying = halo_copies(step + 1)
            for copy in flying:
                copy.start()
        for x in range(8):
            packed[step, x] = turned[x].reshape(8, MEMB, 128).astype(BF16)
        mine = pltpu.make_async_copy(
            packed.at[step, sec], snaps_ref.at[step, pl.ds(sec * 8, 8)], own_sem.at[step]
        )
        mine.start()
        sent.append(mine)
        for ahead in range(1, sec_count):
            target = lax.rem(sec + ahead, sec_count)
            copy = remote(
                packed.at[step, target], snaps_ref.at[step, pl.ds(sec * 8, 8)],
                ss_sem.at[step, ahead], sr_sem.at[step, ahead], {"sec": target},
            )
            copy.start()
            sent.append(copy)
    for copy in sent:
        copy.wait()


def flux(table, state, rock, inflow):
    sec_count = lax.axis_size("sec")
    dma = pltpu.SemaphoreType.DMA
    return pl.pallas_call(
        flux_kernel,
        out_shape=(
            jax.ShapeDtypeStruct((MEMB * 64, 128), F32),
            jax.ShapeDtypeStruct((STEPS, 8 * sec_count, MEMB, 128), BF16),
        ),
        in_specs=[
            pl.BlockSpec(memory_space=pltpu.SMEM),
            pl.BlockSpec(memory_space=VMEM),
            pl.BlockSpec(memory_space=VMEM),
            pl.BlockSpec(memory_space=VMEM),
        ],
        out_specs=(pl.BlockSpec(memory_space=VMEM), pl.BlockSpec(memory_space=VMEM)),
        scratch_shapes=[
            VMEM((4, 8, 128), F32),
            VMEM((4, 8, 128), F32),
            VMEM((STEPS, 2, MEMB, 8, 128), BF16),
            VMEM((STEPS, 2, MEMB, 8, 128), BF16),
            VMEM((STEPS, 2, MEMB * 8, 128), BF16),
            VMEM((STEPS, 2, MEMB * 8, 128), BF16),
            VMEM((2, MEMB * 8, 128), F32),
            VMEM((6, 8, 8, 128), F32),
            VMEM((8, 8 * MEMB, 128), F32),
            VMEM((STEPS, 8, 8, MEMB, 128), BF16),
            dma((4,)), dma((4,)), dma((STEPS, 4)), dma((STEPS, 4)),
            dma((STEPS, sec_count)), dma((STEPS, sec_count)), dma((STEPS,)),
        ],
        compiler_params=pltpu.CompilerParams(
            collective_id=0, has_side_effects=True, vmem_limit_bytes=32 * 1024 * 1024
        ),
        name="flux",
    )(table, state, rock, inflow)


PLANE = 32
COLUMN = 8


def reduce_kernel(x_ref, out_ref, slots, partial, column, send1, recv1, send2, recv2, send3, recv3):
    gx, sec = lax.axis_index("gx"), lax.axis_index("sec")
    z_hi, z_lo = lax.rem(gx // 2, 4), sec // 4
    me = (gx // 8) * 8 + lax.rem(gx, 2) * 4 + lax.rem(sec, 4)
    me_z = z_hi * 2 + z_lo

    def in_plane(p):
        return {"gx": (p // 8) * 8 + z_hi * 2 + lax.rem(p // 4, 2), "sec": z_lo * 4 + lax.rem(p, 4)}

    def in_column(q):
        return {"gx": (gx // 8) * 8 + (q // 2) * 2 + lax.rem(gx, 2), "sec": lax.rem(q, 2) * 4 + lax.rem(sec, 4)}

    barrier = pltpu.get_barrier_semaphore()
    for k in range(1, PLANE):
        pl.semaphore_signal(barrier, inc=1, device_id=in_plane(lax.rem(me + k, PLANE)), device_id_type=MESH)
    for k in range(1, COLUMN):
        pl.semaphore_signal(barrier, inc=1, device_id=in_column(lax.rem(me_z + k, COLUMN)), device_id_type=MESH)
    slots[me] = x_ref[me]
    pl.semaphore_wait(barrier, PLANE + COLUMN - 2)

    def scatter(k):
        p = lax.rem(me + k, PLANE)
        return remote(x_ref.at[p], slots.at[me], send1.at[k], recv1.at[k], in_plane(p))

    for k in range(1, PLANE):
        scatter(k).start()
    for k in range(1, PLANE):
        scatter(k).wait()
    total = slots[0]
    for k in range(1, PLANE):
        total = total + slots[k]
    partial[...] = total
    column[me_z] = total

    def across(k):
        q = lax.rem(me_z + k, COLUMN)
        return remote(partial, column.at[me_z], send2.at[k], recv2.at[k], in_column(q))

    for k in range(1, COLUMN):
        across(k).start()
    for k in range(1, COLUMN):
        across(k).wait()
    total = column[0]
    for k in range(1, COLUMN):
        total = total + column[k]
    out_ref[me] = total

    def gather(k):
        p = lax.rem(me + k, PLANE)
        return remote(out_ref.at[me], out_ref.at[me], send3.at[k], recv3.at[k], in_plane(p))

    for k in range(1, PLANE):
        gather(k).start()
    for k in range(1, PLANE):
        gather(k).wait()


def all_sum(x):
    rows = x.shape[0] // PLANE
    dma = pltpu.SemaphoreType.DMA
    out = pl.pallas_call(
        reduce_kernel,
        out_shape=jax.ShapeDtypeStruct((PLANE, rows, 128), F32),
        in_specs=[pl.BlockSpec(memory_space=VMEM)],
        out_specs=pl.BlockSpec(memory_space=VMEM),
        scratch_shapes=[
            VMEM((PLANE, rows, 128), F32), VMEM((rows, 128), F32), VMEM((COLUMN, rows, 128), F32),
            dma((PLANE,)), dma((PLANE,)), dma((COLUMN,)), dma((COLUMN,)), dma((PLANE,)), dma((PLANE,)),
        ],
        compiler_params=pltpu.CompilerParams(
            collective_id=1, has_side_effects=True, vmem_limit_bytes=16 * 1024 * 1024
        ),
        name="all_sum",
    )(x.reshape(PLANE, rows, 128))
    return out.reshape(x.shape)


HIGH = lax.Precision.HIGHEST


def hdot(a, b):
    return jnp.dot(a, b, precision=HIGH)


def batch_update(coeffs, gram_of, sigma):
    rounded = coeffs.astype(jnp.bfloat16).astype(jnp.float32)
    gram = gram_of(coeffs, rounded)
    square = jnp.diag(sigma * sigma)
    total = square + hdot(coeffs.T, coeffs)
    inner = hdot(total, total) + hdot(coeffs.T, hdot(gram, coeffs))
    factor = jnp.linalg.cholesky(inner)
    eye = jnp.eye(sigma.shape[0], dtype=jnp.float32)
    back = lax.linalg.triangular_solve(factor, eye, left_side=True, lower=True).T
    top = sigma[:, None] * hdot(total, back)
    bottom = hdot(hdot(coeffs, total) + hdot(gram, coeffs), back)
    sigma_next = jnp.sqrt(jnp.sum(top * top, axis=0) + jnp.sum(bottom * bottom, axis=0))
    on_basis = hdot(square + hdot((coeffs - rounded).T, coeffs), back)
    on_snaps = hdot(coeffs, back)
    return on_basis, on_snaps, sigma_next


def small_algebra(uu, su, ss, sigma):
    half = su.shape[0] // 2
    s00, s10, s11 = ss[:half, :half], ss[half:, :half], ss[half:, half:]

    def gram_first(c, r):
        cr = hdot(c, r.T)
        return s00 - cr - cr.T + hdot(r, hdot(uu, r.T))

    wu, ws, sigma1 = batch_update(su[:half], gram_first, sigma)
    coeffs1 = hdot(su[half:], wu) + hdot(s10, ws)

    def gram_second(c, r):
        cr = hdot(c, r.T)
        yu, ys = hdot(wu, r.T), hdot(ws, r.T)
        mixed = hdot(ys.T, hdot(su[:half], yu))
        own = hdot(yu.T, hdot(uu, yu)) + mixed + mixed.T + hdot(ys.T, hdot(s00, ys))
        return s11 - cr - cr.T + own

    wu1, ws1, sigma2 = batch_update(coeffs1, gram_second, sigma1)
    return hdot(wu, wu1), hdot(ws, wu1), ws1, sigma2


def body(state_init, rock_type, perm_table, well_cells, well_rate, basis_in, singular):
    members, across, along, width = state_init.shape
    layers = width // 2
    sec_count = lax.axis_size("sec")
    rock = rock_type.reshape(across, along, layers)
    rock = jnp.concatenate([rock, rock], -1)
    x_start = lax.axis_index("gx") * across
    y_start = lax.axis_index("sec") * along
    total_y = along * sec_count
    x_pos = lax.broadcasted_iota(jnp.int32, (across, along, layers), 0)
    y_pos = lax.broadcasted_iota(jnp.int32, (across, along, layers), 1)
    z_pos = lax.broadcasted_iota(jnp.int32, (across, along, layers), 2)
    cell_ids = ((x_start + x_pos) * total_y + y_start + y_pos) * layers + z_pos
    hits = (well_cells[:, None] == cell_ids.reshape(1, -1)).astype(jnp.float32)
    source = jnp.dot(well_rate, hits, precision=HIGH).reshape(members, across, along, layers)
    source_full = jnp.concatenate([source, jnp.zeros_like(source)], -1)
    rows_total = basis_in.size // basis_in.shape[-1] * lax.axis_size("gx") * sec_count

    final, snaps = flux(perm_table, state_init, rock, source_full)
    state_out = final.reshape(state_init.shape)

    both = snaps.reshape(STEPS, -1, GROUPS, MG, width).transpose(2, 0, 3, 1, 4).reshape(GROUPS * STEPS * MG, -1)
    basis = basis_in.reshape(both.shape[1], basis_in.shape[-1])
    count = basis.shape[1]
    taken = both.shape[0]
    uu = lax.dot_general(basis, basis, (((0,), (0,)), ((), ())), preferred_element_type=jnp.float32)
    su = jnp.dot(both, basis, preferred_element_type=jnp.float32)
    ss = lax.dot_general(both, both, (((1,), (1,)), ((), ())), preferred_element_type=jnp.float32)
    local = jnp.concatenate(
        [
            su[:, :128],
            su[:, 128:],
            uu[:64, :128],
            uu[:64, 128:],
            uu[64:128, 128:],
            uu[128:192, 128:],
            jnp.concatenate([uu[64:128, 64:128], uu[192:, 192:]], 1),
            jnp.pad(ss, ((0, 0), (0, 64))),
        ],
        0,
    )
    whole = all_sum(local) / rows_total
    part = [whole[64 * i : 64 * (i + 1)] for i in range(8)]
    su = jnp.concatenate([part[0], part[1]], 1)
    row0 = jnp.concatenate([part[2], part[3]], 1)
    row1 = jnp.concatenate([row0[:, 64:128].T, part[6][:, :64], part[4]], 1)
    row2 = jnp.concatenate([row0[:, 128:192].T, row1[:, 128:192].T, part[5]], 1)
    row3 = jnp.concatenate([row0[:, 192:].T, row1[:, 192:].T, row2[:, 192:].T, part[6][:, 64:]], 1)
    uu = jnp.concatenate([row0, row1, row2, row3], 0)
    ss = part[7][:, :64]
    w0, w1, w2, sigma = small_algebra(uu, su, ss, singular)
    fresh = jnp.dot(basis, w0.astype(jnp.bfloat16), preferred_element_type=jnp.float32)
    fresh = fresh + lax.dot_general(
        both, jnp.concatenate([w1, w2], 0).astype(jnp.bfloat16), (((0,), (0,)), ((), ())), preferred_element_type=jnp.float32
    )
    return (state_out, fresh.astype(jnp.bfloat16).reshape(basis_in.shape), sigma)


def solution(mesh):
    return jax.shard_map(
        body,
        mesh=mesh,
        in_specs=(
            P(None, "gx", "sec", None),
            P("gx", "sec"),
            P(),
            P(),
            P(),
            P(("gx", "sec"), None, None, None),
            P(),
        ),
        out_specs=(P(None, "gx", "sec", None), P(("gx", "sec"), None, None, None), P()),
        check_vma=False,
    )
```

```python
import jax
import jax.numpy as jnp
from jax import lax
from jax.experimental import pallas as pl
from jax.experimental.pallas import tpu as pltpu
from jax.sharding import PartitionSpec as P

MG = 8
STEPS = 4
GROUPS = 2
MEMB = MG * GROUPS

DT_PRESSURE = 0.12
DT_SATURATION = 0.06
DT_ADVECT = 0.15

MESH = pl.DeviceIdType.MESH
VMEM = pltpu.VMEM
F32 = jnp.float32
BF16 = jnp.bfloat16


def harmonic(left, right):
    return 2.0 * left * right / (left + right)


def remote(src, dst, send_sem, recv_sem, device):
    return pltpu.make_async_remote_copy(
        src_ref=src, dst_ref=dst, send_sem=send_sem, recv_sem=recv_sem, device_id=device, device_id_type=MESH
    )


def flux_kernel(
    table_ref, state_ref, rock_ref, inflow_ref, out_ref, snaps_ref,
    perm_send, perm_recv, x_send, x_recv, y_send, y_recv, y_wide, weights, turned, packed,
    ps_sem, pr_sem, hs_sem, hr_sem, ss_sem, sr_sem, own_sem,
):
    gx_count, sec_count = lax.axis_size("gx"), lax.axis_size("sec")
    gx, sec = lax.axis_index("gx"), lax.axis_index("sec")
    beside = (
        {"gx": lax.rem(gx + gx_count - 1, gx_count)},
        {"gx": lax.rem(gx + 1, gx_count)},
        {"sec": lax.rem(sec + sec_count - 1, sec_count)},
        {"sec": lax.rem(sec + 1, sec_count)},
    )
    barrier = pltpu.get_barrier_semaphore()
    for device in beside[:2]:
        pl.semaphore_signal(barrier, inc=1, device_id=device, device_id_type=MESH)
    for ahead in range(1, sec_count):
        pl.semaphore_signal(
            barrier, inc=1, device_id={"sec": lax.rem(sec + ahead, sec_count)}, device_id_type=MESH
        )

    lane = lax.broadcasted_iota(jnp.int32, (8, 128), 1)
    row = lax.broadcasted_iota(jnp.int32, (8, 128), 0)

    perm = [[], [], []]
    for x in range(8):
        kind = rock_ref[x]
        for d in range(3):
            value = jnp.full((8, 128), table_ref[d, 0], F32)
            for r in range(1, 16):
                value = jnp.where(kind == r, table_ref[d, r], value)
            perm[d].append(value)
    perm_send[0] = perm[0][0]
    perm_send[1] = perm[0][7]
    for x in range(8):
        perm_send[2, pl.ds(x, 1), :] = perm[1][x][0:1]
        perm_send[3, pl.ds(x, 1), :] = perm[1][x][7:8]

    def halo_copies(step):
        pairs = []
        for d in range(4):
            send = (x_send if d < 2 else y_send).at[step, d % 2]
            recv = (x_recv if d < 2 else y_recv).at[step, 1 - d % 2]
            pairs.append(remote(send, recv, hs_sem.at[step, d], hr_sem.at[step, d ^ 1], beside[d]))
        return pairs

    def stage_y(step):
        y_send[step, 0] = out_ref[pl.ds(0, 128, stride=8), :].astype(BF16)
        y_send[step, 1] = out_ref[pl.ds(7, 128, stride=8), :].astype(BF16)

    def first(m, carry):
        x_send[0, 0, m] = state_ref[m, 0].astype(BF16)
        x_send[0, 1, m] = state_ref[m, 7].astype(BF16)
        for x in range(8):
            out_ref[pl.ds(pl.multiple_of(m * 64 + x * 8, 8), 8), :] = state_ref[m, x]
        return carry

    lax.fori_loop(0, MEMB, first, 0)
    stage_y(0)
    pl.semaphore_wait(barrier, 1 + sec_count)
    perm_copies = [
        remote(perm_send.at[d], perm_recv.at[d ^ 1], ps_sem.at[d], pr_sem.at[d ^ 1], beside[d]) for d in range(4)
    ]
    for copy in perm_copies:
        copy.start()
    flying = halo_copies(0)
    for copy in flying:
        copy.start()

    z_up = jnp.where((lane & 63) == 63, 0.0, 1.0)
    z_down = jnp.where((lane & 63) == 0, 0.0, 1.0)
    for x in range(8):
        weights[4, x] = z_up * harmonic(perm[2][x], pltpu.roll(perm[2][x], 127, 1))
        weights[5, x] = z_down * harmonic(perm[2][x], pltpu.roll(perm[2][x], 1, 1))
    for copy in perm_copies:
        copy.wait()
    not_first_x = jnp.where(gx == 0, 0.0, 1.0)
    not_last_x = jnp.where(gx == gx_count - 1, 0.0, 1.0)
    not_first_y = jnp.where(sec == 0, 0.0, 1.0)
    not_last_y = jnp.where(sec == sec_count - 1, 0.0, 1.0)
    for x in range(8):
        above = perm[0][x + 1] if x < 7 else perm_recv[1] * not_last_x
        below = perm[0][x - 1] if x > 0 else perm_recv[0] * not_first_x
        weights[0, x] = harmonic(perm[0][x], above)
        weights[1, x] = harmonic(below, perm[0][x])
        right = jnp.broadcast_to(perm_recv[3, pl.ds(x, 1), :] * not_last_y, (8, 128))
        left = jnp.broadcast_to(perm_recv[2, pl.ds(x, 1), :] * not_first_y, (8, 128))
        weights[2, x] = harmonic(perm[1][x], jnp.where(row == 7, right, pltpu.roll(perm[1][x], 7, 0)))
        weights[3, x] = harmonic(jnp.where(row == 0, left, pltpu.roll(perm[1][x], 1, 0)), perm[1][x])

    step_sizes = jnp.where(lane < 64, DT_PRESSURE, DT_SATURATION)
    advect = jnp.where(lane < 64, 0.0, DT_ADVECT)
    sent = []
    for step in range(STEPS):
        for copy in flying:
            copy.wait()
        y_wide[0] = y_recv[step, 0].astype(F32)
        y_wide[1] = y_recv[step, 1].astype(F32)

        def member(m, carry):
            base = pl.multiple_of(m * 64, 64)
            old = [out_ref[pl.ds(base + x * 8, 8), :] for x in range(8)]
            old_below = x_recv[step, 0, m].astype(F32)
            old_above = x_recv[step, 1, m].astype(F32)
            for x in range(8):
                here = old[x]
                left = jnp.broadcast_to(y_wide[0, pl.ds(m * 8 + x, 1), :], (8, 128))
                right = jnp.broadcast_to(y_wide[1, pl.ds(m * 8 + x, 1), :], (8, 128))
                besides = (
                    old[x + 1] if x < 7 else old_above,
                    old[x - 1] if x > 0 else old_below,
                    jnp.where(row == 7, right, pltpu.roll(here, 7, 0)),
                    jnp.where(row == 0, left, pltpu.roll(here, 1, 0)),
                    pltpu.roll(here, 127, 1),
                    pltpu.roll(here, 1, 1),
                )
                spread = carried = None
                for d in range(6):
                    flow = weights[d, x] * (besides[d] - here)
                    pushed = pltpu.roll(flow, 64, 1)
                    moved = pushed * jnp.where(pushed > 0.0, besides[d], here)
                    spread = flow if spread is None else spread + flow
                    carried = moved if carried is None else carried + moved
                fresh = here + step_sizes * spread + advect * carried + DT_PRESSURE * inflow_ref[m, x]
                out_ref[pl.ds(base + x * 8, 8), :] = fresh
                turned[x, pl.ds(m, 8, stride=MEMB), :] = fresh
                if step + 1 < STEPS and x in (0, 7):
                    x_send[step + 1, x // 7, m] = fresh.astype(BF16)
            return carry

        lax.fori_loop(0, MEMB, member, 0)
        if step + 1 < STEPS:
            stage_y(step + 1)
            flying = halo_copies(step + 1)
            for copy in flying:
                copy.start()
        for x in range(8):
            packed[step, x] = turned[x].reshape(8, MEMB, 128).astype(BF16)
        mine = pltpu.make_async_copy(
            packed.at[step, sec], snaps_ref.at[step, pl.ds(sec * 8, 8)], own_sem.at[step]
        )
        mine.start()
        sent.append(mine)
        for ahead in range(1, sec_count):
            target = lax.rem(sec + ahead, sec_count)
            copy = remote(
                packed.at[step, target], snaps_ref.at[step, pl.ds(sec * 8, 8)],
                ss_sem.at[step, ahead], sr_sem.at[step, ahead], {"sec": target},
            )
            copy.start()
            sent.append(copy)
    for copy in sent:
        copy.wait()


def flux(table, state, rock, inflow):
    sec_count = lax.axis_size("sec")
    dma = pltpu.SemaphoreType.DMA
    return pl.pallas_call(
        flux_kernel,
        out_shape=(
            jax.ShapeDtypeStruct((MEMB * 64, 128), F32),
            jax.ShapeDtypeStruct((STEPS, 8 * sec_count, MEMB, 128), BF16),
        ),
        in_specs=[
            pl.BlockSpec(memory_space=pltpu.SMEM),
            pl.BlockSpec(memory_space=VMEM),
            pl.BlockSpec(memory_space=VMEM),
            pl.BlockSpec(memory_space=VMEM),
        ],
        out_specs=(pl.BlockSpec(memory_space=VMEM), pl.BlockSpec(memory_space=VMEM)),
        scratch_shapes=[
            VMEM((4, 8, 128), F32),
            VMEM((4, 8, 128), F32),
            VMEM((STEPS, 2, MEMB, 8, 128), BF16),
            VMEM((STEPS, 2, MEMB, 8, 128), BF16),
            VMEM((STEPS, 2, MEMB * 8, 128), BF16),
            VMEM((STEPS, 2, MEMB * 8, 128), BF16),
            VMEM((2, MEMB * 8, 128), F32),
            VMEM((6, 8, 8, 128), F32),
            VMEM((8, 8 * MEMB, 128), F32),
            VMEM((STEPS, 8, 8, MEMB, 128), BF16),
            dma((4,)), dma((4,)), dma((STEPS, 4)), dma((STEPS, 4)),
            dma((STEPS, sec_count)), dma((STEPS, sec_count)), dma((STEPS,)),
        ],
        compiler_params=pltpu.CompilerParams(
            collective_id=0, has_side_effects=True, vmem_limit_bytes=32 * 1024 * 1024
        ),
        name="flux",
    )(table, state, rock, inflow)


PLANE = 32
COLUMN = 8


def reduce_kernel(x_ref, out_ref, slots, partial, column, send1, recv1, send2, recv2, send3, recv3):
    gx, sec = lax.axis_index("gx"), lax.axis_index("sec")
    z_hi, z_lo = lax.rem(gx // 2, 4), sec // 4
    me = (gx // 8) * 8 + lax.rem(gx, 2) * 4 + lax.rem(sec, 4)
    me_z = z_hi * 2 + z_lo

    def in_plane(p):
        return {"gx": (p // 8) * 8 + z_hi * 2 + lax.rem(p // 4, 2), "sec": z_lo * 4 + lax.rem(p, 4)}

    def in_column(q):
        return {"gx": (gx // 8) * 8 + (q // 2) * 2 + lax.rem(gx, 2), "sec": lax.rem(q, 2) * 4 + lax.rem(sec, 4)}

    barrier = pltpu.get_barrier_semaphore()
    for k in range(1, PLANE):
        pl.semaphore_signal(barrier, inc=1, device_id=in_plane(lax.rem(me + k, PLANE)), device_id_type=MESH)
    for k in range(1, COLUMN):
        pl.semaphore_signal(barrier, inc=1, device_id=in_column(lax.rem(me_z + k, COLUMN)), device_id_type=MESH)
    slots[me] = x_ref[me]
    pl.semaphore_wait(barrier, PLANE + COLUMN - 2)

    def scatter(k):
        p = lax.rem(me + k, PLANE)
        return remote(x_ref.at[p], slots.at[me], send1.at[k], recv1.at[k], in_plane(p))

    for k in range(1, PLANE):
        scatter(k).start()
    for k in range(1, PLANE):
        scatter(k).wait()
    total = slots[0]
    for k in range(1, PLANE):
        total = total + slots[k]
    partial[...] = total
    column[me_z] = total

    def across(k):
        q = lax.rem(me_z + k, COLUMN)
        return remote(partial, column.at[me_z], send2.at[k], recv2.at[k], in_column(q))

    for k in range(1, COLUMN):
        across(k).start()
    for k in range(1, COLUMN):
        across(k).wait()
    total = column[0]
    for k in range(1, COLUMN):
        total = total + column[k]
    out_ref[me] = total

    def gather(k):
        p = lax.rem(me + k, PLANE)
        return remote(out_ref.at[me], out_ref.at[me], send3.at[k], recv3.at[k], in_plane(p))

    for k in range(1, PLANE):
        gather(k).start()
    for k in range(1, PLANE):
        gather(k).wait()


def all_sum(x):
    rows = x.shape[0] // PLANE
    dma = pltpu.SemaphoreType.DMA
    out = pl.pallas_call(
        reduce_kernel,
        out_shape=jax.ShapeDtypeStruct((PLANE, rows, 128), F32),
        in_specs=[pl.BlockSpec(memory_space=VMEM)],
        out_specs=pl.BlockSpec(memory_space=VMEM),
        scratch_shapes=[
            VMEM((PLANE, rows, 128), F32), VMEM((rows, 128), F32), VMEM((COLUMN, rows, 128), F32),
            dma((PLANE,)), dma((PLANE,)), dma((COLUMN,)), dma((COLUMN,)), dma((PLANE,)), dma((PLANE,)),
        ],
        compiler_params=pltpu.CompilerParams(
            collective_id=1, has_side_effects=True, vmem_limit_bytes=16 * 1024 * 1024
        ),
        name="all_sum",
    )(x.reshape(PLANE, rows, 128))
    return out.reshape(x.shape)


HIGH = lax.Precision.HIGHEST


def dot(a, b, contract=((1,), (0,))):
    return lax.dot_general(a, b, (contract, ((), ())), precision=HIGH, preferred_element_type=F32)


ROWS_BASIS = 256
RANK = 32
BLOCK = 8
STRIDE = RANK + BLOCK


def spread_row(ref, at):
    return jnp.broadcast_to(ref[pl.ds(at, 1), :], (8, 128))


def factor(c, gram, sigma, mx, ct, first, second, coef, yy, nat):
    lane = lax.broadcasted_iota(jnp.int32, (8, 128), 1)
    row = lax.broadcasted_iota(jnp.int32, (8, 128), 0)
    group = lane // 32
    g0, g1, g2 = group == 0, group == 1, group == 2

    def wide(mask, rows):
        return jnp.concatenate([mask] * (rows // 8), 0)

    def turn(x, by):
        return pltpu.roll(x, by, 1)

    padded = jnp.concatenate([c, jnp.broadcast_to(sigma, (96, ROWS_BASIS))], 0)
    ct[...] = padded.T
    sig_col = turn(ct[...], 96)
    sig_col = jnp.where(wide(lane, ROWS_BASIS) < 96, sig_col, turn(sig_col, 32))
    inv2 = 1.0 / (sig_col * sig_col)

    at = lax.broadcasted_iota(jnp.int32, (ROWS_BASIS, 128), 0)
    over = lax.broadcasted_iota(jnp.int32, (ROWS_BASIS, 128), 1)
    before = at < BLOCK * (over & 31)
    pick = over // 32
    masks = jnp.where(
        pick == 0, jnp.where(before, inv2 * inv2, 0.0),
        jnp.where(pick == 1, jnp.where(before, inv2, 0.0), jnp.where((pick == 2) & ~before, 1.0, 0.0)),
    )
    low = lax.broadcasted_iota(jnp.int32, (RANK, 128), 0)
    lanes = wide(group, RANK)
    for chunk in range(4):
        pairs = jnp.concatenate([c * c[a : a + 1] for a in range(chunk * 8, chunk * 8 + 8)], 0)
        sums = dot(pairs, masks)
        for i in range(8):
            a = chunk * 8 + i
            mx[a * STRIDE : a * STRIDE + RANK, :] = (
                sums[i * RANK : (i + 1) * RANK]
                + jnp.where((lanes == 1) & (low == a), 1.0, 0.0)
                + jnp.where(lanes == 2, jnp.broadcast_to(gram[:, a : a + 1], (RANK, 128)), 0.0)
            )
    fourth = []
    for half in range(2):
        mixed = jnp.concatenate([ct[pl.ds(half * 4 + t, 32, stride=8), :] for t in range(4)], 0).T
        for t in range(4):
            here = mixed if t == 0 else turn(mixed, 128 - 32 * t)
            r1 = here[:RANK]
            sig = here[RANK : 2 * RANK]
            r2 = sig * sig * r1
            mx[pl.ds(RANK + half * 4 + t, RANK, stride=STRIDE), :] = jnp.where(
                lanes == 0, r1, jnp.where(lanes == 2, -turn(r2, 64), 0.0)
            )
            sq = sig[:8] * sig[:8]
            fourth.append(sq * sq)

    acc = tuple(jnp.zeros((8, 128), F32) for _ in range(BLOCK))
    for part in range(4):
        skip = part * 8
        count = RANK - skip
        w0, w1, w2 = wide(g0, count), wide(g1, count), wide(g2, count)

        def step(k, acc):
            base = pl.multiple_of(k * STRIDE, 8)
            rk = mx[pl.ds(base + skip, count), :]
            ck = mx[pl.ds(skip * STRIDE + k, count, stride=STRIDE), :]
            pivot = spread_row(mx, base + k)
            up, down, across = turn(pivot, 32), turn(pivot, 96), turn(pivot, 64)
            p = jnp.where(g0, pivot, jnp.where(g1, up, across))
            e = jnp.where(g0, down, jnp.where(g1, pivot, up))
            q = jnp.where(g0, across, jnp.where(g1, down, pivot))
            det = 1.0 / (p * q + e * e)
            p, e, q = p * det, e * det, q * det
            pw, ew, qw = (jnp.concatenate([z] * (count // 8), 0) for z in (p, e, q))
            rk_up, rk_down, ck_down = turn(rk, 32), turn(rk, 96), turn(ck, 96)
            u = jnp.where(w2, rk_up, jnp.where(w1, rk, rk))
            v = jnp.where(w0, ck_down, jnp.where(w1, -rk_down, -rk))
            fa = qw * u + ew * v
            sa = ew * u - pw * v
            first[pl.ds(pl.multiple_of(k * RANK, 8) + skip, count), :] = fa
            second[pl.ds(pl.multiple_of(k * RANK, 8) + skip, count), :] = sa
            coef[0, skip:RANK, :] = jnp.where(w0, rk, jnp.where(w1, rk_up, -rk_up))
            coef[1, skip:RANK, :] = jnp.where(w0, ck_down, ck)
            right = mx[pl.ds(base + RANK, 8), :]
            swapped = turn(right, 64)
            u = jnp.where(g0, right, swapped)
            v = jnp.where(g0, -swapped, -right)
            fr = q * u + e * v
            sr = e * u - p * v
            yy[pl.ds(pl.multiple_of(k * 8, 8), 8), :] = jnp.where(g0, fr, turn(sr, 32))
            acc = tuple(
                acc[t]
                + jnp.broadcast_to(u[t : t + 1], (8, 128)) * fr
                + jnp.broadcast_to(v[t : t + 1], (8, 128)) * sr
                for t in range(BLOCK)
            )
            fall = jnp.concatenate([fa, fr], 0)
            sall = jnp.concatenate([sa, sr], 0)
            for i in range(skip, RANK):
                f = jnp.broadcast_to(coef[0, i : i + 1, :], (8, 128))
                s = jnp.broadcast_to(coef[1, i : i + 1, :], (8, 128))
                for part8 in range(count // 8 + 1):
                    where = i * STRIDE + skip + part8 * 8
                    mx[where : where + 8, :] = mx[where : where + 8, :] - (
                        f * fall[part8 * 8 : part8 * 8 + 8] + s * sall[part8 * 8 : part8 * 8 + 8]
                    )
            return acc

        acc = lax.fori_loop(skip, skip + 8, step, acc)

    ys = [None] * RANK
    for k in range(RANK - 1, -1, -1):
        y = yy[k * 8 : k * 8 + 8, :]
        if k < RANK - 1:
            a1 = a2 = None
            for l in range(RANK - 1, k, -1):
                m1 = spread_row(first, k * RANK + l) * ys[l]
                m2 = spread_row(second, k * RANK + l) * ys[l]
                a1 = m1 if a1 is None else a1 + m1
                a2 = m2 if a2 is None else a2 + m2
            y = y - jnp.where(g0, a1 + turn(a1, 96), a2 + turn(a2, 32))
        ys[k] = y

    block = [acc[t] + jnp.where(row == t, fourth[t], 0.0) for t in range(BLOCK)]
    scale = jnp.zeros((8, 128), F32)
    steps = []
    for s in range(BLOCK):
        d = jnp.broadcast_to(block[s][s : s + 1], (8, 128))
        scale = jnp.where(row == s, lax.rsqrt(d), scale)
        ratio = jnp.where(row > s, block[s] / d, 0.0)
        steps.append(ratio)
        for t in range(s + 1, BLOCK):
            block[t] = block[t] - jnp.broadcast_to(block[s][t : t + 1], (8, 128)) * ratio
    for index in range(2 * RANK + BLOCK):
        if index < RANK:
            value = ys[index]
        elif index < 2 * RANK:
            value = turn(ys[index - RANK], 96)
        else:
            value = jnp.where(row == index - 2 * RANK, 1.0, 0.0)
        for s in range(BLOCK - 1):
            value = value - steps[s] * jnp.broadcast_to(value[s : s + 1], (8, 128))
        yy[index * 8 : index * 8 + 8, :] = value * scale
    for half in range(2):
        mixed = None
        for t in range(4):
            part = yy[pl.ds(half * 4 + t, 128, stride=8), :]
            part = part if t == 0 else turn(part, 32 * t)
            mixed = part if t == 0 else jnp.where(wide(group, 128) == t, part, mixed)
        mixed = mixed.T
        for t in range(4):
            nat[pl.ds(half * 4 + t, 32, stride=8), :] = mixed[32 * t : 32 * t + 32]

    inv_row = 1.0 / (sigma * sigma)
    weighed = jnp.concatenate([c * (inv_row * inv_row), c * inv_row], 0)
    across = lax.broadcasted_iota(jnp.int32, (ROWS_BASIS, ROWS_BASIS), 1)
    down = lax.broadcasted_iota(jnp.int32, (ROWS_BASIS, ROWS_BASIS), 0)
    tile = jnp.where(
        (lax.broadcasted_iota(jnp.int32, (BLOCK, ROWS_BASIS), 1) & 7)
        == lax.broadcasted_iota(jnp.int32, (BLOCK, ROWS_BASIS), 0), 1.0, 0.0
    )
    natural = nat[...]
    below = -dot(natural[:, : 2 * RANK], weighed)
    own = dot(natural[:, 2 * RANK : 2 * RANK + BLOCK], tile)
    inverse = jnp.where(across // 8 < down // 8, below, jnp.where(across // 8 == down // 8, own, 0.0))
    return inverse, sig_col


def batch_update(c, rounded, gram, sigma, *scratch):
    inverse, sig_col = factor(c, gram, sigma, *scratch)
    sig = jnp.concatenate([sig_col, sig_col], 1)
    on_snaps = dot(c, inverse, ((1,), (1,)))
    scaled = sig * sig * inverse.T
    total = scaled + dot(c, on_snaps, ((0,), (0,)))
    on_basis = scaled + dot(c - rounded, on_snaps, ((0,), (0,)))
    top = sig * total
    bottom = dot(c, total) + dot(gram, on_snaps)
    energy = jnp.sum(top * top, axis=0, keepdims=True) + jnp.sum(bottom * bottom, axis=0, keepdims=True)
    return on_basis, on_snaps, jnp.sqrt(energy)


def small_kernel(rows_total, whole_ref, sigma_ref, mix_ref, sigma_out_ref, half_uu, *scratch):
    scale = 1.0 / rows_total

    def piece(index):
        return whole_ref[64 * index : 64 * (index + 1), :] * scale

    high = lax.broadcasted_iota(jnp.int32, (64, 128), 1) >= 64
    last = piece(6)
    half_uu[...] = jnp.zeros((256, 256), F32)
    half_uu[0:64, 0:128] = jnp.where(high, 1.0, 0.5) * piece(2)
    half_uu[0:64, 128:256] = piece(3)
    half_uu[64:128, 0:128] = jnp.where(high, 0.5 * last, 0.0)
    half_uu[64:128, 128:256] = piece(4)
    half_uu[128:192, 128:256] = jnp.where(high, 1.0, 0.5) * piece(5)
    half_uu[192:256, 128:256] = jnp.where(high, 0.5 * pltpu.roll(last, 64, 1), 0.0)
    su = jnp.concatenate([piece(0), piece(1)], 1)
    ss = piece(7)
    s00, s10, s11 = ss[:32, :32], ss[32:, :32], ss[32:, 32:64]

    def of_basis(x):
        part = dot(dot(x, half_uu[...]), x, ((1,), (1,)))
        return part + part.T

    def twice(c, r):
        part = dot(c, r, ((1,), (1,)))
        return part + part.T

    c0 = su[:32]
    r0 = c0.astype(BF16).astype(F32)
    gram0 = s00 - twice(c0, r0) + of_basis(r0)
    wu, ws, sigma1 = batch_update(c0, r0, gram0, sigma_ref[...], *scratch)
    c1 = dot(su[32:], wu) + dot(s10, ws)
    r1 = c1.astype(BF16).astype(F32)
    yu = dot(r1, wu, ((1,), (1,)))
    ys = dot(r1, ws, ((1,), (1,)))
    cross = dot(dot(ys, c0), yu, ((1,), (1,)))
    gram1 = s11 - twice(c1, r1) + of_basis(yu) + cross + cross.T + dot(dot(ys, s00), ys, ((1,), (1,)))
    wu1, ws1, sigma2 = batch_update(c1, r1, gram1, sigma1, *scratch)
    mix_ref[0:256, :] = dot(wu, wu1).astype(BF16)
    mix_ref[256:288, :] = dot(ws, wu1).astype(BF16)
    mix_ref[288:320, :] = ws1.astype(BF16)
    sigma_out_ref[...] = sigma2


def small_algebra(whole, sigma, rows_total):
    return pl.pallas_call(
        lambda *refs: small_kernel(float(rows_total), *refs),
        out_shape=(jax.ShapeDtypeStruct((320, 256), BF16), jax.ShapeDtypeStruct((1, 256), F32)),
        in_specs=[pl.BlockSpec(memory_space=VMEM)] * 2,
        out_specs=(pl.BlockSpec(memory_space=VMEM),) * 2,
        scratch_shapes=[
            VMEM((256, 256), F32),
            VMEM((RANK * STRIDE, 128), F32),
            VMEM((256, 128), F32),
            VMEM((RANK * RANK, 128), F32),
            VMEM((RANK * RANK, 128), F32),
            VMEM((2, RANK, 128), F32),
            VMEM((128 * 8, 128), F32),
            VMEM((256, 128), F32),
        ],
        compiler_params=pltpu.CompilerParams(vmem_limit_bytes=32 * 1024 * 1024),
        name="small_algebra",
    )(whole, sigma.reshape(1, -1))


def body(state_init, rock_type, perm_table, well_cells, well_rate, basis_in, singular):
    members, across, along, width = state_init.shape
    layers = width // 2
    sec_count = lax.axis_size("sec")
    rock = rock_type.reshape(across, along, layers)
    rock = jnp.concatenate([rock, rock], -1)
    x_start = lax.axis_index("gx") * across
    y_start = lax.axis_index("sec") * along
    total_y = along * sec_count
    x_pos = lax.broadcasted_iota(jnp.int32, (across, along, layers), 0)
    y_pos = lax.broadcasted_iota(jnp.int32, (across, along, layers), 1)
    z_pos = lax.broadcasted_iota(jnp.int32, (across, along, layers), 2)
    cell_ids = ((x_start + x_pos) * total_y + y_start + y_pos) * layers + z_pos
    hits = (well_cells[:, None] == cell_ids.reshape(1, -1)).astype(jnp.float32)
    source = jnp.dot(well_rate, hits, precision=HIGH).reshape(members, across, along, layers)
    source_full = jnp.concatenate([source, jnp.zeros_like(source)], -1)
    rows_total = basis_in.size // basis_in.shape[-1] * lax.axis_size("gx") * sec_count

    final, snaps = flux(perm_table, state_init, rock, source_full)
    state_out = final.reshape(state_init.shape)

    both = snaps.reshape(STEPS, -1, GROUPS, MG, width).transpose(2, 0, 3, 1, 4).reshape(GROUPS * STEPS * MG, -1)
    basis = basis_in.reshape(both.shape[1], basis_in.shape[-1])
    count = basis.shape[1]
    taken = both.shape[0]
    uu = lax.dot_general(basis, basis, (((0,), (0,)), ((), ())), preferred_element_type=jnp.float32)
    su = jnp.dot(both, basis, preferred_element_type=jnp.float32)
    ss = lax.dot_general(both, both, (((1,), (1,)), ((), ())), preferred_element_type=jnp.float32)
    local = jnp.concatenate(
        [
            su[:, :128],
            su[:, 128:],
            uu[:64, :128],
            uu[:64, 128:],
            uu[64:128, 128:],
            uu[128:192, 128:],
            jnp.concatenate([uu[192:, 192:], uu[64:128, 64:128]], 1),
            jnp.pad(ss, ((0, 0), (0, 64))),
        ],
        0,
    )
    mix, sigma = small_algebra(all_sum(local), singular, rows_total)
    fresh = jnp.dot(basis, mix[:count], preferred_element_type=jnp.float32)
    fresh = fresh + lax.dot_general(both, mix[count:], (((0,), (0,)), ((), ())), preferred_element_type=jnp.float32)
    return (state_out, fresh.astype(jnp.bfloat16).reshape(basis_in.shape), sigma.reshape(-1))


def solution(mesh):
    return jax.shard_map(
        body,
        mesh=mesh,
        in_specs=(
            P(None, "gx", "sec", None),
            P("gx", "sec"),
            P(),
            P(),
            P(),
            P(("gx", "sec"), None, None, None),
            P(),
        ),
        out_specs=(P(None, "gx", "sec", None), P(("gx", "sec"), None, None, None), P()),
        check_vma=False,
    )
```

```python
import jax
import jax.numpy as jnp
from jax import lax
from jax.experimental import pallas as pl
from jax.experimental.pallas import tpu as pltpu
from jax.sharding import PartitionSpec as P

MG = 8
STEPS = 4
GROUPS = 2
MEMB = MG * GROUPS

DT_PRESSURE = 0.12
DT_SATURATION = 0.06
DT_ADVECT = 0.15

MESH = pl.DeviceIdType.MESH
VMEM = pltpu.VMEM
F32 = jnp.float32
BF16 = jnp.bfloat16


def harmonic(left, right):
    return 2.0 * left * right / (left + right)


def remote(src, dst, send_sem, recv_sem, device):
    return pltpu.make_async_remote_copy(
        src_ref=src, dst_ref=dst, send_sem=send_sem, recv_sem=recv_sem, device_id=device, device_id_type=MESH
    )


PLANE = 32
COLUMN = 8


SHARE = 16
CHUNKS = 8


def slab_kernel(
    table_ref, state_ref, rock_ref, cells_ref, rate_ref, basis_hbm, out_ref, snaps_ref, sum_ref,
    basis, uu, inflow, kinds, perm_send, perm_recv, x_send, x_recv, y_send, y_recv, y_wide, weights, turned, packed,
    local, slots, partial, column,
    load_sem, ps_sem, pr_sem, hs_sem, hr_sem, ss_sem, sr_sem, own_sem, send1, recv1, send2, recv2, send3, recv3,
):
    gx_count, sec_count = lax.axis_size("gx"), lax.axis_size("sec")
    gx, sec = lax.axis_index("gx"), lax.axis_index("sec")
    beside = (
        {"gx": lax.rem(gx + gx_count - 1, gx_count)},
        {"gx": lax.rem(gx + 1, gx_count)},
        {"sec": lax.rem(sec + sec_count - 1, sec_count)},
        {"sec": lax.rem(sec + 1, sec_count)},
    )
    z_hi, z_lo = lax.rem(gx // 2, 4), sec // 4
    me = (gx // 8) * 8 + lax.rem(gx, 2) * 4 + lax.rem(sec, 4)
    me_z = z_hi * 2 + z_lo

    def in_plane(p):
        return {"gx": (p // 8) * 8 + z_hi * 2 + lax.rem(p // 4, 2), "sec": z_lo * 4 + lax.rem(p, 4)}

    def in_column(q):
        return {"gx": (gx // 8) * 8 + (q // 2) * 2 + lax.rem(gx, 2), "sec": lax.rem(q, 2) * 4 + lax.rem(sec, 4)}

    barrier = pltpu.get_barrier_semaphore()

    def greet(device):
        pl.semaphore_signal(barrier, inc=1, device_id=device, device_id_type=MESH)

    greet(beside[0])
    greet(beside[1])
    for ahead in range(1, sec_count):
        greet({"sec": lax.rem(sec + ahead, sec_count)})
    for k in range(1, COLUMN):
        greet(in_column(lax.rem(me_z + k, COLUMN)))
    for k in range(1, PLANE):
        greet(in_plane(lax.rem(me + k, PLANE)))

    def load(c):
        rows = pl.ds(pl.multiple_of(c * 1024, 1024), 1024)
        return pltpu.make_async_copy(basis_hbm.at[rows], basis.at[rows], load_sem.at[c])

    for c in range(CHUNKS):
        load(c).start()

    lane = lax.broadcasted_iota(jnp.int32, (8, 128), 1)
    row = lax.broadcasted_iota(jnp.int32, (8, 128), 0)

    def uu_chunk(c, carry):
        load(c).wait()
        part = basis[pl.ds(pl.multiple_of(c * 1024, 1024), 1024), :]
        tn = (((0,), (0,)), ((), ()))
        uu[0:128, :] += lax.dot_general(part[:, :128], part, tn, preferred_element_type=F32)
        uu[128:256, 128:256] += lax.dot_general(part[:, 128:], part[:, 128:], tn, preferred_element_type=F32)
        return carry

    def halo_copies(step, g):
        copies = []
        for d in range(4):
            if d < 2:
                src = x_send.at[step, d, pl.ds(g * MG, MG)]
                dst = x_recv.at[step, 1 - d, pl.ds(g * MG, MG)]
            else:
                rows = pl.ds(pl.multiple_of(g * 8 * MG, 8 * MG), 8 * MG)
                src = y_send.at[step, d - 2, rows]
                dst = y_recv.at[step, 3 - d, rows]
            copies.append(remote(src, dst, hs_sem.at[step, g, d], hr_sem.at[step, g, d ^ 1], beside[d]))
        return copies

    def stage_y(step, g):
        for side, y in ((0, 0), (1, 7)):
            rows = pl.ds(pl.multiple_of(g * 8 * MG, 8 * MG), 8 * MG)
            y_send[step, side, rows, :] = out_ref[pl.ds(g * 64 * MG + y, 8 * MG, stride=8), :].astype(BF16)

    def first(m, carry):
        x_send[0, 0, m] = state_ref[m, 0].astype(BF16)
        x_send[0, 1, m] = state_ref[m, 7].astype(BF16)
        for x in range(8):
            out_ref[pl.ds(pl.multiple_of(m * 64 + x * 8, 8), 8), :] = state_ref[m, x]
        return carry

    lax.fori_loop(0, MEMB, first, 0)
    stage_y(0, 0)
    stage_y(0, 1)

    for pair in range(4):
        both = rock_ref[:, pair * 128 : pair * 128 + 128]
        other = pltpu.roll(both, 64, 1)
        kinds[pl.ds(2 * pair, 8, stride=8), :] = jnp.where(lane < 64, both, other)
        kinds[pl.ds(2 * pair + 1, 8, stride=8), :] = jnp.where(lane < 64, other, both)
    perm = [[], [], []]
    for x in range(8):
        kind = kinds[x * 8 : x * 8 + 8, :]
        for d in range(3):
            value = jnp.full((8, 128), table_ref[d, 0], F32)
            for r in range(1, 16):
                value = jnp.where(kind == r, table_ref[d, r], value)
            perm[d].append(value)
    perm_send[0] = perm[0][0]
    perm_send[1] = perm[0][7]
    for x in range(8):
        perm_send[2, pl.ds(x, 1), :] = perm[1][x][0:1]
        perm_send[3, pl.ds(x, 1), :] = perm[1][x][7:8]

    uu[...] = jnp.zeros((256, 256), F32)
    pl.semaphore_wait(barrier, 2 + (sec_count - 1) + (COLUMN - 1) + (PLANE - 1))
    perm_copies = [
        remote(perm_send.at[d], perm_recv.at[d ^ 1], ps_sem.at[d], pr_sem.at[d ^ 1], beside[d]) for d in range(4)
    ]
    for copy in perm_copies:
        copy.start()
    for g in range(GROUPS):
        for copy in halo_copies(0, g):
            copy.start()

    rate = rate_ref[...]
    top = rate.astype(BF16)
    rest = rate - top.astype(F32)
    middle = rest.astype(BF16)
    parts = jnp.concatenate([top, middle, (rest - middle.astype(F32)).astype(BF16)], 0)
    wells = cells_ref[...]
    cell = lax.broadcasted_iota(jnp.int32, (512, 256), 0)

    def place(x, carry):
        ids = ((gx * 8 + x) * (8 * sec_count) + sec * 8) * 64 + cell
        hits = jnp.where(ids == wells, 1.0, 0.0).astype(BF16)
        found = lax.dot_general(parts, hits, (((1,), (1,)), ((), ())), preferred_element_type=F32)
        found = found[:MEMB] + found[MEMB : 2 * MEMB] + found[2 * MEMB :]
        for y in range(8):
            pair = found[:, (y // 2) * 128 : (y // 2) * 128 + 128]
            pair = pair if y % 2 == 0 else pltpu.roll(pair, 64, 1)
            half = lax.broadcasted_iota(jnp.int32, (MEMB, 128), 1) < 64
            inflow[pl.ds(x * 8 + y, MEMB, stride=64), :] = jnp.where(half, DT_PRESSURE * pair, 0.0)
        return carry

    lax.fori_loop(0, 8, place, 0)

    z_up = jnp.where((lane & 63) == 63, 0.0, 1.0)
    z_down = jnp.where((lane & 63) == 0, 0.0, 1.0)
    for x in range(8):
        weights[4, x] = z_up * harmonic(perm[2][x], pltpu.roll(perm[2][x], 127, 1))
        weights[5, x] = z_down * harmonic(perm[2][x], pltpu.roll(perm[2][x], 1, 1))
    for copy in perm_copies:
        copy.wait()
    not_first_x = jnp.where(gx == 0, 0.0, 1.0)
    not_last_x = jnp.where(gx == gx_count - 1, 0.0, 1.0)
    not_first_y = jnp.where(sec == 0, 0.0, 1.0)
    not_last_y = jnp.where(sec == sec_count - 1, 0.0, 1.0)
    for x in range(8):
        above = perm[0][x + 1] if x < 7 else perm_recv[1] * not_last_x
        below = perm[0][x - 1] if x > 0 else perm_recv[0] * not_first_x
        weights[0, x] = harmonic(perm[0][x], above)
        weights[1, x] = harmonic(below, perm[0][x])
        right = jnp.broadcast_to(perm_recv[3, pl.ds(x, 1), :] * not_last_y, (8, 128))
        left = jnp.broadcast_to(perm_recv[2, pl.ds(x, 1), :] * not_first_y, (8, 128))
        weights[2, x] = harmonic(perm[1][x], jnp.where(row == 7, right, pltpu.roll(perm[1][x], 7, 0)))
        weights[3, x] = harmonic(jnp.where(row == 0, left, pltpu.roll(perm[1][x], 1, 0)), perm[1][x])

    step_sizes = jnp.where(lane < 64, DT_PRESSURE, DT_SATURATION)
    advect = jnp.where(lane < 64, 0.0, DT_ADVECT)

    def snap_copies(step):
        copies = [
            pltpu.make_async_copy(packed.at[step, sec], snaps_ref.at[step, pl.ds(sec * 8, 8)], own_sem.at[step])
        ]
        for ahead in range(1, sec_count):
            target = lax.rem(sec + ahead, sec_count)
            copies.append(
                remote(
                    packed.at[step, target], snaps_ref.at[step, pl.ds(sec * 8, 8)],
                    ss_sem.at[step, ahead], sr_sem.at[step, ahead], {"sec": target},
                )
            )
        return copies

    for step in range(STEPS):

        def half_step(g, carry):
            for copy in halo_copies(step, g):
                copy.wait()
            rows = pl.ds(pl.multiple_of(g * 8 * MG, 8 * MG), 8 * MG)
            y_wide[0, rows, :] = y_recv[step, 0, rows, :].astype(F32)
            y_wide[1, rows, :] = y_recv[step, 1, rows, :].astype(F32)

            def member(index, carry):
                m = g * MG + index
                base = pl.multiple_of(m * 64, 64)
                old = [out_ref[pl.ds(base + x * 8, 8), :] for x in range(8)]
                old_below = x_recv[step, 0, m].astype(F32)
                old_above = x_recv[step, 1, m].astype(F32)
                for x in range(8):
                    here = old[x]
                    left = jnp.broadcast_to(y_wide[0, pl.ds(m * 8 + x, 1), :], (8, 128))
                    right = jnp.broadcast_to(y_wide[1, pl.ds(m * 8 + x, 1), :], (8, 128))
                    besides = (
                        old[x + 1] if x < 7 else old_above,
                        old[x - 1] if x > 0 else old_below,
                        jnp.where(row == 7, right, pltpu.roll(here, 7, 0)),
                        jnp.where(row == 0, left, pltpu.roll(here, 1, 0)),
                        pltpu.roll(here, 127, 1),
                        pltpu.roll(here, 1, 1),
                    )
                    spread = carried = None
                    for d in range(6):
                        flow = weights[d, x] * (besides[d] - here)
                        pushed = pltpu.roll(flow, 64, 1)
                        moved = pushed * jnp.where(pushed > 0.0, besides[d], here)
                        spread = flow if spread is None else spread + flow
                        carried = moved if carried is None else carried + moved
                    fresh = here + step_sizes * spread + advect * carried + inflow[pl.ds(base + x * 8, 8), :]
                    out_ref[pl.ds(base + x * 8, 8), :] = fresh
                    turned[x, pl.ds(m, 8, stride=MEMB), :] = fresh
                    if step + 1 < STEPS and x in (0, 7):
                        x_send[step + 1, x // 7, m] = fresh.astype(BF16)
                return carry

            lax.fori_loop(0, MG, member, 0)
            if step + 1 < STEPS:
                stage_y(step + 1, g)
                for copy in halo_copies(step + 1, g):
                    copy.start()
            return carry

        lax.fori_loop(0, GROUPS, half_step, 0)
        for x in range(8):
            packed[step, x] = turned[x].reshape(8, MEMB, 128).astype(BF16)
        for copy in snap_copies(step):
            copy.start()
        lax.fori_loop(2 * step, 2 * step + 2, uu_chunk, 0)
    for step in range(STEPS):
        for copy in snap_copies(step):
            copy.wait()

    def gram(pair, carry):
        su, ss = carry
        lhs = jnp.concatenate(
            [snaps_ref[:, 2 * pair].reshape(64, 128), snaps_ref[:, 2 * pair + 1].reshape(64, 128)], 1
        )
        rhs = basis[pl.ds(pl.multiple_of(pair * 256, 256), 256), :]
        su = su + jnp.dot(lhs, rhs, preferred_element_type=F32)
        ss = ss + lax.dot_general(lhs, lhs, (((1,), (1,)), ((), ())), preferred_element_type=F32)
        return su, ss

    su, ss = lax.fori_loop(
        0, 4 * sec_count, gram, (jnp.zeros((64, 256), F32), jnp.zeros((64, 64), F32)), unroll=4
    )
    zero = jnp.zeros((64, 64), F32)
    for index, block in enumerate(
        (
            su[:, :128],
            su[:, 128:],
            uu[0:64, 0:128],
            uu[0:64, 128:256],
            uu[64:128, 128:256],
            uu[128:192, 128:256],
            jnp.concatenate([uu[192:256, 192:256], uu[64:128, 64:128]], 1),
            jnp.concatenate([ss, zero], 1),
        )
    ):
        local[4 * index : 4 * index + 4] = block.reshape(4, SHARE, 128)

    slots[me] = local[me]

    def scatter(k):
        p = lax.rem(me + k, PLANE)
        return remote(local.at[p], slots.at[me], send1.at[k], recv1.at[k], in_plane(p))

    for k in range(1, PLANE):
        scatter(k).start()
    for k in range(1, PLANE):
        scatter(k).wait()
    total = slots[0]
    for k in range(1, PLANE):
        total = total + slots[k]
    partial[...] = total
    column[me_z] = total

    def across(k):
        q = lax.rem(me_z + k, COLUMN)
        return remote(partial, column.at[me_z], send2.at[k], recv2.at[k], in_column(q))

    for k in range(1, COLUMN):
        across(k).start()
    for k in range(1, COLUMN):
        across(k).wait()
    total = column[0]
    for k in range(1, COLUMN):
        total = total + column[k]
    sum_ref[me] = total

    def gather(k):
        p = lax.rem(me + k, PLANE)
        return remote(sum_ref.at[me], sum_ref.at[me], send3.at[k], recv3.at[k], in_plane(p))

    for k in range(1, PLANE):
        gather(k).start()
    for k in range(1, PLANE):
        gather(k).wait()


def slab(table, state, rock, cells, rate, basis):
    sec_count = lax.axis_size("sec")
    dma = pltpu.SemaphoreType.DMA
    in_vmem = pl.BlockSpec(memory_space=VMEM)
    return pl.pallas_call(
        slab_kernel,
        out_shape=(
            jax.ShapeDtypeStruct((MEMB * 64, 128), F32),
            jax.ShapeDtypeStruct((STEPS, 8 * sec_count, MEMB, 128), BF16),
            jax.ShapeDtypeStruct((PLANE, SHARE, 128), F32),
        ),
        in_specs=[pl.BlockSpec(memory_space=pltpu.SMEM)] + [in_vmem] * 4 + [pl.BlockSpec(memory_space=pltpu.HBM)],
        out_specs=(in_vmem,) * 3,
        scratch_shapes=[
            VMEM(basis.shape, BF16),
            VMEM((256, 256), F32),
            VMEM((MEMB * 64, 128), F32),
            VMEM((64, 128), jnp.int32),
            VMEM((4, 8, 128), F32),
            VMEM((4, 8, 128), F32),
            VMEM((STEPS, 2, MEMB, 8, 128), BF16),
            VMEM((STEPS, 2, MEMB, 8, 128), BF16),
            VMEM((STEPS, 2, MEMB * 8, 128), BF16),
            VMEM((STEPS, 2, MEMB * 8, 128), BF16),
            VMEM((2, MEMB * 8, 128), F32),
            VMEM((6, 8, 8, 128), F32),
            VMEM((8, 8 * MEMB, 128), F32),
            VMEM((STEPS, 8, 8, MEMB, 128), BF16),
            VMEM((PLANE, SHARE, 128), F32),
            VMEM((PLANE, SHARE, 128), F32),
            VMEM((SHARE, 128), F32),
            VMEM((COLUMN, SHARE, 128), F32),
            dma((CHUNKS,)), dma((4,)), dma((4,)), dma((STEPS, GROUPS, 4)), dma((STEPS, GROUPS, 4)),
            dma((STEPS, sec_count)), dma((STEPS, sec_count)), dma((STEPS,)),
            dma((PLANE,)), dma((PLANE,)), dma((COLUMN,)), dma((COLUMN,)), dma((PLANE,)), dma((PLANE,)),
        ],
        compiler_params=pltpu.CompilerParams(
            collective_id=0, has_side_effects=True, vmem_limit_bytes=40 * 1024 * 1024
        ),
        name="slab",
    )(table, state, rock, cells, rate, basis)


def rotate_kernel(basis_ref, snaps_ref, mix_ref, out_ref):
    taken = jnp.concatenate([snaps_ref[:, y].reshape(64, 128).T for y in range(8)], 0)
    lhs = jnp.concatenate([basis_ref[...], taken], 1)
    out_ref[...] = jnp.dot(lhs, mix_ref[...], preferred_element_type=F32).astype(BF16)


def rotate(basis, snaps, mix):
    rows = basis.shape[0]
    return pl.pallas_call(
        rotate_kernel,
        grid=(rows // 1024,),
        out_shape=jax.ShapeDtypeStruct(basis.shape, BF16),
        in_specs=[
            pl.BlockSpec((1024, 256), lambda i: (i, 0)),
            pl.BlockSpec((STEPS, 8, MEMB, 128), lambda i: (0, i, 0, 0)),
            pl.BlockSpec((320, 256), lambda i: (0, 0)),
        ],
        out_specs=pl.BlockSpec((1024, 256), lambda i: (i, 0)),
        compiler_params=pltpu.CompilerParams(vmem_limit_bytes=24 * 1024 * 1024),
        name="rotate",
    )(basis, snaps, mix)


HIGH = lax.Precision.HIGHEST


def dot(a, b, contract=((1,), (0,))):
    return lax.dot_general(a, b, (contract, ((), ())), precision=HIGH, preferred_element_type=F32)


ROWS_BASIS = 256
RANK = 32
BLOCK = 8
STRIDE = RANK + BLOCK


def spread_row(ref, at):
    return jnp.broadcast_to(ref[pl.ds(at, 1), :], (8, 128))


def factor(c, gram, sigma, mx, ct, first, second, coef, yy, nat):
    lane = lax.broadcasted_iota(jnp.int32, (8, 128), 1)
    row = lax.broadcasted_iota(jnp.int32, (8, 128), 0)
    group = lane // 32
    g0, g1, g2 = group == 0, group == 1, group == 2

    def wide(mask, rows):
        return jnp.concatenate([mask] * (rows // 8), 0)

    def turn(x, by):
        return pltpu.roll(x, by, 1)

    padded = jnp.concatenate([c, jnp.broadcast_to(sigma, (96, ROWS_BASIS))], 0)
    ct[...] = padded.T
    sig_col = turn(ct[...], 96)
    sig_col = jnp.where(wide(lane, ROWS_BASIS) < 96, sig_col, turn(sig_col, 32))
    inv2 = 1.0 / (sig_col * sig_col)

    at = lax.broadcasted_iota(jnp.int32, (ROWS_BASIS, 128), 0)
    over = lax.broadcasted_iota(jnp.int32, (ROWS_BASIS, 128), 1)
    before = at < BLOCK * (over & 31)
    pick = over // 32
    masks = jnp.where(
        pick == 0, jnp.where(before, inv2 * inv2, 0.0),
        jnp.where(pick == 1, jnp.where(before, inv2, 0.0), jnp.where((pick == 2) & ~before, 1.0, 0.0)),
    )
    low = lax.broadcasted_iota(jnp.int32, (RANK, 128), 0)
    lanes = wide(group, RANK)
    for chunk in range(4):
        pairs = jnp.concatenate([c * c[a : a + 1] for a in range(chunk * 8, chunk * 8 + 8)], 0)
        sums = dot(pairs, masks)
        for i in range(8):
            a = chunk * 8 + i
            mx[a * STRIDE : a * STRIDE + RANK, :] = (
                sums[i * RANK : (i + 1) * RANK]
                + jnp.where((lanes == 1) & (low == a), 1.0, 0.0)
                + jnp.where(lanes == 2, jnp.broadcast_to(gram[:, a : a + 1], (RANK, 128)), 0.0)
            )
    fourth = []
    for half in range(2):
        mixed = jnp.concatenate([ct[pl.ds(half * 4 + t, 32, stride=8), :] for t in range(4)], 0).T
        for t in range(4):
            here = mixed if t == 0 else turn(mixed, 128 - 32 * t)
            r1 = here[:RANK]
            sig = here[RANK : 2 * RANK]
            r2 = sig * sig * r1
            mx[pl.ds(RANK + half * 4 + t, RANK, stride=STRIDE), :] = jnp.where(
                lanes == 0, r1, jnp.where(lanes == 2, -turn(r2, 64), 0.0)
            )
            sq = sig[:8] * sig[:8]
            fourth.append(sq * sq)

    acc = tuple(jnp.zeros((8, 128), F32) for _ in range(BLOCK))
    for part in range(4):
        skip = part * 8
        count = RANK - skip
        w0, w1, w2 = wide(g0, count), wide(g1, count), wide(g2, count)

        def step(k, acc):
            base = pl.multiple_of(k * STRIDE, 8)
            rk = mx[pl.ds(base + skip, count), :]
            ck = mx[pl.ds(skip * STRIDE + k, count, stride=STRIDE), :]
            pivot = spread_row(mx, base + k)
            up, down, across = turn(pivot, 32), turn(pivot, 96), turn(pivot, 64)
            p = jnp.where(g0, pivot, jnp.where(g1, up, across))
            e = jnp.where(g0, down, jnp.where(g1, pivot, up))
            q = jnp.where(g0, across, jnp.where(g1, down, pivot))
            det = 1.0 / (p * q + e * e)
            p, e, q = p * det, e * det, q * det
            pw, ew, qw = (jnp.concatenate([z] * (count // 8), 0) for z in (p, e, q))
            rk_up, rk_down, ck_down = turn(rk, 32), turn(rk, 96), turn(ck, 96)
            u = jnp.where(w2, rk_up, jnp.where(w1, rk, rk))
            v = jnp.where(w0, ck_down, jnp.where(w1, -rk_down, -rk))
            fa = qw * u + ew * v
            sa = ew * u - pw * v
            first[pl.ds(pl.multiple_of(k * RANK, 8) + skip, count), :] = fa
            second[pl.ds(pl.multiple_of(k * RANK, 8) + skip, count), :] = sa
            coef[0, skip:RANK, :] = jnp.where(w0, rk, jnp.where(w1, rk_up, -rk_up))
            coef[1, skip:RANK, :] = jnp.where(w0, ck_down, ck)
            right = mx[pl.ds(base + RANK, 8), :]
            swapped = turn(right, 64)
            u = jnp.where(g0, right, swapped)
            v = jnp.where(g0, -swapped, -right)
            fr = q * u + e * v
            sr = e * u - p * v
            yy[pl.ds(pl.multiple_of(k * 8, 8), 8), :] = jnp.where(g0, fr, turn(sr, 32))
            acc = tuple(
                acc[t]
                + jnp.broadcast_to(u[t : t + 1], (8, 128)) * fr
                + jnp.broadcast_to(v[t : t + 1], (8, 128)) * sr
                for t in range(BLOCK)
            )
            fall = jnp.concatenate([fa, fr], 0)
            sall = jnp.concatenate([sa, sr], 0)
            for i in range(skip, RANK):
                f = jnp.broadcast_to(coef[0, i : i + 1, :], (8, 128))
                s = jnp.broadcast_to(coef[1, i : i + 1, :], (8, 128))
                for part8 in range(count // 8 + 1):
                    where = i * STRIDE + skip + part8 * 8
                    mx[where : where + 8, :] = mx[where : where + 8, :] - (
                        f * fall[part8 * 8 : part8 * 8 + 8] + s * sall[part8 * 8 : part8 * 8 + 8]
                    )
            return acc

        acc = lax.fori_loop(skip, skip + 8, step, acc)

    ys = [None] * RANK
    for k in range(RANK - 1, -1, -1):
        y = yy[k * 8 : k * 8 + 8, :]
        if k < RANK - 1:
            a1 = a2 = None
            for l in range(RANK - 1, k, -1):
                m1 = spread_row(first, k * RANK + l) * ys[l]
                m2 = spread_row(second, k * RANK + l) * ys[l]
                a1 = m1 if a1 is None else a1 + m1
                a2 = m2 if a2 is None else a2 + m2
            y = y - jnp.where(g0, a1 + turn(a1, 96), a2 + turn(a2, 32))
        ys[k] = y

    block = [acc[t] + jnp.where(row == t, fourth[t], 0.0) for t in range(BLOCK)]
    scale = jnp.zeros((8, 128), F32)
    steps = []
    for s in range(BLOCK):
        d = jnp.broadcast_to(block[s][s : s + 1], (8, 128))
        scale = jnp.where(row == s, lax.rsqrt(d), scale)
        ratio = jnp.where(row > s, block[s] / d, 0.0)
        steps.append(ratio)
        for t in range(s + 1, BLOCK):
            block[t] = block[t] - jnp.broadcast_to(block[s][t : t + 1], (8, 128)) * ratio
    for index in range(2 * RANK + BLOCK):
        if index < RANK:
            value = ys[index]
        elif index < 2 * RANK:
            value = turn(ys[index - RANK], 96)
        else:
            value = jnp.where(row == index - 2 * RANK, 1.0, 0.0)
        for s in range(BLOCK - 1):
            value = value - steps[s] * jnp.broadcast_to(value[s : s + 1], (8, 128))
        yy[index * 8 : index * 8 + 8, :] = value * scale
    for half in range(2):
        mixed = None
        for t in range(4):
            part = yy[pl.ds(half * 4 + t, 128, stride=8), :]
            part = part if t == 0 else turn(part, 32 * t)
            mixed = part if t == 0 else jnp.where(wide(group, 128) == t, part, mixed)
        mixed = mixed.T
        for t in range(4):
            nat[pl.ds(half * 4 + t, 32, stride=8), :] = mixed[32 * t : 32 * t + 32]

    inv_row = 1.0 / (sigma * sigma)
    weighed = jnp.concatenate([c * (inv_row * inv_row), c * inv_row], 0)
    across = lax.broadcasted_iota(jnp.int32, (ROWS_BASIS, ROWS_BASIS), 1)
    down = lax.broadcasted_iota(jnp.int32, (ROWS_BASIS, ROWS_BASIS), 0)
    tile = jnp.where(
        (lax.broadcasted_iota(jnp.int32, (BLOCK, ROWS_BASIS), 1) & 7)
        == lax.broadcasted_iota(jnp.int32, (BLOCK, ROWS_BASIS), 0), 1.0, 0.0
    )
    natural = nat[...]
    below = -dot(natural[:, : 2 * RANK], weighed)
    own = dot(natural[:, 2 * RANK : 2 * RANK + BLOCK], tile)
    inverse = jnp.where(across // 8 < down // 8, below, jnp.where(across // 8 == down // 8, own, 0.0))
    return inverse, sig_col


def batch_update(c, rounded, gram, sigma, *scratch):
    inverse, sig_col = factor(c, gram, sigma, *scratch)
    sig = jnp.concatenate([sig_col, sig_col], 1)
    on_snaps = dot(c, inverse, ((1,), (1,)))
    scaled = sig * sig * inverse.T
    total = scaled + dot(c, on_snaps, ((0,), (0,)))
    on_basis = scaled + dot(c - rounded, on_snaps, ((0,), (0,)))
    top = sig * total
    bottom = dot(c, total) + dot(gram, on_snaps)
    energy = jnp.sum(top * top, axis=0, keepdims=True) + jnp.sum(bottom * bottom, axis=0, keepdims=True)
    return on_basis, on_snaps, jnp.sqrt(energy)


def by_batch(x):
    return jnp.concatenate([x[16 * step + 8 * g : 16 * step + 8 * g + 8] for g in range(2) for step in range(4)], 0)


def small_kernel(rows_total, whole_ref, sigma_ref, mix_ref, sigma_out_ref, half_uu, *scratch):
    scale = 1.0 / rows_total

    def piece(index):
        return whole_ref[64 * index : 64 * (index + 1), :] * scale

    high = lax.broadcasted_iota(jnp.int32, (64, 128), 1) >= 64
    last = piece(6)
    half_uu[...] = jnp.zeros((256, 256), F32)
    half_uu[0:64, 0:128] = jnp.where(high, 1.0, 0.5) * piece(2)
    half_uu[0:64, 128:256] = piece(3)
    half_uu[64:128, 0:128] = jnp.where(high, 0.5 * last, 0.0)
    half_uu[64:128, 128:256] = piece(4)
    half_uu[128:192, 128:256] = jnp.where(high, 1.0, 0.5) * piece(5)
    half_uu[192:256, 128:256] = jnp.where(high, 0.5 * pltpu.roll(last, 64, 1), 0.0)
    su = by_batch(jnp.concatenate([piece(0), piece(1)], 1))
    source = lax.broadcasted_iota(jnp.int32, (64, 64), 0)
    target = lax.broadcasted_iota(jnp.int32, (64, 64), 1)
    wanted = (target // 8 % 4) * 16 + (target // 32) * 8 + (target & 7)
    ss = dot(by_batch(piece(7)[:, :64]), jnp.where(source == wanted, 1.0, 0.0))
    s00, s10, s11 = ss[:32, :32], ss[32:, :32], ss[32:, 32:]

    def of_basis(x):
        part = dot(dot(x, half_uu[...]), x, ((1,), (1,)))
        return part + part.T

    def twice(c, r):
        part = dot(c, r, ((1,), (1,)))
        return part + part.T

    c0 = su[:32]
    r0 = c0.astype(BF16).astype(F32)
    gram0 = s00 - twice(c0, r0) + of_basis(r0)
    wu, ws, sigma1 = batch_update(c0, r0, gram0, sigma_ref[...], *scratch)
    c1 = dot(su[32:], wu) + dot(s10, ws)
    r1 = c1.astype(BF16).astype(F32)
    yu = dot(r1, wu, ((1,), (1,)))
    ys = dot(r1, ws, ((1,), (1,)))
    cross = dot(dot(ys, c0), yu, ((1,), (1,)))
    gram1 = s11 - twice(c1, r1) + of_basis(yu) + cross + cross.T + dot(dot(ys, s00), ys, ((1,), (1,)))
    wu1, ws1, sigma2 = batch_update(c1, r1, gram1, sigma1, *scratch)
    mix_ref[0:256, :] = dot(wu, wu1).astype(BF16)
    w0, w1 = dot(ws, wu1), ws1
    mix_ref[256:320, :] = jnp.concatenate(
        [w[8 * step : 8 * step + 8] for step in range(4) for w in (w0, w1)], 0
    ).astype(BF16)
    sigma_out_ref[...] = sigma2


def small_algebra(whole, sigma, rows_total):
    return pl.pallas_call(
        lambda *refs: small_kernel(float(rows_total), *refs),
        out_shape=(jax.ShapeDtypeStruct((320, 256), BF16), jax.ShapeDtypeStruct((1, 256), F32)),
        in_specs=[pl.BlockSpec(memory_space=VMEM)] * 2,
        out_specs=(pl.BlockSpec(memory_space=VMEM),) * 2,
        scratch_shapes=[
            VMEM((256, 256), F32),
            VMEM((RANK * STRIDE, 128), F32),
            VMEM((256, 128), F32),
            VMEM((RANK * RANK, 128), F32),
            VMEM((RANK * RANK, 128), F32),
            VMEM((2, RANK, 128), F32),
            VMEM((128 * 8, 128), F32),
            VMEM((256, 128), F32),
        ],
        compiler_params=pltpu.CompilerParams(vmem_limit_bytes=32 * 1024 * 1024),
        name="small_algebra",
    )(whole, sigma.reshape(1, -1))


def body(state_init, rock_type, perm_table, well_cells, well_rate, basis_in, singular):
    basis = basis_in.reshape(-1, basis_in.shape[-1])
    rows_total = basis.shape[0] * lax.axis_size("gx") * lax.axis_size("sec")
    final, snaps, whole = slab(perm_table, state_init, rock_type, well_cells.reshape(1, -1), well_rate, basis)
    mix, sigma = small_algebra(whole.reshape(-1, 128), singular, rows_total)
    fresh = rotate(basis, snaps, mix)
    return (final.reshape(state_init.shape), fresh.reshape(basis_in.shape), sigma.reshape(-1))


def solution(mesh):
    return jax.shard_map(
        body,
        mesh=mesh,
        in_specs=(
            P(None, "gx", "sec", None),
            P("gx", "sec"),
            P(),
            P(),
            P(),
            P(("gx", "sec"), None, None, None),
            P(),
        ),
        out_specs=(P(None, "gx", "sec", None), P(("gx", "sec"), None, None, None), P()),
        check_vma=False,
    )
```

```python
import jax
import jax.numpy as jnp
from jax import lax
from jax.experimental import pallas as pl
from jax.experimental.pallas import tpu as pltpu
from jax.sharding import PartitionSpec as P

MG = 8
STEPS = 4
GROUPS = 2
MEMB = MG * GROUPS

DT_PRESSURE = 0.12
DT_SATURATION = 0.06
DT_ADVECT = 0.15

MESH = pl.DeviceIdType.MESH
VMEM = pltpu.VMEM
F32 = jnp.float32
BF16 = jnp.bfloat16


def harmonic(left, right):
    return 2.0 * left * right / (left + right)


def remote(src, dst, send_sem, recv_sem, device):
    return pltpu.make_async_remote_copy(
        src_ref=src, dst_ref=dst, send_sem=send_sem, recv_sem=recv_sem, device_id=device, device_id_type=MESH
    )


PLANE = 32
COLUMN = 8


SHARE = 16
CHUNKS = 8
TEAMS = 4
TEAM = MEMB // TEAMS


def slab_kernel(
    table_hbm, state_hbm, rock_hbm, cells_hbm, rate_hbm, basis_hbm, out_ref, snaps_ref, sum_ref,
    table_ref, rock_ref, cells_ref, rate_ref, basis, uu, inflow, kinds, perm_send, perm_recv, x_send, x_recv, y_send, y_recv, y_wide, weights, turned, packed,
    local, slots, partial, column,
    load_sem, in_sem, ps_sem, pr_sem, hs_sem, hr_sem, ss_sem, sr_sem, own_sem, send1, recv1, send2, recv2, send3, recv3,
):
    gx_count, sec_count = lax.axis_size("gx"), lax.axis_size("sec")
    gx, sec = lax.axis_index("gx"), lax.axis_index("sec")
    beside = (
        {"gx": lax.rem(gx + gx_count - 1, gx_count)},
        {"gx": lax.rem(gx + 1, gx_count)},
        {"sec": lax.rem(sec + sec_count - 1, sec_count)},
        {"sec": lax.rem(sec + 1, sec_count)},
    )
    z_hi, z_lo = lax.rem(gx // 2, 4), sec // 4
    me = (gx // 8) * 8 + lax.rem(gx, 2) * 4 + lax.rem(sec, 4)
    me_z = z_hi * 2 + z_lo

    def in_plane(p):
        return {"gx": (p // 8) * 8 + z_hi * 2 + lax.rem(p // 4, 2), "sec": z_lo * 4 + lax.rem(p, 4)}

    def in_column(q):
        return {"gx": (gx // 8) * 8 + (q // 2) * 2 + lax.rem(gx, 2), "sec": lax.rem(q, 2) * 4 + lax.rem(sec, 4)}

    barrier = pltpu.get_barrier_semaphore()

    def greet(device):
        pl.semaphore_signal(barrier, inc=1, device_id=device, device_id_type=MESH)

    greet(beside[0])
    greet(beside[1])
    for ahead in range(1, sec_count):
        greet({"sec": lax.rem(sec + ahead, sec_count)})
    for k in range(1, COLUMN):
        greet(in_column(lax.rem(me_z + k, COLUMN)))
    for k in range(1, PLANE):
        greet(in_plane(lax.rem(me + k, PLANE)))

    def load(c):
        rows = pl.ds(pl.multiple_of(c * 1024, 1024), 1024)
        return pltpu.make_async_copy(basis_hbm.at[rows], basis.at[rows], load_sem.at[c])

    arriving = [
        pltpu.make_async_copy(src, dst, in_sem.at[i])
        for i, (src, dst) in enumerate(
            ((table_hbm, table_ref), (state_hbm, out_ref), (rock_hbm, rock_ref), (rate_hbm, rate_ref), (cells_hbm, cells_ref))
        )
    ]
    for copy in arriving:
        copy.start()
    for c in range(CHUNKS):
        load(c).start()

    lane = lax.broadcasted_iota(jnp.int32, (8, 128), 1)
    row = lax.broadcasted_iota(jnp.int32, (8, 128), 0)

    def uu_chunk(c, carry):
        load(c).wait()
        part = basis[pl.ds(pl.multiple_of(c * 1024, 1024), 1024), :]
        tn = (((0,), (0,)), ((), ()))
        uu[0:128, :] += lax.dot_general(part[:, :128], part, tn, preferred_element_type=F32)
        uu[128:256, 128:256] += lax.dot_general(part[:, 128:], part[:, 128:], tn, preferred_element_type=F32)
        return carry

    def halo_copies(step, g):
        copies = []
        for d in range(4):
            if d < 2:
                src = x_send.at[step, d, pl.ds(g * TEAM, TEAM)]
                dst = x_recv.at[step, 1 - d, pl.ds(g * TEAM, TEAM)]
            else:
                rows = pl.ds(pl.multiple_of(g * 8 * TEAM, 8 * TEAM), 8 * TEAM)
                src = y_send.at[step, d - 2, rows]
                dst = y_recv.at[step, 3 - d, rows]
            copies.append(remote(src, dst, hs_sem.at[step, g, d], hr_sem.at[step, g, d ^ 1], beside[d]))
        return copies

    def stage_y(step, g):
        for side, y in ((0, 0), (1, 7)):
            rows = pl.ds(pl.multiple_of(g * 8 * TEAM, 8 * TEAM), 8 * TEAM)
            y_send[step, side, rows, :] = out_ref[pl.ds(g * 64 * TEAM + y, 8 * TEAM, stride=8), :].astype(BF16)

    def first(m, carry):
        x_send[0, 0, m] = out_ref[pl.ds(pl.multiple_of(m * 64, 8), 8), :].astype(BF16)
        x_send[0, 1, m] = out_ref[pl.ds(pl.multiple_of(m * 64 + 56, 8), 8), :].astype(BF16)
        return carry

    for copy in arriving:
        copy.wait()
    lax.fori_loop(0, MEMB, first, 0)
    for g in range(TEAMS):
        stage_y(0, g)

    for pair in range(4):
        both = rock_ref[:, pair * 128 : pair * 128 + 128]
        other = pltpu.roll(both, 64, 1)
        kinds[pl.ds(2 * pair, 8, stride=8), :] = jnp.where(lane < 64, both, other)
        kinds[pl.ds(2 * pair + 1, 8, stride=8), :] = jnp.where(lane < 64, other, both)
    table = [[jnp.broadcast_to(table_ref[d : d + 1, r : r + 1], (8, 128)) for r in range(16)] for d in range(3)]
    perm = [[], [], []]
    for x in range(8):
        kind = kinds[x * 8 : x * 8 + 8, :]
        for d in range(3):
            value = table[d][0]
            for r in range(1, 16):
                value = jnp.where(kind == r, table[d][r], value)
            perm[d].append(value)
    perm_send[0] = perm[0][0]
    perm_send[1] = perm[0][7]
    for x in range(8):
        perm_send[2, pl.ds(x, 1), :] = perm[1][x][0:1]
        perm_send[3, pl.ds(x, 1), :] = perm[1][x][7:8]

    uu[...] = jnp.zeros((256, 256), F32)
    lax.fori_loop(0, 3, uu_chunk, 0)
    pl.semaphore_wait(barrier, 2 + (sec_count - 1) + (COLUMN - 1) + (PLANE - 1))
    perm_copies = [
        remote(perm_send.at[d], perm_recv.at[d ^ 1], ps_sem.at[d], pr_sem.at[d ^ 1], beside[d]) for d in range(4)
    ]
    for copy in perm_copies:
        copy.start()
    for g in range(TEAMS):
        for copy in halo_copies(0, g):
            copy.start()

    rate = rate_ref[...]
    top = rate.astype(BF16)
    rest = rate - top.astype(F32)
    middle = rest.astype(BF16)
    parts = jnp.concatenate([top, middle, (rest - middle.astype(F32)).astype(BF16)], 0)
    wells = cells_ref[...]
    cell = lax.broadcasted_iota(jnp.int32, (512, 256), 0)

    def place(x, carry):
        ids = ((gx * 8 + x) * (8 * sec_count) + sec * 8) * 64 + cell
        hits = jnp.where(ids == wells, 1.0, 0.0).astype(BF16)
        found = lax.dot_general(parts, hits, (((1,), (1,)), ((), ())), preferred_element_type=F32)
        found = found[:MEMB] + found[MEMB : 2 * MEMB] + found[2 * MEMB :]
        for y in range(8):
            pair = found[:, (y // 2) * 128 : (y // 2) * 128 + 128]
            pair = pair if y % 2 == 0 else pltpu.roll(pair, 64, 1)
            half = lax.broadcasted_iota(jnp.int32, (MEMB, 128), 1) < 64
            inflow[pl.ds(x * 8 + y, MEMB, stride=64), :] = jnp.where(half, DT_PRESSURE * pair, 0.0)
        return carry

    lax.fori_loop(0, 8, place, 0)
    lax.fori_loop(3, 5, uu_chunk, 0)

    z_up = jnp.where((lane & 63) == 63, 0.0, 1.0)
    z_down = jnp.where((lane & 63) == 0, 0.0, 1.0)
    for x in range(8):
        weights[4, x] = z_up * harmonic(perm[2][x], pltpu.roll(perm[2][x], 127, 1))
        weights[5, x] = z_down * harmonic(perm[2][x], pltpu.roll(perm[2][x], 1, 1))
    for copy in perm_copies:
        copy.wait()
    not_first_x = jnp.where(gx == 0, 0.0, 1.0)
    not_last_x = jnp.where(gx == gx_count - 1, 0.0, 1.0)
    not_first_y = jnp.where(sec == 0, 0.0, 1.0)
    not_last_y = jnp.where(sec == sec_count - 1, 0.0, 1.0)
    for x in range(8):
        above = perm[0][x + 1] if x < 7 else perm_recv[1] * not_last_x
        below = perm[0][x - 1] if x > 0 else perm_recv[0] * not_first_x
        weights[0, x] = harmonic(perm[0][x], above)
        weights[1, x] = harmonic(below, perm[0][x])
        right = jnp.broadcast_to(perm_recv[3, pl.ds(x, 1), :] * not_last_y, (8, 128))
        left = jnp.broadcast_to(perm_recv[2, pl.ds(x, 1), :] * not_first_y, (8, 128))
        weights[2, x] = harmonic(perm[1][x], jnp.where(row == 7, right, pltpu.roll(perm[1][x], 7, 0)))
        weights[3, x] = harmonic(jnp.where(row == 0, left, pltpu.roll(perm[1][x], 1, 0)), perm[1][x])

    step_sizes = jnp.where(lane < 64, DT_PRESSURE, DT_SATURATION)
    advect = jnp.where(lane < 64, 0.0, DT_ADVECT)

    def snap_copies(step):
        copies = [
            pltpu.make_async_copy(packed.at[step, sec], snaps_ref.at[step, pl.ds(sec * 8, 8)], own_sem.at[step])
        ]
        for ahead in range(1, sec_count):
            target = lax.rem(sec + ahead, sec_count)
            copies.append(
                remote(
                    packed.at[step, target], snaps_ref.at[step, pl.ds(sec * 8, 8)],
                    ss_sem.at[step, ahead], sr_sem.at[step, ahead], {"sec": target},
                )
            )
        return copies

    for step in range(STEPS):

        def team_step(g, carry):
            for copy in halo_copies(step, g):
                copy.wait()
            rows = pl.ds(pl.multiple_of(g * 8 * TEAM, 8 * TEAM), 8 * TEAM)
            y_wide[0, rows, :] = y_recv[step, 0, rows, :].astype(F32)
            y_wide[1, rows, :] = y_recv[step, 1, rows, :].astype(F32)

            def member(index, carry):
                m = g * TEAM + index
                base = pl.multiple_of(m * 64, 64)
                old = [out_ref[pl.ds(base + x * 8, 8), :] for x in range(8)]
                old_below = x_recv[step, 0, m].astype(F32)
                old_above = x_recv[step, 1, m].astype(F32)
                for x in range(8):
                    here = old[x]
                    left = jnp.broadcast_to(y_wide[0, pl.ds(m * 8 + x, 1), :], (8, 128))
                    right = jnp.broadcast_to(y_wide[1, pl.ds(m * 8 + x, 1), :], (8, 128))
                    besides = (
                        old[x + 1] if x < 7 else old_above,
                        old[x - 1] if x > 0 else old_below,
                        jnp.where(row == 7, right, pltpu.roll(here, 7, 0)),
                        jnp.where(row == 0, left, pltpu.roll(here, 1, 0)),
                        pltpu.roll(here, 127, 1),
                        pltpu.roll(here, 1, 1),
                    )
                    spread = carried = None
                    for d in range(6):
                        flow = weights[d, x] * (besides[d] - here)
                        pushed = pltpu.roll(flow, 64, 1)
                        moved = pushed * jnp.where(pushed > 0.0, besides[d], here)
                        spread = flow if spread is None else spread + flow
                        carried = moved if carried is None else carried + moved
                    fresh = here + step_sizes * spread + advect * carried + inflow[pl.ds(base + x * 8, 8), :]
                    out_ref[pl.ds(base + x * 8, 8), :] = fresh
                    turned[x, pl.ds(m, 8, stride=MEMB), :] = fresh
                    if step + 1 < STEPS and x in (0, 7):
                        x_send[step + 1, x // 7, m] = fresh.astype(BF16)
                return carry

            lax.fori_loop(0, TEAM, member, 0)
            if step + 1 < STEPS:
                stage_y(step + 1, g)
                for copy in halo_copies(step + 1, g):
                    copy.start()
            return carry

        lax.fori_loop(0, TEAMS, team_step, 0)
        for x in range(8):
            packed[step, x] = turned[x].reshape(8, MEMB, 128).astype(BF16)
        for copy in snap_copies(step):
            copy.start()
    lax.fori_loop(5, CHUNKS, uu_chunk, 0)
    for step in range(STEPS):
        for copy in snap_copies(step):
            copy.wait()

    def gram(pair, carry):
        su, ss = carry
        lhs = jnp.concatenate(
            [snaps_ref[:, 2 * pair].reshape(64, 128), snaps_ref[:, 2 * pair + 1].reshape(64, 128)], 1
        )
        rhs = basis[pl.ds(pl.multiple_of(pair * 256, 256), 256), :]
        su = su + jnp.dot(lhs, rhs, preferred_element_type=F32)
        ss = ss + lax.dot_general(lhs, lhs, (((1,), (1,)), ((), ())), preferred_element_type=F32)
        return su, ss

    su, ss = lax.fori_loop(
        0, 4 * sec_count, gram, (jnp.zeros((64, 256), F32), jnp.zeros((64, 64), F32)), unroll=4
    )
    zero = jnp.zeros((64, 64), F32)
    for index, block in enumerate(
        (
            su[:, :128],
            su[:, 128:],
            uu[0:64, 0:128],
            uu[0:64, 128:256],
            uu[64:128, 128:256],
            uu[128:192, 128:256],
            jnp.concatenate([uu[192:256, 192:256], uu[64:128, 64:128]], 1),
            jnp.concatenate([ss, zero], 1),
        )
    ):
        local[4 * index : 4 * index + 4] = block.reshape(4, SHARE, 128)

    slots[me] = local[me]

    def scatter(k):
        p = lax.rem(me + k, PLANE)
        return remote(local.at[p], slots.at[me], send1.at[k], recv1.at[k], in_plane(p))

    for k in range(1, PLANE):
        scatter(k).start()
    for k in range(1, PLANE):
        scatter(k).wait()
    total = slots[0]
    for k in range(1, PLANE):
        total = total + slots[k]
    partial[...] = total
    column[me_z] = total

    def across(k):
        q = lax.rem(me_z + k, COLUMN)
        return remote(partial, column.at[me_z], send2.at[k], recv2.at[k], in_column(q))

    for k in range(1, COLUMN):
        across(k).start()
    for k in range(1, COLUMN):
        across(k).wait()
    total = column[0]
    for k in range(1, COLUMN):
        total = total + column[k]
    sum_ref[me] = total

    def gather(k):
        p = lax.rem(me + k, PLANE)
        return remote(sum_ref.at[me], sum_ref.at[me], send3.at[k], recv3.at[k], in_plane(p))

    for k in range(1, PLANE):
        gather(k).start()
    for k in range(1, PLANE):
        gather(k).wait()


def slab(table, state, rock, cells, rate, basis):
    sec_count = lax.axis_size("sec")
    dma = pltpu.SemaphoreType.DMA
    in_vmem = pl.BlockSpec(memory_space=VMEM)
    return pl.pallas_call(
        slab_kernel,
        out_shape=(
            jax.ShapeDtypeStruct((MEMB * 64, 128), F32),
            jax.ShapeDtypeStruct((STEPS, 8 * sec_count, MEMB, 128), BF16),
            jax.ShapeDtypeStruct((PLANE, SHARE, 128), F32),
        ),
        in_specs=[pl.BlockSpec(memory_space=pltpu.HBM)] * 6,
        out_specs=(in_vmem,) * 3,
        scratch_shapes=[
            VMEM(table.shape, F32),
            VMEM(rock.shape, jnp.int32),
            VMEM(cells.shape, jnp.int32),
            VMEM(rate.shape, F32),
            VMEM(basis.shape, BF16),
            VMEM((256, 256), F32),
            VMEM((MEMB * 64, 128), F32),
            VMEM((64, 128), jnp.int32),
            VMEM((4, 8, 128), F32),
            VMEM((4, 8, 128), F32),
            VMEM((STEPS, 2, MEMB, 8, 128), BF16),
            VMEM((STEPS, 2, MEMB, 8, 128), BF16),
            VMEM((STEPS, 2, MEMB * 8, 128), BF16),
            VMEM((STEPS, 2, MEMB * 8, 128), BF16),
            VMEM((2, MEMB * 8, 128), F32),
            VMEM((6, 8, 8, 128), F32),
            VMEM((8, 8 * MEMB, 128), F32),
            VMEM((STEPS, 8, 8, MEMB, 128), BF16),
            VMEM((PLANE, SHARE, 128), F32),
            VMEM((PLANE, SHARE, 128), F32),
            VMEM((SHARE, 128), F32),
            VMEM((COLUMN, SHARE, 128), F32),
            dma((CHUNKS,)), dma((5,)), dma((4,)), dma((4,)), dma((STEPS, TEAMS, 4)), dma((STEPS, TEAMS, 4)),
            dma((STEPS, sec_count)), dma((STEPS, sec_count)), dma((STEPS,)),
            dma((PLANE,)), dma((PLANE,)), dma((COLUMN,)), dma((COLUMN,)), dma((PLANE,)), dma((PLANE,)),
        ],
        compiler_params=pltpu.CompilerParams(
            collective_id=0, has_side_effects=True, vmem_limit_bytes=40 * 1024 * 1024
        ),
        name="slab",
    )(*(pltpu.with_memory_space_constraint(x, pltpu.HBM) for x in (table, state.reshape(-1, 128), rock, cells, rate, basis)))


def rotate_kernel(basis_ref, snaps_ref, mix_ref, out_ref):
    taken = jnp.concatenate([snaps_ref[:, y].reshape(64, 128).T for y in range(8)], 0)
    lhs = jnp.concatenate([basis_ref[...], taken], 1)
    out_ref[...] = jnp.dot(lhs, mix_ref[...], preferred_element_type=F32).astype(BF16)


def rotate(basis, snaps, mix):
    rows = basis.shape[0]
    return pl.pallas_call(
        rotate_kernel,
        grid=(rows // 1024,),
        out_shape=jax.ShapeDtypeStruct(basis.shape, BF16),
        in_specs=[
            pl.BlockSpec((1024, 256), lambda i: (i, 0)),
            pl.BlockSpec((STEPS, 8, MEMB, 128), lambda i: (0, i, 0, 0)),
            pl.BlockSpec((320, 256), lambda i: (0, 0)),
        ],
        out_specs=pl.BlockSpec((1024, 256), lambda i: (i, 0)),
        compiler_params=pltpu.CompilerParams(vmem_limit_bytes=24 * 1024 * 1024),
        name="rotate",
    )(basis, snaps, mix)


def dot(a, b, contract=((1,), (0,))):
    a1, b1 = a.astype(BF16), b.astype(BF16)
    a2, b2 = (a - a1.astype(F32)).astype(BF16), (b - b1.astype(F32)).astype(BF16)

    def one(x, y):
        return lax.dot_general(x, y, (contract, ((), ())), preferred_element_type=F32)

    return one(a1, b1) + (one(a1, b2) + one(a2, b1))


ROWS_BASIS = 256
RANK = 32
BLOCK = 8
STRIDE = RANK + BLOCK


def spread_row(ref, at):
    return jnp.broadcast_to(ref[pl.ds(at, 1), :], (8, 128))


def factor(c, gram, sigma, mx, ct, first, second, coef, yy, nat):
    lane = lax.broadcasted_iota(jnp.int32, (8, 128), 1)
    row = lax.broadcasted_iota(jnp.int32, (8, 128), 0)
    group = lane // 32
    g0, g1, g2 = group == 0, group == 1, group == 2

    def wide(mask, rows):
        return jnp.concatenate([mask] * (rows // 8), 0)

    def turn(x, by):
        return pltpu.roll(x, by, 1)

    padded = jnp.concatenate([c, jnp.broadcast_to(sigma, (96, ROWS_BASIS))], 0)
    ct[...] = padded.T
    sig_col = turn(ct[...], 96)
    sig_col = jnp.where(wide(lane, ROWS_BASIS) < 96, sig_col, turn(sig_col, 32))
    inv2 = 1.0 / (sig_col * sig_col)

    at = lax.broadcasted_iota(jnp.int32, (ROWS_BASIS, 128), 0)
    over = lax.broadcasted_iota(jnp.int32, (ROWS_BASIS, 128), 1)
    before = at < BLOCK * (over & 31)
    pick = over // 32
    masks = jnp.where(
        pick == 0, jnp.where(before, inv2 * inv2, 0.0),
        jnp.where(pick == 1, jnp.where(before, inv2, 0.0), jnp.where((pick == 2) & ~before, 1.0, 0.0)),
    )
    low = lax.broadcasted_iota(jnp.int32, (RANK, 128), 0)
    lanes = wide(group, RANK)
    for chunk in range(4):
        pairs = jnp.concatenate([c * c[a : a + 1] for a in range(chunk * 8, chunk * 8 + 8)], 0)
        sums = dot(pairs, masks)
        for i in range(8):
            a = chunk * 8 + i
            mx[a * STRIDE : a * STRIDE + RANK, :] = (
                sums[i * RANK : (i + 1) * RANK]
                + jnp.where((lanes == 1) & (low == a), 1.0, 0.0)
                + jnp.where(lanes == 2, jnp.broadcast_to(gram[:, a : a + 1], (RANK, 128)), 0.0)
            )
    fourth = []
    for half in range(2):
        mixed = jnp.concatenate([ct[pl.ds(half * 4 + t, 32, stride=8), :] for t in range(4)], 0).T
        for t in range(4):
            here = mixed if t == 0 else turn(mixed, 128 - 32 * t)
            r1 = here[:RANK]
            sig = here[RANK : 2 * RANK]
            r2 = sig * sig * r1
            mx[pl.ds(RANK + half * 4 + t, RANK, stride=STRIDE), :] = jnp.where(
                lanes == 0, r1, jnp.where(lanes == 2, -turn(r2, 64), 0.0)
            )
            sq = sig[:8] * sig[:8]
            fourth.append(sq * sq)

    acc = tuple(jnp.zeros((8, 128), F32) for _ in range(BLOCK))
    for part in range(4):
        skip = part * 8
        count = RANK - skip
        w0, w1, w2 = wide(g0, count), wide(g1, count), wide(g2, count)

        def step(k, acc):
            base = pl.multiple_of(k * STRIDE, 8)
            rk = mx[pl.ds(base + skip, count), :]
            ck = mx[pl.ds(skip * STRIDE + k, count, stride=STRIDE), :]
            pivot = spread_row(mx, base + k)
            up, down, across = turn(pivot, 32), turn(pivot, 96), turn(pivot, 64)
            p = jnp.where(g0, pivot, jnp.where(g1, up, across))
            e = jnp.where(g0, down, jnp.where(g1, pivot, up))
            q = jnp.where(g0, across, jnp.where(g1, down, pivot))
            det = 1.0 / (p * q + e * e)
            p, e, q = p * det, e * det, q * det
            pw, ew, qw = (jnp.concatenate([z] * (count // 8), 0) for z in (p, e, q))
            rk_up, rk_down, ck_down = turn(rk, 32), turn(rk, 96), turn(ck, 96)
            u = jnp.where(w2, rk_up, jnp.where(w1, rk, rk))
            v = jnp.where(w0, ck_down, jnp.where(w1, -rk_down, -rk))
            fa = qw * u + ew * v
            sa = ew * u - pw * v
            first[pl.ds(pl.multiple_of(k * RANK, 8) + skip, count), :] = fa
            second[pl.ds(pl.multiple_of(k * RANK, 8) + skip, count), :] = sa
            coef[0, skip:RANK, :] = jnp.where(w0, rk, jnp.where(w1, rk_up, -rk_up))
            coef[1, skip:RANK, :] = jnp.where(w0, ck_down, ck)
            right = mx[pl.ds(base + RANK, 8), :]
            swapped = turn(right, 64)
            u = jnp.where(g0, right, swapped)
            v = jnp.where(g0, -swapped, -right)
            fr = q * u + e * v
            sr = e * u - p * v
            yy[pl.ds(pl.multiple_of(k * 8, 8), 8), :] = jnp.where(g0, fr, turn(sr, 32))
            acc = tuple(
                acc[t]
                + jnp.broadcast_to(u[t : t + 1], (8, 128)) * fr
                + jnp.broadcast_to(v[t : t + 1], (8, 128)) * sr
                for t in range(BLOCK)
            )
            fall = jnp.concatenate([fa, fr], 0)
            sall = jnp.concatenate([sa, sr], 0)
            for i in range(skip, RANK):
                f = jnp.broadcast_to(coef[0, i : i + 1, :], (8, 128))
                s = jnp.broadcast_to(coef[1, i : i + 1, :], (8, 128))
                for part8 in range(count // 8 + 1):
                    where = i * STRIDE + skip + part8 * 8
                    mx[where : where + 8, :] = mx[where : where + 8, :] - (
                        f * fall[part8 * 8 : part8 * 8 + 8] + s * sall[part8 * 8 : part8 * 8 + 8]
                    )
            return acc

        acc = lax.fori_loop(skip, skip + 8, step, acc)

    ys = [None] * RANK
    for k in range(RANK - 1, -1, -1):
        y = yy[k * 8 : k * 8 + 8, :]
        if k < RANK - 1:
            a1 = a2 = None
            for l in range(RANK - 1, k, -1):
                m1 = spread_row(first, k * RANK + l) * ys[l]
                m2 = spread_row(second, k * RANK + l) * ys[l]
                a1 = m1 if a1 is None else a1 + m1
                a2 = m2 if a2 is None else a2 + m2
            y = y - jnp.where(g0, a1 + turn(a1, 96), a2 + turn(a2, 32))
        ys[k] = y

    block = [acc[t] + jnp.where(row == t, fourth[t], 0.0) for t in range(BLOCK)]
    scale = jnp.zeros((8, 128), F32)
    steps = []
    for s in range(BLOCK):
        d = jnp.broadcast_to(block[s][s : s + 1], (8, 128))
        scale = jnp.where(row == s, lax.rsqrt(d), scale)
        ratio = jnp.where(row > s, block[s] / d, 0.0)
        steps.append(ratio)
        for t in range(s + 1, BLOCK):
            block[t] = block[t] - jnp.broadcast_to(block[s][t : t + 1], (8, 128)) * ratio
    for index in range(2 * RANK + BLOCK):
        if index < RANK:
            value = ys[index]
        elif index < 2 * RANK:
            value = turn(ys[index - RANK], 96)
        else:
            value = jnp.where(row == index - 2 * RANK, 1.0, 0.0)
        for s in range(BLOCK - 1):
            value = value - steps[s] * jnp.broadcast_to(value[s : s + 1], (8, 128))
        yy[index * 8 : index * 8 + 8, :] = value * scale
    for half in range(2):
        mixed = None
        for t in range(4):
            part = yy[pl.ds(half * 4 + t, 128, stride=8), :]
            part = part if t == 0 else turn(part, 32 * t)
            mixed = part if t == 0 else jnp.where(wide(group, 128) == t, part, mixed)
        mixed = mixed.T
        for t in range(4):
            nat[pl.ds(half * 4 + t, 32, stride=8), :] = mixed[32 * t : 32 * t + 32]

    inv_row = 1.0 / (sigma * sigma)
    weighed = jnp.concatenate([c * (inv_row * inv_row), c * inv_row], 0)
    across = lax.broadcasted_iota(jnp.int32, (ROWS_BASIS, ROWS_BASIS), 1)
    down = lax.broadcasted_iota(jnp.int32, (ROWS_BASIS, ROWS_BASIS), 0)
    tile = jnp.where(
        (lax.broadcasted_iota(jnp.int32, (BLOCK, ROWS_BASIS), 1) & 7)
        == lax.broadcasted_iota(jnp.int32, (BLOCK, ROWS_BASIS), 0), 1.0, 0.0
    )
    natural = nat[...]
    below = -dot(natural[:, : 2 * RANK], weighed)
    own = dot(natural[:, 2 * RANK : 2 * RANK + BLOCK], tile)
    inverse = jnp.where(across // 8 < down // 8, below, jnp.where(across // 8 == down // 8, own, 0.0))
    return inverse, sig_col


def batch_update(c, rounded, gram, sigma, *scratch):
    inverse, sig_col = factor(c, gram, sigma, *scratch)
    sig = jnp.concatenate([sig_col, sig_col], 1)
    on_snaps = dot(c, inverse, ((1,), (1,)))
    scaled = sig * sig * inverse.T
    total = scaled + dot(c, on_snaps, ((0,), (0,)))
    on_basis = scaled + dot(c - rounded, on_snaps, ((0,), (0,)))
    top = sig * total
    bottom = dot(c, total) + dot(gram, on_snaps)
    energy = jnp.sum(top * top, axis=0, keepdims=True) + jnp.sum(bottom * bottom, axis=0, keepdims=True)
    return on_basis, on_snaps, jnp.sqrt(energy)


def by_batch(x):
    return jnp.concatenate([x[16 * step + 8 * g : 16 * step + 8 * g + 8] for g in range(2) for step in range(4)], 0)


def small_kernel(
    rows_total, whole_ref, sigma_ref, fields_ref, mix_ref, sigma_out_ref, fields_out, half_uu, copy_sem, *scratch
):
    writing = pltpu.make_async_copy(fields_ref, fields_out, copy_sem)
    writing.start()
    scale = 1.0 / rows_total

    def piece(index):
        return whole_ref[64 * index : 64 * (index + 1), :] * scale

    high = lax.broadcasted_iota(jnp.int32, (64, 128), 1) >= 64
    last = piece(6)
    half_uu[...] = jnp.zeros((256, 256), F32)
    half_uu[0:64, 0:128] = jnp.where(high, 1.0, 0.5) * piece(2)
    half_uu[0:64, 128:256] = piece(3)
    half_uu[64:128, 0:128] = jnp.where(high, 0.5 * last, 0.0)
    half_uu[64:128, 128:256] = piece(4)
    half_uu[128:192, 128:256] = jnp.where(high, 1.0, 0.5) * piece(5)
    half_uu[192:256, 128:256] = jnp.where(high, 0.5 * pltpu.roll(last, 64, 1), 0.0)
    su = by_batch(jnp.concatenate([piece(0), piece(1)], 1))
    source = lax.broadcasted_iota(jnp.int32, (64, 64), 0)
    target = lax.broadcasted_iota(jnp.int32, (64, 64), 1)
    wanted = (target // 8 % 4) * 16 + (target // 32) * 8 + (target & 7)
    ss = dot(by_batch(piece(7)[:, :64]), jnp.where(source == wanted, 1.0, 0.0))
    s00, s10, s11 = ss[:32, :32], ss[32:, :32], ss[32:, 32:]

    def of_basis(x):
        part = dot(dot(x, half_uu[...]), x, ((1,), (1,)))
        return part + part.T

    def twice(c, r):
        part = dot(c, r, ((1,), (1,)))
        return part + part.T

    c0 = su[:32]
    r0 = c0.astype(BF16).astype(F32)
    gram0 = s00 - twice(c0, r0) + of_basis(r0)
    wu, ws, sigma1 = batch_update(c0, r0, gram0, sigma_ref[...], *scratch)
    c1 = dot(su[32:], wu) + dot(s10, ws)
    r1 = c1.astype(BF16).astype(F32)
    yu = dot(r1, wu, ((1,), (1,)))
    ys = dot(r1, ws, ((1,), (1,)))
    cross = dot(dot(ys, c0), yu, ((1,), (1,)))
    gram1 = s11 - twice(c1, r1) + of_basis(yu) + cross + cross.T + dot(dot(ys, s00), ys, ((1,), (1,)))
    wu1, ws1, sigma2 = batch_update(c1, r1, gram1, sigma1, *scratch)
    mix_ref[0:256, :] = dot(wu, wu1).astype(BF16)
    w0, w1 = dot(ws, wu1), ws1
    mix_ref[256:320, :] = jnp.concatenate(
        [w[8 * step : 8 * step + 8] for step in range(4) for w in (w0, w1)], 0
    ).astype(BF16)
    sigma_out_ref[...] = sigma2
    writing.wait()


def small_algebra(whole, sigma, fields, rows_total):
    return pl.pallas_call(
        lambda *refs: small_kernel(float(rows_total), *refs),
        out_shape=(jax.ShapeDtypeStruct((320, 256), BF16), jax.ShapeDtypeStruct((1, 256), F32), jax.ShapeDtypeStruct(fields.shape, F32)),
        in_specs=[pl.BlockSpec(memory_space=VMEM)] * 3,
        out_specs=(pl.BlockSpec(memory_space=VMEM),) * 2 + (pl.BlockSpec(memory_space=pltpu.HBM),),
        scratch_shapes=[
            VMEM((256, 256), F32),
            pltpu.SemaphoreType.DMA,
            VMEM((RANK * STRIDE, 128), F32),
            VMEM((256, 128), F32),
            VMEM((RANK * RANK, 128), F32),
            VMEM((RANK * RANK, 128), F32),
            VMEM((2, RANK, 128), F32),
            VMEM((128 * 8, 128), F32),
            VMEM((256, 128), F32),
        ],
        compiler_params=pltpu.CompilerParams(vmem_limit_bytes=32 * 1024 * 1024),
        name="small_algebra",
    )(whole, sigma.reshape(1, -1), fields)


def body(state_init, rock_type, perm_table, well_cells, well_rate, basis_in, singular):
    basis = basis_in.reshape(-1, basis_in.shape[-1])
    rows_total = basis.shape[0] * lax.axis_size("gx") * lax.axis_size("sec")
    final, snaps, whole = slab(perm_table, state_init, rock_type, well_cells.reshape(1, -1), well_rate, basis)
    mix, sigma, final = small_algebra(whole.reshape(-1, 128), singular, final, rows_total)
    fresh = rotate(basis, snaps, mix)
    return (final.reshape(state_init.shape), fresh.reshape(basis_in.shape), sigma.reshape(-1))


def solution(mesh):
    return jax.shard_map(
        body,
        mesh=mesh,
        in_specs=(
            P(None, "gx", "sec", None),
            P("gx", "sec"),
            P(),
            P(),
            P(),
            P(("gx", "sec"), None, None, None),
            P(),
        ),
        out_specs=(P(None, "gx", "sec", None), P(("gx", "sec"), None, None, None), P()),
        check_vma=False,
    )
```

```python
import jax
import jax.numpy as jnp
from jax import lax
from jax.experimental import pallas as pl
from jax.experimental.pallas import tpu as pltpu
from jax.sharding import PartitionSpec as P

MG = 8
STEPS = 4
GROUPS = 2
MEMB = MG * GROUPS

DT_PRESSURE = 0.12
DT_SATURATION = 0.06
DT_ADVECT = 0.15

MESH = pl.DeviceIdType.MESH
VMEM = pltpu.VMEM
F32 = jnp.float32
BF16 = jnp.bfloat16


def harmonic(left, right):
    return 2.0 * left * right / (left + right)


def remote(src, dst, send_sem, recv_sem, device):
    return pltpu.make_async_remote_copy(
        src_ref=src, dst_ref=dst, send_sem=send_sem, recv_sem=recv_sem, device_id=device, device_id_type=MESH
    )


PLANE = 32
COLUMN = 8


SHARE = 16
CHUNKS = 8
TEAMS = 4
TEAM = MEMB // TEAMS


def slab_kernel(
    table_hbm, state_hbm, rock_hbm, cells_hbm, rate_hbm, basis_hbm, out_ref, snaps_ref, sum_ref,
    table_ref, rock_ref, cells_ref, rate_ref, fields, basis, uu, inflow, kinds, perm_send, perm_recv, x_send, x_recv, y_send, y_recv, y_wide, weights, turned, packed,
    local, slots, partial, column,
    load_sem, in_sem, ps_sem, pr_sem, hs_sem, hr_sem, ss_sem, sr_sem, own_sem, send1, recv1, send2, recv2, send3, recv3,
):
    gx_count, sec_count = lax.axis_size("gx"), lax.axis_size("sec")
    gx, sec = lax.axis_index("gx"), lax.axis_index("sec")
    beside = (
        {"gx": lax.rem(gx + gx_count - 1, gx_count)},
        {"gx": lax.rem(gx + 1, gx_count)},
        {"sec": lax.rem(sec + sec_count - 1, sec_count)},
        {"sec": lax.rem(sec + 1, sec_count)},
    )
    z_hi, z_lo = lax.rem(gx // 2, 4), sec // 4
    me = (gx // 8) * 8 + lax.rem(gx, 2) * 4 + lax.rem(sec, 4)
    me_z = z_hi * 2 + z_lo

    def in_plane(p):
        return {"gx": (p // 8) * 8 + z_hi * 2 + lax.rem(p // 4, 2), "sec": z_lo * 4 + lax.rem(p, 4)}

    def in_column(q):
        return {"gx": (gx // 8) * 8 + (q // 2) * 2 + lax.rem(gx, 2), "sec": lax.rem(q, 2) * 4 + lax.rem(sec, 4)}

    barrier = pltpu.get_barrier_semaphore()

    def greet(device):
        pl.semaphore_signal(barrier, inc=1, device_id=device, device_id_type=MESH)

    greet(beside[0])
    greet(beside[1])
    for ahead in range(1, sec_count):
        greet({"sec": lax.rem(sec + ahead, sec_count)})
    for k in range(1, COLUMN):
        greet(in_column(lax.rem(me_z + k, COLUMN)))
    for k in range(1, PLANE):
        greet(in_plane(lax.rem(me + k, PLANE)))

    def load(c):
        rows = pl.ds(pl.multiple_of(c * 1024, 1024), 1024)
        return pltpu.make_async_copy(basis_hbm.at[rows], basis.at[rows], load_sem.at[c])

    arriving = [
        pltpu.make_async_copy(src, dst, in_sem.at[i])
        for i, (src, dst) in enumerate(
            ((table_hbm, table_ref), (state_hbm, out_ref), (rock_hbm, rock_ref), (rate_hbm, rate_ref), (cells_hbm, cells_ref))
        )
    ]
    for copy in arriving:
        copy.start()
    for c in range(CHUNKS):
        load(c).start()

    lane = lax.broadcasted_iota(jnp.int32, (8, 128), 1)
    row = lax.broadcasted_iota(jnp.int32, (8, 128), 0)

    def uu_chunk(c, carry):
        load(c).wait()
        part = basis[pl.ds(pl.multiple_of(c * 1024, 1024), 1024), :]
        tn = (((0,), (0,)), ((), ()))
        uu[0:128, :] += lax.dot_general(part[:, :128], part, tn, preferred_element_type=F32)
        uu[128:256, 128:256] += lax.dot_general(part[:, 128:], part[:, 128:], tn, preferred_element_type=F32)
        return carry

    def halo_copies(step, g):
        copies = []
        for d in range(4):
            if d < 2:
                src = x_send.at[step, d, pl.ds(g * TEAM, TEAM)]
                dst = x_recv.at[step, 1 - d, pl.ds(g * TEAM, TEAM)]
            else:
                rows = pl.ds(pl.multiple_of(g * 8 * TEAM, 8 * TEAM), 8 * TEAM)
                src = y_send.at[step, d - 2, rows]
                dst = y_recv.at[step, 3 - d, rows]
            copies.append(remote(src, dst, hs_sem.at[step, g, d], hr_sem.at[step, g, d ^ 1], beside[d]))
        return copies

    def stage_y(step, g):
        for side, y in ((0, 0), (1, 7)):
            rows = pl.ds(pl.multiple_of(g * 8 * TEAM, 8 * TEAM), 8 * TEAM)
            y_send[step, side, rows, :] = fields[pl.ds(g * 64 * TEAM + y, 8 * TEAM, stride=8), :].astype(BF16)

    low_half = lane < 64

    def first(q, carry):
        base = pl.multiple_of(q * 128, 128)
        for x in range(8):
            a = out_ref[pl.ds(base + x * 8, 8), :]
            b = out_ref[pl.ds(base + 64 + x * 8, 8), :]
            p = jnp.where(low_half, a, pltpu.roll(b, 64, 1))
            s = jnp.where(low_half, pltpu.roll(a, 64, 1), b)
            fields[pl.ds(base + x * 8, 8), :] = p
            fields[pl.ds(base + 64 + x * 8, 8), :] = s
            if x in (0, 7):
                x_send[0, x // 7, 2 * q] = p.astype(BF16)
                x_send[0, x // 7, 2 * q + 1] = s.astype(BF16)
        return carry

    for copy in arriving:
        copy.wait()
    lax.fori_loop(0, MEMB // 2, first, 0)
    for g in range(TEAMS):
        stage_y(0, g)

    for pair in range(4):
        both = rock_ref[:, pair * 128 : pair * 128 + 128]
        other = pltpu.roll(both, 64, 1)
        kinds[pl.ds(2 * pair, 8, stride=8), :] = jnp.where(lane < 64, both, other)
        kinds[pl.ds(2 * pair + 1, 8, stride=8), :] = jnp.where(lane < 64, other, both)
    table = [[jnp.broadcast_to(table_ref[d : d + 1, r : r + 1], (8, 128)) for r in range(16)] for d in range(3)]
    perm = [[], [], []]
    for x in range(8):
        kind = kinds[x * 8 : x * 8 + 8, :]
        for d in range(3):
            value = table[d][0]
            for r in range(1, 16):
                value = jnp.where(kind == r, table[d][r], value)
            perm[d].append(value)
    perm_send[0] = perm[0][0]
    perm_send[1] = perm[0][7]
    for x in range(8):
        perm_send[2, pl.ds(x, 1), :] = perm[1][x][0:1]
        perm_send[3, pl.ds(x, 1), :] = perm[1][x][7:8]

    uu[...] = jnp.zeros((256, 256), F32)
    lax.fori_loop(0, 3, uu_chunk, 0)
    pl.semaphore_wait(barrier, 2 + (sec_count - 1) + (COLUMN - 1) + (PLANE - 1))
    perm_copies = [
        remote(perm_send.at[d], perm_recv.at[d ^ 1], ps_sem.at[d], pr_sem.at[d ^ 1], beside[d]) for d in range(4)
    ]
    for copy in perm_copies:
        copy.start()
    for g in range(TEAMS):
        for copy in halo_copies(0, g):
            copy.start()

    rate = jnp.concatenate([rate_ref[m : m + 1, :] for start in range(2) for m in range(start, MEMB, 2)], 0)
    top = rate.astype(BF16)
    rest = rate - top.astype(F32)
    middle = rest.astype(BF16)
    parts = jnp.concatenate([top, middle, (rest - middle.astype(F32)).astype(BF16)], 0)
    wells = cells_ref[...]
    cell = lax.broadcasted_iota(jnp.int32, (512, 256), 0)

    def place(x, carry):
        ids = ((gx * 8 + x) * (8 * sec_count) + sec * 8) * 64 + cell
        hits = jnp.where(ids == wells, 1.0, 0.0).astype(BF16)
        found = lax.dot_general(parts, hits, (((1,), (1,)), ((), ())), preferred_element_type=F32)
        found = found[:MEMB] + found[MEMB : 2 * MEMB] + found[2 * MEMB :]
        for y in range(8):
            columns = slice((y // 2) * 128, (y // 2) * 128 + 128)
            even, odd = found[:8, columns], found[8:, columns]
            if y % 2 == 0:
                both = jnp.where(low_half, even, pltpu.roll(odd, 64, 1))
            else:
                both = jnp.where(low_half, pltpu.roll(even, 64, 1), odd)
            inflow[pl.ds(x * 8 + y, 8, stride=64), :] = DT_PRESSURE * both
        return carry

    lax.fori_loop(0, 8, place, 0)
    lax.fori_loop(3, 5, uu_chunk, 0)

    z_up = jnp.where((lane & 63) == 63, 0.0, 1.0)
    z_down = jnp.where((lane & 63) == 0, 0.0, 1.0)
    for x in range(8):
        weights[4, x] = z_up * harmonic(perm[2][x], pltpu.roll(perm[2][x], 127, 1))
        weights[5, x] = z_down * harmonic(perm[2][x], pltpu.roll(perm[2][x], 1, 1))
    for copy in perm_copies:
        copy.wait()
    not_first_x = jnp.where(gx == 0, 0.0, 1.0)
    not_last_x = jnp.where(gx == gx_count - 1, 0.0, 1.0)
    not_first_y = jnp.where(sec == 0, 0.0, 1.0)
    not_last_y = jnp.where(sec == sec_count - 1, 0.0, 1.0)
    for x in range(8):
        above = perm[0][x + 1] if x < 7 else perm_recv[1] * not_last_x
        below = perm[0][x - 1] if x > 0 else perm_recv[0] * not_first_x
        weights[0, x] = harmonic(perm[0][x], above)
        weights[1, x] = harmonic(below, perm[0][x])
        right = jnp.broadcast_to(perm_recv[3, pl.ds(x, 1), :] * not_last_y, (8, 128))
        left = jnp.broadcast_to(perm_recv[2, pl.ds(x, 1), :] * not_first_y, (8, 128))
        weights[2, x] = harmonic(perm[1][x], jnp.where(row == 7, right, pltpu.roll(perm[1][x], 7, 0)))
        weights[3, x] = harmonic(jnp.where(row == 0, left, pltpu.roll(perm[1][x], 1, 0)), perm[1][x])

    def snap_copies(step):
        copies = [
            pltpu.make_async_copy(packed.at[step, sec], snaps_ref.at[step, pl.ds(sec * 8, 8)], own_sem.at[step])
        ]
        for ahead in range(1, sec_count):
            target = lax.rem(sec + ahead, sec_count)
            copies.append(
                remote(
                    packed.at[step, target], snaps_ref.at[step, pl.ds(sec * 8, 8)],
                    ss_sem.at[step, ahead], sr_sem.at[step, ahead], {"sec": target},
                )
            )
        return copies

    for step in range(STEPS):

        def team_step(g, carry):
            for copy in halo_copies(step, g):
                copy.wait()
            rows = pl.ds(pl.multiple_of(g * 8 * TEAM, 8 * TEAM), 8 * TEAM)
            y_wide[0, rows, :] = y_recv[step, 0, rows, :].astype(F32)
            y_wide[1, rows, :] = y_recv[step, 1, rows, :].astype(F32)

            def pair_step(index, carry):
                q = g * (TEAM // 2) + index
                base = pl.multiple_of(q * 128, 128)
                ps = [fields[pl.ds(base + x * 8, 8), :] for x in range(8)]
                ss = [fields[pl.ds(base + 64 + x * 8, 8), :] for x in range(8)]
                ends = [[x_recv[step, side, 2 * q + i].astype(F32) for side in range(2)] for i in range(2)]

                def besides(all_x, x, i):
                    here = all_x[x]
                    at = (2 * q + i) * 8 + x
                    left = jnp.broadcast_to(y_wide[0, pl.ds(at, 1), :], (8, 128))
                    right = jnp.broadcast_to(y_wide[1, pl.ds(at, 1), :], (8, 128))
                    return (
                        all_x[x + 1] if x < 7 else ends[i][1],
                        all_x[x - 1] if x > 0 else ends[i][0],
                        jnp.where(row == 7, right, pltpu.roll(here, 7, 0)),
                        jnp.where(row == 0, left, pltpu.roll(here, 1, 0)),
                        pltpu.roll(here, 127, 1),
                        pltpu.roll(here, 1, 1),
                    )

                for x in range(8):
                    p, s = ps[x], ss[x]
                    p_beside, s_beside = besides(ps, x, 0), besides(ss, x, 1)
                    p_spread = s_spread = carried = None
                    for d in range(6):
                        weight = weights[d, x]
                        flow = weight * (p_beside[d] - p)
                        spread = weight * (s_beside[d] - s)
                        moved = flow * jnp.where(flow > 0.0, s_beside[d], s)
                        p_spread = flow if p_spread is None else p_spread + flow
                        s_spread = spread if s_spread is None else s_spread + spread
                        carried = moved if carried is None else carried + moved
                    p = p + DT_PRESSURE * p_spread + inflow[pl.ds(pl.multiple_of(q * 64 + x * 8, 8), 8), :]
                    s = s + DT_SATURATION * s_spread + DT_ADVECT * carried
                    a = jnp.where(low_half, p, pltpu.roll(s, 64, 1))
                    b = jnp.where(low_half, pltpu.roll(p, 64, 1), s)
                    turned[x, pl.ds(2 * q, 8, stride=MEMB), :] = a
                    turned[x, pl.ds(2 * q + 1, 8, stride=MEMB), :] = b
                    if step + 1 < STEPS:
                        fields[pl.ds(base + x * 8, 8), :] = p
                        fields[pl.ds(base + 64 + x * 8, 8), :] = s
                        if x in (0, 7):
                            x_send[step + 1, x // 7, 2 * q] = p.astype(BF16)
                            x_send[step + 1, x // 7, 2 * q + 1] = s.astype(BF16)
                    else:
                        out_ref[pl.ds(base + x * 8, 8), :] = a
                        out_ref[pl.ds(base + 64 + x * 8, 8), :] = b
                return carry

            lax.fori_loop(0, TEAM // 2, pair_step, 0)
            if step + 1 < STEPS:
                stage_y(step + 1, g)
                for copy in halo_copies(step + 1, g):
                    copy.start()
            return carry

        lax.fori_loop(0, TEAMS, team_step, 0)
        for x in range(8):
            packed[step, x] = turned[x].reshape(8, MEMB, 128).astype(BF16)
        for copy in snap_copies(step):
            copy.start()
    lax.fori_loop(5, CHUNKS, uu_chunk, 0)
    for step in range(STEPS):
        for copy in snap_copies(step):
            copy.wait()

    def gram(pair, carry):
        su, ss = carry
        lhs = jnp.concatenate(
            [snaps_ref[:, 2 * pair].reshape(64, 128), snaps_ref[:, 2 * pair + 1].reshape(64, 128)], 1
        )
        rhs = basis[pl.ds(pl.multiple_of(pair * 256, 256), 256), :]
        su = su + jnp.dot(lhs, rhs, preferred_element_type=F32)
        ss = ss + lax.dot_general(lhs, lhs, (((1,), (1,)), ((), ())), preferred_element_type=F32)
        return su, ss

    su, ss = lax.fori_loop(
        0, 4 * sec_count, gram, (jnp.zeros((64, 256), F32), jnp.zeros((64, 64), F32)), unroll=4
    )
    zero = jnp.zeros((64, 64), F32)
    for index, block in enumerate(
        (
            su[:, :128],
            su[:, 128:],
            uu[0:64, 0:128],
            uu[0:64, 128:256],
            uu[64:128, 128:256],
            uu[128:192, 128:256],
            jnp.concatenate([uu[192:256, 192:256], uu[64:128, 64:128]], 1),
            jnp.concatenate([ss, zero], 1),
        )
    ):
        local[4 * index : 4 * index + 4] = block.reshape(4, SHARE, 128)

    slots[me] = local[me]

    def scatter(k):
        p = lax.rem(me + k, PLANE)
        return remote(local.at[p], slots.at[me], send1.at[k], recv1.at[k], in_plane(p))

    for k in range(1, PLANE):
        scatter(k).start()
    for k in range(1, PLANE):
        scatter(k).wait()
    total = slots[0]
    for k in range(1, PLANE):
        total = total + slots[k]
    partial[...] = total
    column[me_z] = total

    def across(k):
        q = lax.rem(me_z + k, COLUMN)
        return remote(partial, column.at[me_z], send2.at[k], recv2.at[k], in_column(q))

    for k in range(1, COLUMN):
        across(k).start()
    for k in range(1, COLUMN):
        across(k).wait()
    total = column[0]
    for k in range(1, COLUMN):
        total = total + column[k]
    sum_ref[me] = total

    def gather(k):
        p = lax.rem(me + k, PLANE)
        return remote(sum_ref.at[me], sum_ref.at[me], send3.at[k], recv3.at[k], in_plane(p))

    for k in range(1, PLANE):
        gather(k).start()
    for k in range(1, PLANE):
        gather(k).wait()


def slab(table, state, rock, cells, rate, basis):
    sec_count = lax.axis_size("sec")
    dma = pltpu.SemaphoreType.DMA
    in_vmem = pl.BlockSpec(memory_space=VMEM)
    return pl.pallas_call(
        slab_kernel,
        out_shape=(
            jax.ShapeDtypeStruct((MEMB * 64, 128), F32),
            jax.ShapeDtypeStruct((STEPS, 8 * sec_count, MEMB, 128), BF16),
            jax.ShapeDtypeStruct((PLANE, SHARE, 128), F32),
        ),
        in_specs=[pl.BlockSpec(memory_space=pltpu.HBM)] * 6,
        out_specs=(in_vmem,) * 3,
        scratch_shapes=[
            VMEM(table.shape, F32),
            VMEM(rock.shape, jnp.int32),
            VMEM(cells.shape, jnp.int32),
            VMEM(rate.shape, F32),
            VMEM((MEMB * 64, 128), F32),
            VMEM(basis.shape, BF16),
            VMEM((256, 256), F32),
            VMEM((MEMB * 32, 128), F32),
            VMEM((64, 128), jnp.int32),
            VMEM((4, 8, 128), F32),
            VMEM((4, 8, 128), F32),
            VMEM((STEPS, 2, MEMB, 8, 128), BF16),
            VMEM((STEPS, 2, MEMB, 8, 128), BF16),
            VMEM((STEPS, 2, MEMB * 8, 128), BF16),
            VMEM((STEPS, 2, MEMB * 8, 128), BF16),
            VMEM((2, MEMB * 8, 128), F32),
            VMEM((6, 8, 8, 128), F32),
            VMEM((8, 8 * MEMB, 128), F32),
            VMEM((STEPS, 8, 8, MEMB, 128), BF16),
            VMEM((PLANE, SHARE, 128), F32),
            VMEM((PLANE, SHARE, 128), F32),
            VMEM((SHARE, 128), F32),
            VMEM((COLUMN, SHARE, 128), F32),
            dma((CHUNKS,)), dma((5,)), dma((4,)), dma((4,)), dma((STEPS, TEAMS, 4)), dma((STEPS, TEAMS, 4)),
            dma((STEPS, sec_count)), dma((STEPS, sec_count)), dma((STEPS,)),
            dma((PLANE,)), dma((PLANE,)), dma((COLUMN,)), dma((COLUMN,)), dma((PLANE,)), dma((PLANE,)),
        ],
        compiler_params=pltpu.CompilerParams(
            collective_id=0, has_side_effects=True, vmem_limit_bytes=40 * 1024 * 1024
        ),
        name="slab",
    )(*(pltpu.with_memory_space_constraint(x, pltpu.HBM) for x in (table, state.reshape(-1, 128), rock, cells, rate, basis)))


def rotate_kernel(basis_ref, snaps_ref, mix_ref, out_ref):
    block = pl.program_id(0)
    taken = jnp.concatenate([snaps_ref[:, block * 8 + y].reshape(64, 128).T for y in range(8)], 0)
    lhs = jnp.concatenate([basis_ref[pl.ds(pl.multiple_of(block * 1024, 1024), 1024), :], taken], 1)
    out_ref[...] = jnp.dot(lhs, mix_ref[...], preferred_element_type=F32).astype(BF16)


def rotate(basis, snaps, mix):
    rows = basis.shape[0]
    return pl.pallas_call(
        rotate_kernel,
        grid=(rows // 1024,),
        out_shape=jax.ShapeDtypeStruct(basis.shape, BF16),
        in_specs=[
            pl.BlockSpec(memory_space=VMEM),
            pl.BlockSpec(memory_space=VMEM),
            pl.BlockSpec(memory_space=VMEM),
        ],
        out_specs=pl.BlockSpec((1024, 256), lambda i: (i, 0)),
        compiler_params=pltpu.CompilerParams(vmem_limit_bytes=24 * 1024 * 1024),
        name="rotate",
    )(basis, snaps, mix)


def dot(a, b, contract=((1,), (0,))):
    a1, b1 = a.astype(BF16), b.astype(BF16)
    a2, b2 = (a - a1.astype(F32)).astype(BF16), (b - b1.astype(F32)).astype(BF16)

    def one(x, y):
        return lax.dot_general(x, y, (contract, ((), ())), preferred_element_type=F32)

    return one(a1, b1) + (one(a1, b2) + one(a2, b1))


ROWS_BASIS = 256
RANK = 32
BLOCK = 8
STRIDE = RANK + BLOCK


def spread_row(ref, at):
    return jnp.broadcast_to(ref[pl.ds(at, 1), :], (8, 128))


def factor(c, gram, sigma, mx, ct, first, second, coef, yy, nat):
    lane = lax.broadcasted_iota(jnp.int32, (8, 128), 1)
    row = lax.broadcasted_iota(jnp.int32, (8, 128), 0)
    group = lane // 32
    g0, g1, g2 = group == 0, group == 1, group == 2

    def wide(mask, rows):
        return jnp.concatenate([mask] * (rows // 8), 0)

    def turn(x, by):
        return pltpu.roll(x, by, 1)

    padded = jnp.concatenate([c, jnp.broadcast_to(sigma, (96, ROWS_BASIS))], 0)
    ct[...] = padded.T
    sig_col = turn(ct[...], 96)
    sig_col = jnp.where(wide(lane, ROWS_BASIS) < 96, sig_col, turn(sig_col, 32))
    inv2 = 1.0 / (sig_col * sig_col)

    at = lax.broadcasted_iota(jnp.int32, (ROWS_BASIS, 128), 0)
    over = lax.broadcasted_iota(jnp.int32, (ROWS_BASIS, 128), 1)
    before = at < BLOCK * (over & 31)
    pick = over // 32
    masks = jnp.where(
        pick == 0, jnp.where(before, inv2 * inv2, 0.0),
        jnp.where(pick == 1, jnp.where(before, inv2, 0.0), jnp.where((pick == 2) & ~before, 1.0, 0.0)),
    )
    low = lax.broadcasted_iota(jnp.int32, (RANK, 128), 0)
    lanes = wide(group, RANK)
    for chunk in range(4):
        pairs = jnp.concatenate([c * c[a : a + 1] for a in range(chunk * 8, chunk * 8 + 8)], 0)
        sums = dot(pairs, masks)
        for i in range(8):
            a = chunk * 8 + i
            mx[a * STRIDE : a * STRIDE + RANK, :] = (
                sums[i * RANK : (i + 1) * RANK]
                + jnp.where((lanes == 1) & (low == a), 1.0, 0.0)
                + jnp.where(lanes == 2, jnp.broadcast_to(gram[:, a : a + 1], (RANK, 128)), 0.0)
            )
    fourth = []
    for half in range(2):
        mixed = jnp.concatenate([ct[pl.ds(half * 4 + t, 32, stride=8), :] for t in range(4)], 0).T
        for t in range(4):
            here = mixed if t == 0 else turn(mixed, 128 - 32 * t)
            r1 = here[:RANK]
            sig = here[RANK : 2 * RANK]
            r2 = sig * sig * r1
            mx[pl.ds(RANK + half * 4 + t, RANK, stride=STRIDE), :] = jnp.where(
                lanes == 0, r1, jnp.where(lanes == 2, -turn(r2, 64), 0.0)
            )
            sq = sig[:8] * sig[:8]
            fourth.append(sq * sq)

    acc = tuple(jnp.zeros((8, 128), F32) for _ in range(BLOCK))
    for part in range(4):
        skip = part * 8
        count = RANK - skip
        w0, w1, w2 = wide(g0, count), wide(g1, count), wide(g2, count)

        def step(k, acc):
            base = pl.multiple_of(k * STRIDE, 8)
            rk = mx[pl.ds(base + skip, count), :]
            ck = mx[pl.ds(skip * STRIDE + k, count, stride=STRIDE), :]
            pivot = spread_row(mx, base + k)
            up, down, across = turn(pivot, 32), turn(pivot, 96), turn(pivot, 64)
            p = jnp.where(g0, pivot, jnp.where(g1, up, across))
            e = jnp.where(g0, down, jnp.where(g1, pivot, up))
            q = jnp.where(g0, across, jnp.where(g1, down, pivot))
            det = 1.0 / (p * q + e * e)
            p, e, q = p * det, e * det, q * det
            pw, ew, qw = (jnp.concatenate([z] * (count // 8), 0) for z in (p, e, q))
            rk_up, rk_down, ck_down = turn(rk, 32), turn(rk, 96), turn(ck, 96)
            u = jnp.where(w2, rk_up, jnp.where(w1, rk, rk))
            v = jnp.where(w0, ck_down, jnp.where(w1, -rk_down, -rk))
            fa = qw * u + ew * v
            sa = ew * u - pw * v
            first[pl.ds(pl.multiple_of(k * RANK, 8) + skip, count), :] = fa
            second[pl.ds(pl.multiple_of(k * RANK, 8) + skip, count), :] = sa
            coef[0, skip:RANK, :] = jnp.where(w0, rk, jnp.where(w1, rk_up, -rk_up))
            coef[1, skip:RANK, :] = jnp.where(w0, ck_down, ck)
            right = mx[pl.ds(base + RANK, 8), :]
            swapped = turn(right, 64)
            u = jnp.where(g0, right, swapped)
            v = jnp.where(g0, -swapped, -right)
            fr = q * u + e * v
            sr = e * u - p * v
            yy[pl.ds(pl.multiple_of(k * 8, 8), 8), :] = jnp.where(g0, fr, turn(sr, 32))
            acc = tuple(
                acc[t]
                + jnp.broadcast_to(u[t : t + 1], (8, 128)) * fr
                + jnp.broadcast_to(v[t : t + 1], (8, 128)) * sr
                for t in range(BLOCK)
            )
            fall = jnp.concatenate([fa, fr], 0)
            sall = jnp.concatenate([sa, sr], 0)
            for i in range(skip, RANK):
                f = jnp.broadcast_to(coef[0, i : i + 1, :], (8, 128))
                s = jnp.broadcast_to(coef[1, i : i + 1, :], (8, 128))
                for part8 in range(count // 8 + 1):
                    where = i * STRIDE + skip + part8 * 8
                    mx[where : where + 8, :] = mx[where : where + 8, :] - (
                        f * fall[part8 * 8 : part8 * 8 + 8] + s * sall[part8 * 8 : part8 * 8 + 8]
                    )
            return acc

        acc = lax.fori_loop(skip, skip + 8, step, acc)

    ys = [None] * RANK
    for k in range(RANK - 1, -1, -1):
        y = yy[k * 8 : k * 8 + 8, :]
        if k < RANK - 1:
            a1 = a2 = None
            for l in range(RANK - 1, k, -1):
                m1 = spread_row(first, k * RANK + l) * ys[l]
                m2 = spread_row(second, k * RANK + l) * ys[l]
                a1 = m1 if a1 is None else a1 + m1
                a2 = m2 if a2 is None else a2 + m2
            y = y - jnp.where(g0, a1 + turn(a1, 96), a2 + turn(a2, 32))
        ys[k] = y

    block = [acc[t] + jnp.where(row == t, fourth[t], 0.0) for t in range(BLOCK)]
    scale = jnp.zeros((8, 128), F32)
    steps = []
    for s in range(BLOCK):
        d = jnp.broadcast_to(block[s][s : s + 1], (8, 128))
        scale = jnp.where(row == s, lax.rsqrt(d), scale)
        ratio = jnp.where(row > s, block[s] / d, 0.0)
        steps.append(ratio)
        for t in range(s + 1, BLOCK):
            block[t] = block[t] - jnp.broadcast_to(block[s][t : t + 1], (8, 128)) * ratio
    for index in range(2 * RANK + BLOCK):
        if index < RANK:
            value = ys[index]
        elif index < 2 * RANK:
            value = turn(ys[index - RANK], 96)
        else:
            value = jnp.where(row == index - 2 * RANK, 1.0, 0.0)
        for s in range(BLOCK - 1):
            value = value - steps[s] * jnp.broadcast_to(value[s : s + 1], (8, 128))
        yy[index * 8 : index * 8 + 8, :] = value * scale
    for half in range(2):
        mixed = None
        for t in range(4):
            part = yy[pl.ds(half * 4 + t, 128, stride=8), :]
            part = part if t == 0 else turn(part, 32 * t)
            mixed = part if t == 0 else jnp.where(wide(group, 128) == t, part, mixed)
        mixed = mixed.T
        for t in range(4):
            nat[pl.ds(half * 4 + t, 32, stride=8), :] = mixed[32 * t : 32 * t + 32]

    inv_row = 1.0 / (sigma * sigma)
    weighed = jnp.concatenate([c * (inv_row * inv_row), c * inv_row], 0)
    across = lax.broadcasted_iota(jnp.int32, (ROWS_BASIS, ROWS_BASIS), 1)
    down = lax.broadcasted_iota(jnp.int32, (ROWS_BASIS, ROWS_BASIS), 0)
    tile = jnp.where(
        (lax.broadcasted_iota(jnp.int32, (BLOCK, ROWS_BASIS), 1) & 7)
        == lax.broadcasted_iota(jnp.int32, (BLOCK, ROWS_BASIS), 0), 1.0, 0.0
    )
    natural = nat[...]
    below = -dot(natural[:, : 2 * RANK], weighed)
    own = dot(natural[:, 2 * RANK : 2 * RANK + BLOCK], tile)
    inverse = jnp.where(across // 8 < down // 8, below, jnp.where(across // 8 == down // 8, own, 0.0))
    return inverse, sig_col


def batch_update(c, rounded, gram, sigma, *scratch):
    inverse, sig_col = factor(c, gram, sigma, *scratch)
    sig = jnp.concatenate([sig_col, sig_col], 1)
    on_snaps = dot(c, inverse, ((1,), (1,)))
    scaled = sig * sig * inverse.T
    total = scaled + dot(c, on_snaps, ((0,), (0,)))
    on_basis = scaled + dot(c - rounded, on_snaps, ((0,), (0,)))
    top = sig * total
    bottom = dot(c, total) + dot(gram, on_snaps)
    energy = jnp.sum(top * top, axis=0, keepdims=True) + jnp.sum(bottom * bottom, axis=0, keepdims=True)
    return on_basis, on_snaps, jnp.sqrt(energy)


def by_batch(x):
    return jnp.concatenate([x[16 * step + 8 * g : 16 * step + 8 * g + 8] for g in range(2) for step in range(4)], 0)


def small_kernel(
    rows_total, whole_ref, sigma_ref, fields_ref, mix_ref, sigma_out_ref, fields_out, half_uu, copy_sem, *scratch
):
    writing = pltpu.make_async_copy(fields_ref, fields_out, copy_sem)
    writing.start()
    scale = 1.0 / rows_total

    def piece(index):
        return whole_ref[64 * index : 64 * (index + 1), :] * scale

    high = lax.broadcasted_iota(jnp.int32, (64, 128), 1) >= 64
    last = piece(6)
    half_uu[...] = jnp.zeros((256, 256), F32)
    half_uu[0:64, 0:128] = jnp.where(high, 1.0, 0.5) * piece(2)
    half_uu[0:64, 128:256] = piece(3)
    half_uu[64:128, 0:128] = jnp.where(high, 0.5 * last, 0.0)
    half_uu[64:128, 128:256] = piece(4)
    half_uu[128:192, 128:256] = jnp.where(high, 1.0, 0.5) * piece(5)
    half_uu[192:256, 128:256] = jnp.where(high, 0.5 * pltpu.roll(last, 64, 1), 0.0)
    su = by_batch(jnp.concatenate([piece(0), piece(1)], 1))
    source = lax.broadcasted_iota(jnp.int32, (64, 64), 0)
    target = lax.broadcasted_iota(jnp.int32, (64, 64), 1)
    wanted = (target // 8 % 4) * 16 + (target // 32) * 8 + (target & 7)
    ss = dot(by_batch(piece(7)[:, :64]), jnp.where(source == wanted, 1.0, 0.0))
    s00, s10, s11 = ss[:32, :32], ss[32:, :32], ss[32:, 32:]

    def of_basis(x):
        part = dot(dot(x, half_uu[...]), x, ((1,), (1,)))
        return part + part.T

    def twice(c, r):
        part = dot(c, r, ((1,), (1,)))
        return part + part.T

    c0 = su[:32]
    r0 = c0.astype(BF16).astype(F32)
    gram0 = s00 - twice(c0, r0) + of_basis(r0)
    wu, ws, sigma1 = batch_update(c0, r0, gram0, sigma_ref[...], *scratch)
    c1 = dot(su[32:], wu) + dot(s10, ws)
    r1 = c1.astype(BF16).astype(F32)
    yu = dot(r1, wu, ((1,), (1,)))
    ys = dot(r1, ws, ((1,), (1,)))
    cross = dot(dot(ys, c0), yu, ((1,), (1,)))
    gram1 = s11 - twice(c1, r1) + of_basis(yu) + cross + cross.T + dot(dot(ys, s00), ys, ((1,), (1,)))
    wu1, ws1, sigma2 = batch_update(c1, r1, gram1, sigma1, *scratch)
    mix_ref[0:256, :] = dot(wu, wu1).astype(BF16)
    w0, w1 = dot(ws, wu1), ws1
    mix_ref[256:320, :] = jnp.concatenate(
        [w[8 * step : 8 * step + 8] for step in range(4) for w in (w0, w1)], 0
    ).astype(BF16)
    sigma_out_ref[...] = sigma2
    writing.wait()


def small_algebra(whole, sigma, fields, rows_total):
    return pl.pallas_call(
        lambda *refs: small_kernel(float(rows_total), *refs),
        out_shape=(jax.ShapeDtypeStruct((320, 256), BF16), jax.ShapeDtypeStruct((1, 256), F32), jax.ShapeDtypeStruct(fields.shape, F32)),
        in_specs=[pl.BlockSpec(memory_space=VMEM)] * 3,
        out_specs=(pl.BlockSpec(memory_space=VMEM),) * 2 + (pl.BlockSpec(memory_space=pltpu.HBM),),
        scratch_shapes=[
            VMEM((256, 256), F32),
            pltpu.SemaphoreType.DMA,
            VMEM((RANK * STRIDE, 128), F32),
            VMEM((256, 128), F32),
            VMEM((RANK * RANK, 128), F32),
            VMEM((RANK * RANK, 128), F32),
            VMEM((2, RANK, 128), F32),
            VMEM((128 * 8, 128), F32),
            VMEM((256, 128), F32),
        ],
        compiler_params=pltpu.CompilerParams(vmem_limit_bytes=32 * 1024 * 1024),
        name="small_algebra",
    )(whole, sigma.reshape(1, -1), fields)


def body(state_init, rock_type, perm_table, well_cells, well_rate, basis_in, singular):
    basis = basis_in.reshape(-1, basis_in.shape[-1])
    rows_total = basis.shape[0] * lax.axis_size("gx") * lax.axis_size("sec")
    final, snaps, whole = slab(perm_table, state_init, rock_type, well_cells.reshape(1, -1), well_rate, basis)
    mix, sigma, final = small_algebra(whole.reshape(-1, 128), singular, final, rows_total)
    fresh = rotate(basis, snaps, mix)
    return (final.reshape(state_init.shape), fresh.reshape(basis_in.shape), sigma.reshape(-1))


def solution(mesh):
    return jax.shard_map(
        body,
        mesh=mesh,
        in_specs=(
            P(None, "gx", "sec", None),
            P("gx", "sec"),
            P(),
            P(),
            P(),
            P(("gx", "sec"), None, None, None),
            P(),
        ),
        out_specs=(P(None, "gx", "sec", None), P(("gx", "sec"), None, None, None), P()),
        check_vma=False,
    )
```

```python
import jax
import jax.numpy as jnp
from jax import lax
from jax.experimental import pallas as pl
from jax.experimental.pallas import tpu as pltpu
from jax.sharding import PartitionSpec as P

MG = 8
STEPS = 4
GROUPS = 2
MEMB = MG * GROUPS

DT_PRESSURE = 0.12
DT_SATURATION = 0.06
DT_ADVECT = 0.15

MESH = pl.DeviceIdType.MESH
VMEM = pltpu.VMEM
F32 = jnp.float32
BF16 = jnp.bfloat16


def harmonic(left, right):
    return 2.0 * left * right / (left + right)


def remote(src, dst, send_sem, recv_sem, device):
    return pltpu.make_async_remote_copy(
        src_ref=src, dst_ref=dst, send_sem=send_sem, recv_sem=recv_sem, device_id=device, device_id_type=MESH
    )


PLANE = 32
COLUMN = 8


SHARE = 16
CHUNKS = 8
TEAMS = 4
TEAM = MEMB // TEAMS


def slab_kernel(
    table_hbm, state_hbm, rock_hbm, cells_hbm, rate_hbm, basis_hbm, out_ref, snaps_ref, sum_ref,
    table_ref, rock_ref, cells_ref, rate_ref, fields, basis, uu, inflow, kinds, perm_send, perm_recv, x_send, x_recv, y_send, y_recv, y_wide, weights, turned, packed,
    local, slots, partial, column,
    load_sem, in_sem, ps_sem, pr_sem, hs_sem, hr_sem, ss_sem, sr_sem, own_sem, send1, recv1, send2, recv2, send3, recv3,
):
    gx_count, sec_count = lax.axis_size("gx"), lax.axis_size("sec")
    gx, sec = lax.axis_index("gx"), lax.axis_index("sec")
    beside = (
        {"gx": lax.rem(gx + gx_count - 1, gx_count)},
        {"gx": lax.rem(gx + 1, gx_count)},
        {"sec": lax.rem(sec + sec_count - 1, sec_count)},
        {"sec": lax.rem(sec + 1, sec_count)},
    )
    z_hi, z_lo = lax.rem(gx // 2, 4), sec // 4
    me = (gx // 8) * 8 + lax.rem(gx, 2) * 4 + lax.rem(sec, 4)
    me_z = z_hi * 2 + z_lo

    def in_plane(p):
        return {"gx": (p // 8) * 8 + z_hi * 2 + lax.rem(p // 4, 2), "sec": z_lo * 4 + lax.rem(p, 4)}

    def in_column(q):
        return {"gx": (gx // 8) * 8 + (q // 2) * 2 + lax.rem(gx, 2), "sec": lax.rem(q, 2) * 4 + lax.rem(sec, 4)}

    barrier = pltpu.get_barrier_semaphore()

    def greet(device):
        pl.semaphore_signal(barrier, inc=1, device_id=device, device_id_type=MESH)

    greet(beside[0])
    greet(beside[1])
    for ahead in range(1, sec_count):
        greet({"sec": lax.rem(sec + ahead, sec_count)})
    for k in range(1, COLUMN):
        greet(in_column(lax.rem(me_z + k, COLUMN)))
    for k in range(1, PLANE):
        greet(in_plane(lax.rem(me + k, PLANE)))

    def load(c):
        rows = pl.ds(pl.multiple_of(c * 1024, 1024), 1024)
        return pltpu.make_async_copy(basis_hbm.at[rows], basis.at[rows], load_sem.at[c])

    arriving = [
        pltpu.make_async_copy(src, dst, in_sem.at[i])
        for i, (src, dst) in enumerate(
            ((table_hbm, table_ref), (state_hbm, out_ref), (rock_hbm, rock_ref), (rate_hbm, rate_ref), (cells_hbm, cells_ref))
        )
    ]
    for copy in arriving:
        copy.start()
    for c in range(CHUNKS):
        load(c).start()

    lane = lax.broadcasted_iota(jnp.int32, (8, 128), 1)
    row = lax.broadcasted_iota(jnp.int32, (8, 128), 0)

    def uu_chunk(c, carry):
        load(c).wait()
        part = basis[pl.ds(pl.multiple_of(c * 1024, 1024), 1024), :]
        tn = (((0,), (0,)), ((), ()))
        uu[0:128, :] += lax.dot_general(part[:, :128], part, tn, preferred_element_type=F32)
        uu[128:256, 128:256] += lax.dot_general(part[:, 128:], part[:, 128:], tn, preferred_element_type=F32)
        return carry

    def halo_copies(step, g):
        copies = []
        for d in range(4):
            if d < 2:
                src = x_send.at[step, d, pl.ds(g * TEAM, TEAM)]
                dst = x_recv.at[step, 1 - d, pl.ds(g * TEAM, TEAM)]
            else:
                rows = pl.ds(pl.multiple_of(g * 8 * TEAM, 8 * TEAM), 8 * TEAM)
                src = y_send.at[step, d - 2, rows]
                dst = y_recv.at[step, 3 - d, rows]
            copies.append(remote(src, dst, hs_sem.at[step, g, d], hr_sem.at[step, g, d ^ 1], beside[d]))
        return copies

    def stage_y(step, g):
        for side, y in ((0, 0), (1, 7)):
            rows = pl.ds(pl.multiple_of(g * 8 * TEAM, 8 * TEAM), 8 * TEAM)
            y_send[step, side, rows, :] = fields[pl.ds(g * 64 * TEAM + y, 8 * TEAM, stride=8), :].astype(BF16)

    low_half = lane < 64

    def first(q, carry):
        base = pl.multiple_of(q * 128, 128)
        for x in range(8):
            a = out_ref[pl.ds(base + x * 8, 8), :]
            b = out_ref[pl.ds(base + 64 + x * 8, 8), :]
            p = jnp.where(low_half, a, pltpu.roll(b, 64, 1))
            s = jnp.where(low_half, pltpu.roll(a, 64, 1), b)
            fields[pl.ds(base + x * 8, 8), :] = p
            fields[pl.ds(base + 64 + x * 8, 8), :] = s
            if x in (0, 7):
                x_send[0, x // 7, 2 * q] = p.astype(BF16)
                x_send[0, x // 7, 2 * q + 1] = s.astype(BF16)
        return carry

    for copy in arriving:
        copy.wait()
    lax.fori_loop(0, MEMB // 2, first, 0)
    for g in range(TEAMS):
        stage_y(0, g)

    for pair in range(4):
        both = rock_ref[:, pair * 128 : pair * 128 + 128]
        other = pltpu.roll(both, 64, 1)
        kinds[pl.ds(2 * pair, 8, stride=8), :] = jnp.where(lane < 64, both, other)
        kinds[pl.ds(2 * pair + 1, 8, stride=8), :] = jnp.where(lane < 64, other, both)
    table = [[jnp.broadcast_to(table_ref[d : d + 1, r : r + 1], (8, 128)) for r in range(16)] for d in range(3)]
    perm = [[], [], []]
    for x in range(8):
        kind = kinds[x * 8 : x * 8 + 8, :]
        for d in range(3):
            value = table[d][0]
            for r in range(1, 16):
                value = jnp.where(kind == r, table[d][r], value)
            perm[d].append(value)
    perm_send[0] = perm[0][0]
    perm_send[1] = perm[0][7]
    for x in range(8):
        perm_send[2, pl.ds(x, 1), :] = perm[1][x][0:1]
        perm_send[3, pl.ds(x, 1), :] = perm[1][x][7:8]

    uu[...] = jnp.zeros((256, 256), F32)
    lax.fori_loop(0, 3, uu_chunk, 0)
    pl.semaphore_wait(barrier, 2 + (sec_count - 1) + (COLUMN - 1) + (PLANE - 1))
    perm_copies = [
        remote(perm_send.at[d], perm_recv.at[d ^ 1], ps_sem.at[d], pr_sem.at[d ^ 1], beside[d]) for d in range(4)
    ]
    for copy in perm_copies:
        copy.start()
    for g in range(TEAMS):
        for copy in halo_copies(0, g):
            copy.start()

    rate = jnp.concatenate([rate_ref[m : m + 1, :] for start in range(2) for m in range(start, MEMB, 2)], 0)
    top = rate.astype(BF16)
    rest = rate - top.astype(F32)
    middle = rest.astype(BF16)
    parts = jnp.concatenate([top, middle, (rest - middle.astype(F32)).astype(BF16)], 0)
    wells = cells_ref[...]
    cell = lax.broadcasted_iota(jnp.int32, (512, 256), 0)

    def place(x, carry):
        ids = ((gx * 8 + x) * (8 * sec_count) + sec * 8) * 64 + cell
        hits = jnp.where(ids == wells, 1.0, 0.0).astype(BF16)
        found = lax.dot_general(parts, hits, (((1,), (1,)), ((), ())), preferred_element_type=F32)
        found = found[:MEMB] + found[MEMB : 2 * MEMB] + found[2 * MEMB :]
        for y in range(8):
            columns = slice((y // 2) * 128, (y // 2) * 128 + 128)
            even, odd = found[:8, columns], found[8:, columns]
            if y % 2 == 0:
                both = jnp.where(low_half, even, pltpu.roll(odd, 64, 1))
            else:
                both = jnp.where(low_half, pltpu.roll(even, 64, 1), odd)
            inflow[pl.ds(x * 8 + y, 8, stride=64), :] = DT_PRESSURE * both
        return carry

    lax.fori_loop(0, 8, place, 0)
    lax.fori_loop(3, 5, uu_chunk, 0)

    z_up = jnp.where((lane & 63) == 63, 0.0, 1.0)
    z_down = jnp.where((lane & 63) == 0, 0.0, 1.0)
    for x in range(8):
        weights[4, x] = z_up * harmonic(perm[2][x], pltpu.roll(perm[2][x], 127, 1))
        weights[5, x] = z_down * harmonic(perm[2][x], pltpu.roll(perm[2][x], 1, 1))
    for copy in perm_copies:
        copy.wait()
    not_first_x = jnp.where(gx == 0, 0.0, 1.0)
    not_last_x = jnp.where(gx == gx_count - 1, 0.0, 1.0)
    not_first_y = jnp.where(sec == 0, 0.0, 1.0)
    not_last_y = jnp.where(sec == sec_count - 1, 0.0, 1.0)
    for x in range(8):
        above = perm[0][x + 1] if x < 7 else perm_recv[1] * not_last_x
        below = perm[0][x - 1] if x > 0 else perm_recv[0] * not_first_x
        weights[0, x] = harmonic(perm[0][x], above)
        weights[1, x] = harmonic(below, perm[0][x])
        right = jnp.broadcast_to(perm_recv[3, pl.ds(x, 1), :] * not_last_y, (8, 128))
        left = jnp.broadcast_to(perm_recv[2, pl.ds(x, 1), :] * not_first_y, (8, 128))
        weights[2, x] = harmonic(perm[1][x], jnp.where(row == 7, right, pltpu.roll(perm[1][x], 7, 0)))
        weights[3, x] = harmonic(jnp.where(row == 0, left, pltpu.roll(perm[1][x], 1, 0)), perm[1][x])

    def snap_copies(step):
        copies = [
            pltpu.make_async_copy(packed.at[step, sec], snaps_ref.at[step, pl.ds(sec * 8, 8)], own_sem.at[step])
        ]
        for ahead in range(1, sec_count):
            target = lax.rem(sec + ahead, sec_count)
            copies.append(
                remote(
                    packed.at[step, target], snaps_ref.at[step, pl.ds(sec * 8, 8)],
                    ss_sem.at[step, ahead], sr_sem.at[step, ahead], {"sec": target},
                )
            )
        return copies

    for step in range(STEPS):

        def team_step(g, carry):
            for copy in halo_copies(step, g):
                copy.wait()
            rows = pl.ds(pl.multiple_of(g * 8 * TEAM, 8 * TEAM), 8 * TEAM)
            y_wide[0, rows, :] = y_recv[step, 0, rows, :].astype(F32)
            y_wide[1, rows, :] = y_recv[step, 1, rows, :].astype(F32)

            def pair_step(index, carry):
                q = g * (TEAM // 2) + index
                base = pl.multiple_of(q * 128, 128)
                ps = [fields[pl.ds(base + x * 8, 8), :] for x in range(8)]
                ss = [fields[pl.ds(base + 64 + x * 8, 8), :] for x in range(8)]
                ends = [[x_recv[step, side, 2 * q + i].astype(F32) for side in range(2)] for i in range(2)]

                def besides(all_x, x, i):
                    here = all_x[x]
                    at = (2 * q + i) * 8 + x
                    left = jnp.broadcast_to(y_wide[0, pl.ds(at, 1), :], (8, 128))
                    right = jnp.broadcast_to(y_wide[1, pl.ds(at, 1), :], (8, 128))
                    return (
                        all_x[x + 1] if x < 7 else ends[i][1],
                        all_x[x - 1] if x > 0 else ends[i][0],
                        jnp.where(row == 7, right, pltpu.roll(here, 7, 0)),
                        jnp.where(row == 0, left, pltpu.roll(here, 1, 0)),
                        pltpu.roll(here, 127, 1),
                        pltpu.roll(here, 1, 1),
                    )

                for x in range(8):
                    p, s = ps[x], ss[x]
                    p_beside, s_beside = besides(ps, x, 0), besides(ss, x, 1)
                    p_spread = s_spread = carried = None
                    for d in range(6):
                        weight = weights[d, x]
                        flow = weight * (p_beside[d] - p)
                        spread = weight * (s_beside[d] - s)
                        moved = flow * jnp.where(flow > 0.0, s_beside[d], s)
                        p_spread = flow if p_spread is None else p_spread + flow
                        s_spread = spread if s_spread is None else s_spread + spread
                        carried = moved if carried is None else carried + moved
                    p = p + DT_PRESSURE * p_spread + inflow[pl.ds(pl.multiple_of(q * 64 + x * 8, 8), 8), :]
                    s = s + DT_SATURATION * s_spread + DT_ADVECT * carried
                    a = jnp.where(low_half, p, pltpu.roll(s, 64, 1))
                    b = jnp.where(low_half, pltpu.roll(p, 64, 1), s)
                    turned[x, pl.ds(2 * q, 8, stride=MEMB), :] = a
                    turned[x, pl.ds(2 * q + 1, 8, stride=MEMB), :] = b
                    if step + 1 < STEPS:
                        fields[pl.ds(base + x * 8, 8), :] = p
                        fields[pl.ds(base + 64 + x * 8, 8), :] = s
                        if x in (0, 7):
                            x_send[step + 1, x // 7, 2 * q] = p.astype(BF16)
                            x_send[step + 1, x // 7, 2 * q + 1] = s.astype(BF16)
                    else:
                        out_ref[pl.ds(base + x * 8, 8), :] = a
                        out_ref[pl.ds(base + 64 + x * 8, 8), :] = b
                return carry

            lax.fori_loop(0, TEAM // 2, pair_step, 0)
            if step + 1 < STEPS:
                stage_y(step + 1, g)
                for copy in halo_copies(step + 1, g):
                    copy.start()
            return carry

        lax.fori_loop(0, TEAMS, team_step, 0)
        for x in range(8):
            packed[step, x] = turned[x].reshape(8, MEMB, 128).astype(BF16)
        for copy in snap_copies(step):
            copy.start()
    lax.fori_loop(5, CHUNKS, uu_chunk, 0)
    for step in range(STEPS):
        for copy in snap_copies(step):
            copy.wait()

    def gram(pair, carry):
        su, ss = carry
        lhs = jnp.concatenate(
            [snaps_ref[:, 2 * pair].reshape(64, 128), snaps_ref[:, 2 * pair + 1].reshape(64, 128)], 1
        )
        rhs = basis[pl.ds(pl.multiple_of(pair * 256, 256), 256), :]
        su = su + jnp.dot(lhs, rhs, preferred_element_type=F32)
        ss = ss + lax.dot_general(lhs, lhs, (((1,), (1,)), ((), ())), preferred_element_type=F32)
        return su, ss

    su, ss = lax.fori_loop(
        0, 4 * sec_count, gram, (jnp.zeros((64, 256), F32), jnp.zeros((64, 64), F32)), unroll=4
    )
    zero = jnp.zeros((64, 64), F32)
    for index, block in enumerate(
        (
            su[:, :128],
            su[:, 128:],
            uu[0:64, 0:128],
            uu[0:64, 128:256],
            uu[64:128, 128:256],
            uu[128:192, 128:256],
            jnp.concatenate([uu[192:256, 192:256], uu[64:128, 64:128]], 1),
            jnp.concatenate([ss, zero], 1),
        )
    ):
        local[4 * index : 4 * index + 4] = block.reshape(4, SHARE, 128)

    slots[me] = local[me]

    def scatter(k):
        p = lax.rem(me + k, PLANE)
        return remote(local.at[p], slots.at[me], send1.at[k], recv1.at[k], in_plane(p))

    for k in range(1, PLANE):
        scatter(k).start()
    for k in range(1, PLANE):
        scatter(k).wait()
    total = slots[0]
    for k in range(1, PLANE):
        total = total + slots[k]
    partial[...] = total
    column[me_z] = total

    def across(k):
        q = lax.rem(me_z + k, COLUMN)
        return remote(partial, column.at[me_z], send2.at[k], recv2.at[k], in_column(q))

    for k in range(1, COLUMN):
        across(k).start()
    for k in range(1, COLUMN):
        across(k).wait()
    total = column[0]
    for k in range(1, COLUMN):
        total = total + column[k]
    sum_ref[me] = total

    def gather(k):
        p = lax.rem(me + k, PLANE)
        return remote(sum_ref.at[me], sum_ref.at[me], send3.at[k], recv3.at[k], in_plane(p))

    for k in range(1, PLANE):
        gather(k).start()
    for k in range(1, PLANE):
        gather(k).wait()


def slab(table, state, rock, cells, rate, basis):
    sec_count = lax.axis_size("sec")
    dma = pltpu.SemaphoreType.DMA
    in_vmem = pl.BlockSpec(memory_space=VMEM)
    return pl.pallas_call(
        slab_kernel,
        out_shape=(
            jax.ShapeDtypeStruct((MEMB * 64, 128), F32),
            jax.ShapeDtypeStruct((STEPS, 8 * sec_count, MEMB, 128), BF16),
            jax.ShapeDtypeStruct((PLANE, SHARE, 128), F32),
        ),
        in_specs=[pl.BlockSpec(memory_space=pltpu.HBM)] * 6,
        out_specs=(in_vmem,) * 3,
        scratch_shapes=[
            VMEM(table.shape, F32),
            VMEM(rock.shape, jnp.int32),
            VMEM(cells.shape, jnp.int32),
            VMEM(rate.shape, F32),
            VMEM((MEMB * 64, 128), F32),
            VMEM(basis.shape, BF16),
            VMEM((256, 256), F32),
            VMEM((MEMB * 32, 128), F32),
            VMEM((64, 128), jnp.int32),
            VMEM((4, 8, 128), F32),
            VMEM((4, 8, 128), F32),
            VMEM((STEPS, 2, MEMB, 8, 128), BF16),
            VMEM((STEPS, 2, MEMB, 8, 128), BF16),
            VMEM((STEPS, 2, MEMB * 8, 128), BF16),
            VMEM((STEPS, 2, MEMB * 8, 128), BF16),
            VMEM((2, MEMB * 8, 128), F32),
            VMEM((6, 8, 8, 128), F32),
            VMEM((8, 8 * MEMB, 128), F32),
            VMEM((STEPS, 8, 8, MEMB, 128), BF16),
            VMEM((PLANE, SHARE, 128), F32),
            VMEM((PLANE, SHARE, 128), F32),
            VMEM((SHARE, 128), F32),
            VMEM((COLUMN, SHARE, 128), F32),
            dma((CHUNKS,)), dma((5,)), dma((4,)), dma((4,)), dma((STEPS, TEAMS, 4)), dma((STEPS, TEAMS, 4)),
            dma((STEPS, sec_count)), dma((STEPS, sec_count)), dma((STEPS,)),
            dma((PLANE,)), dma((PLANE,)), dma((COLUMN,)), dma((COLUMN,)), dma((PLANE,)), dma((PLANE,)),
        ],
        compiler_params=pltpu.CompilerParams(
            collective_id=0, has_side_effects=True, vmem_limit_bytes=40 * 1024 * 1024
        ),
        name="slab",
    )(*(pltpu.with_memory_space_constraint(x, pltpu.HBM) for x in (table, state.reshape(-1, 128), rock, cells, rate, basis)))


def rotate_kernel(basis_ref, snaps_ref, mix_ref, out_ref):
    block = pl.program_id(0)
    taken = jnp.concatenate([snaps_ref[:, block * 8 + y].reshape(64, 128).T for y in range(8)], 0)
    lhs = jnp.concatenate([basis_ref[pl.ds(pl.multiple_of(block * 1024, 1024), 1024), :], taken], 1)
    out_ref[...] = jnp.dot(lhs, mix_ref[...], preferred_element_type=F32).astype(BF16)


def rotate(basis, snaps, mix):
    rows = basis.shape[0]
    return pl.pallas_call(
        rotate_kernel,
        grid=(rows // 1024,),
        out_shape=jax.ShapeDtypeStruct(basis.shape, BF16),
        in_specs=[
            pl.BlockSpec(memory_space=VMEM),
            pl.BlockSpec(memory_space=VMEM),
            pl.BlockSpec(memory_space=VMEM),
        ],
        out_specs=pl.BlockSpec((1024, 256), lambda i: (i, 0)),
        compiler_params=pltpu.CompilerParams(vmem_limit_bytes=24 * 1024 * 1024),
        name="rotate",
    )(basis, snaps, mix)


def dot(a, b, contract=((1,), (0,))):
    a1, b1 = a.astype(BF16), b.astype(BF16)
    a2, b2 = (a - a1.astype(F32)).astype(BF16), (b - b1.astype(F32)).astype(BF16)

    def one(x, y):
        return lax.dot_general(x, y, (contract, ((), ())), preferred_element_type=F32)

    return one(a1, b1) + (one(a1, b2) + one(a2, b1))


ROWS_BASIS = 256
RANK = 32
BLOCK = 8
STRIDE = RANK + BLOCK


def spread_row(ref, at):
    return jnp.broadcast_to(ref[pl.ds(at, 1), :], (8, 128))


def factor(c, gram, sigma, mx, ct, first, second, coef, yy, nat):
    lane = lax.broadcasted_iota(jnp.int32, (8, 128), 1)
    row = lax.broadcasted_iota(jnp.int32, (8, 128), 0)
    group = lane // 32
    g0, g1, g2 = group == 0, group == 1, group == 2

    def wide(mask, rows):
        return jnp.concatenate([mask] * (rows // 8), 0)

    def turn(x, by):
        return pltpu.roll(x, by, 1)

    padded = jnp.concatenate([c, jnp.broadcast_to(sigma, (96, ROWS_BASIS))], 0)
    ct[...] = padded.T
    sig_col = turn(ct[...], 96)
    sig_col = jnp.where(wide(lane, ROWS_BASIS) < 96, sig_col, turn(sig_col, 32))
    inv2 = 1.0 / (sig_col * sig_col)

    at = lax.broadcasted_iota(jnp.int32, (ROWS_BASIS, 128), 0)
    over = lax.broadcasted_iota(jnp.int32, (ROWS_BASIS, 128), 1)
    before = at < BLOCK * (over & 31)
    pick = over // 32
    masks = jnp.where(
        pick == 0, jnp.where(before, inv2 * inv2, 0.0),
        jnp.where(pick == 1, jnp.where(before, inv2, 0.0), jnp.where((pick == 2) & ~before, 1.0, 0.0)),
    )
    low = lax.broadcasted_iota(jnp.int32, (RANK, 128), 0)
    lanes = wide(group, RANK)
    for chunk in range(4):
        pairs = jnp.concatenate([c * c[a : a + 1] for a in range(chunk * 8, chunk * 8 + 8)], 0)
        sums = dot(pairs, masks)
        for i in range(8):
            a = chunk * 8 + i
            mx[a * STRIDE : a * STRIDE + RANK, :] = (
                sums[i * RANK : (i + 1) * RANK]
                + jnp.where((lanes == 1) & (low == a), 1.0, 0.0)
                + jnp.where(lanes == 2, jnp.broadcast_to(gram[:, a : a + 1], (RANK, 128)), 0.0)
            )
    fourth = []
    for half in range(2):
        mixed = jnp.concatenate([ct[pl.ds(half * 4 + t, 32, stride=8), :] for t in range(4)], 0).T
        for t in range(4):
            here = mixed if t == 0 else turn(mixed, 128 - 32 * t)
            r1 = here[:RANK]
            sig = here[RANK : 2 * RANK]
            r2 = sig * sig * r1
            mx[pl.ds(RANK + half * 4 + t, RANK, stride=STRIDE), :] = jnp.where(
                lanes == 0, r1, jnp.where(lanes == 2, -turn(r2, 64), 0.0)
            )
            sq = sig[:8] * sig[:8]
            fourth.append(sq * sq)

    acc = tuple(jnp.zeros((8, 128), F32) for _ in range(BLOCK))
    for part in range(8):
        start = part * 4
        skip = part // 2 * 8
        count = RANK - skip
        w0, w1, w2 = wide(g0, count), wide(g1, count), wide(g2, count)

        def step(k, acc):
            base = pl.multiple_of(k * STRIDE, 8)
            rk = mx[pl.ds(base + skip, count), :]
            ck = mx[pl.ds(skip * STRIDE + k, count, stride=STRIDE), :]
            pivot = spread_row(mx, base + k)
            up, down, across = turn(pivot, 32), turn(pivot, 96), turn(pivot, 64)
            p = jnp.where(g0, pivot, jnp.where(g1, up, across))
            e = jnp.where(g0, down, jnp.where(g1, pivot, up))
            q = jnp.where(g0, across, jnp.where(g1, down, pivot))
            det = 1.0 / (p * q + e * e)
            p, e, q = p * det, e * det, q * det
            pw, ew, qw = (jnp.concatenate([z] * (count // 8), 0) for z in (p, e, q))
            rk_up, rk_down, ck_down = turn(rk, 32), turn(rk, 96), turn(ck, 96)
            u = jnp.where(w2, rk_up, jnp.where(w1, rk, rk))
            v = jnp.where(w0, ck_down, jnp.where(w1, -rk_down, -rk))
            fa = qw * u + ew * v
            sa = ew * u - pw * v
            first[pl.ds(pl.multiple_of(k * RANK, 8) + skip, count), :] = fa
            second[pl.ds(pl.multiple_of(k * RANK, 8) + skip, count), :] = sa
            coef[0, skip:RANK, :] = jnp.where(w0, rk, jnp.where(w1, rk_up, -rk_up))
            coef[1, skip:RANK, :] = jnp.where(w0, ck_down, ck)
            right = mx[pl.ds(base + RANK, 8), :]
            swapped = turn(right, 64)
            u = jnp.where(g0, right, swapped)
            v = jnp.where(g0, -swapped, -right)
            fr = q * u + e * v
            sr = e * u - p * v
            yy[pl.ds(pl.multiple_of(k * 8, 8), 8), :] = jnp.where(g0, fr, turn(sr, 32))
            acc = tuple(
                acc[t]
                + jnp.broadcast_to(u[t : t + 1], (8, 128)) * fr
                + jnp.broadcast_to(v[t : t + 1], (8, 128)) * sr
                for t in range(BLOCK)
            )
            fall = jnp.concatenate([fa, fr], 0)
            sall = jnp.concatenate([sa, sr], 0)
            for i in range(start, RANK):
                f = jnp.broadcast_to(coef[0, i : i + 1, :], (8, 128))
                s = jnp.broadcast_to(coef[1, i : i + 1, :], (8, 128))
                for part8 in range(count // 8 + 1):
                    where = i * STRIDE + skip + part8 * 8
                    mx[where : where + 8, :] = mx[where : where + 8, :] - (
                        f * fall[part8 * 8 : part8 * 8 + 8] + s * sall[part8 * 8 : part8 * 8 + 8]
                    )
            return acc

        acc = lax.fori_loop(start, start + 4, step, acc)

    ys = [None] * RANK
    for k in range(RANK - 1, -1, -1):
        y = yy[k * 8 : k * 8 + 8, :]
        if k < RANK - 1:
            a1 = a2 = None
            for l in range(RANK - 1, k, -1):
                m1 = spread_row(first, k * RANK + l) * ys[l]
                m2 = spread_row(second, k * RANK + l) * ys[l]
                a1 = m1 if a1 is None else a1 + m1
                a2 = m2 if a2 is None else a2 + m2
            y = y - jnp.where(g0, a1 + turn(a1, 96), a2 + turn(a2, 32))
        ys[k] = y

    block = [acc[t] + jnp.where(row == t, fourth[t], 0.0) for t in range(BLOCK)]
    scale = jnp.zeros((8, 128), F32)
    steps = []
    for s in range(BLOCK):
        d = jnp.broadcast_to(block[s][s : s + 1], (8, 128))
        scale = jnp.where(row == s, lax.rsqrt(d), scale)
        ratio = jnp.where(row > s, block[s] / d, 0.0)
        steps.append(ratio)
        for t in range(s + 1, BLOCK):
            block[t] = block[t] - jnp.broadcast_to(block[s][t : t + 1], (8, 128)) * ratio
    for index in range(2 * RANK + BLOCK):
        if index < RANK:
            value = ys[index]
        elif index < 2 * RANK:
            value = turn(ys[index - RANK], 96)
        else:
            value = jnp.where(row == index - 2 * RANK, 1.0, 0.0)
        for s in range(BLOCK - 1):
            value = value - steps[s] * jnp.broadcast_to(value[s : s + 1], (8, 128))
        yy[index * 8 : index * 8 + 8, :] = value * scale
    for half in range(2):
        mixed = None
        for t in range(4):
            part = yy[pl.ds(half * 4 + t, 128, stride=8), :]
            part = part if t == 0 else turn(part, 32 * t)
            mixed = part if t == 0 else jnp.where(wide(group, 128) == t, part, mixed)
        mixed = mixed.T
        for t in range(4):
            nat[pl.ds(half * 4 + t, 32, stride=8), :] = mixed[32 * t : 32 * t + 32]

    inv_row = 1.0 / (sigma * sigma)
    weighed = jnp.concatenate([c * (inv_row * inv_row), c * inv_row], 0)
    across = lax.broadcasted_iota(jnp.int32, (ROWS_BASIS, ROWS_BASIS), 1)
    down = lax.broadcasted_iota(jnp.int32, (ROWS_BASIS, ROWS_BASIS), 0)
    tile = jnp.where(
        (lax.broadcasted_iota(jnp.int32, (BLOCK, ROWS_BASIS), 1) & 7)
        == lax.broadcasted_iota(jnp.int32, (BLOCK, ROWS_BASIS), 0), 1.0, 0.0
    )
    natural = nat[...]
    below = -dot(natural[:, : 2 * RANK], weighed)
    own = dot(natural[:, 2 * RANK : 2 * RANK + BLOCK], tile)
    inverse = jnp.where(across // 8 < down // 8, below, jnp.where(across // 8 == down // 8, own, 0.0))
    return inverse, sig_col


def batch_update(c, rounded, gram, sigma, *scratch):
    inverse, sig_col = factor(c, gram, sigma, *scratch)
    sig = jnp.concatenate([sig_col, sig_col], 1)
    on_snaps = dot(c, inverse, ((1,), (1,)))
    scaled = sig * sig * inverse.T
    total = scaled + dot(c, on_snaps, ((0,), (0,)))
    on_basis = scaled + dot(c - rounded, on_snaps, ((0,), (0,)))
    top = sig * total
    bottom = dot(c, total) + dot(gram, on_snaps)
    energy = jnp.sum(top * top, axis=0, keepdims=True) + jnp.sum(bottom * bottom, axis=0, keepdims=True)
    return on_basis, on_snaps, jnp.sqrt(energy)


def by_batch(x):
    return jnp.concatenate([x[16 * step + 8 * g : 16 * step + 8 * g + 8] for g in range(2) for step in range(4)], 0)


def small_kernel(
    rows_total, whole_ref, sigma_ref, fields_ref, mix_ref, sigma_out_ref, fields_out, half_uu, copy_sem, *scratch
):
    writing = pltpu.make_async_copy(fields_ref, fields_out, copy_sem)
    writing.start()
    scale = 1.0 / rows_total

    def piece(index):
        return whole_ref[64 * index : 64 * (index + 1), :] * scale

    high = lax.broadcasted_iota(jnp.int32, (64, 128), 1) >= 64
    last = piece(6)
    half_uu[...] = jnp.zeros((256, 256), F32)
    half_uu[0:64, 0:128] = jnp.where(high, 1.0, 0.5) * piece(2)
    half_uu[0:64, 128:256] = piece(3)
    half_uu[64:128, 0:128] = jnp.where(high, 0.5 * last, 0.0)
    half_uu[64:128, 128:256] = piece(4)
    half_uu[128:192, 128:256] = jnp.where(high, 1.0, 0.5) * piece(5)
    half_uu[192:256, 128:256] = jnp.where(high, 0.5 * pltpu.roll(last, 64, 1), 0.0)
    su = by_batch(jnp.concatenate([piece(0), piece(1)], 1))
    source = lax.broadcasted_iota(jnp.int32, (64, 64), 0)
    target = lax.broadcasted_iota(jnp.int32, (64, 64), 1)
    wanted = (target // 8 % 4) * 16 + (target // 32) * 8 + (target & 7)
    ss = dot(by_batch(piece(7)[:, :64]), jnp.where(source == wanted, 1.0, 0.0))
    s00, s10, s11 = ss[:32, :32], ss[32:, :32], ss[32:, 32:]

    def of_basis(x):
        part = dot(dot(x, half_uu[...]), x, ((1,), (1,)))
        return part + part.T

    def twice(c, r):
        part = dot(c, r, ((1,), (1,)))
        return part + part.T

    c0 = su[:32]
    r0 = c0.astype(BF16).astype(F32)
    gram0 = s00 - twice(c0, r0) + of_basis(r0)
    wu, ws, sigma1 = batch_update(c0, r0, gram0, sigma_ref[...], *scratch)
    c1 = dot(su[32:], wu) + dot(s10, ws)
    r1 = c1.astype(BF16).astype(F32)
    yu = dot(r1, wu, ((1,), (1,)))
    ys = dot(r1, ws, ((1,), (1,)))
    cross = dot(dot(ys, c0), yu, ((1,), (1,)))
    gram1 = s11 - twice(c1, r1) + of_basis(yu) + cross + cross.T + dot(dot(ys, s00), ys, ((1,), (1,)))
    wu1, ws1, sigma2 = batch_update(c1, r1, gram1, sigma1, *scratch)
    mix_ref[0:256, :] = dot(wu, wu1).astype(BF16)
    w0, w1 = dot(ws, wu1), ws1
    mix_ref[256:320, :] = jnp.concatenate(
        [w[8 * step : 8 * step + 8] for step in range(4) for w in (w0, w1)], 0
    ).astype(BF16)
    sigma_out_ref[...] = sigma2
    writing.wait()


def small_algebra(whole, sigma, fields, rows_total):
    return pl.pallas_call(
        lambda *refs: small_kernel(float(rows_total), *refs),
        out_shape=(jax.ShapeDtypeStruct((320, 256), BF16), jax.ShapeDtypeStruct((1, 256), F32), jax.ShapeDtypeStruct(fields.shape, F32)),
        in_specs=[pl.BlockSpec(memory_space=VMEM)] * 3,
        out_specs=(pl.BlockSpec(memory_space=VMEM),) * 2 + (pl.BlockSpec(memory_space=pltpu.HBM),),
        scratch_shapes=[
            VMEM((256, 256), F32),
            pltpu.SemaphoreType.DMA,
            VMEM((RANK * STRIDE, 128), F32),
            VMEM((256, 128), F32),
            VMEM((RANK * RANK, 128), F32),
            VMEM((RANK * RANK, 128), F32),
            VMEM((2, RANK, 128), F32),
            VMEM((128 * 8, 128), F32),
            VMEM((256, 128), F32),
        ],
        compiler_params=pltpu.CompilerParams(vmem_limit_bytes=32 * 1024 * 1024),
        name="small_algebra",
    )(whole, sigma.reshape(1, -1), fields)


def body(state_init, rock_type, perm_table, well_cells, well_rate, basis_in, singular):
    basis = basis_in.reshape(-1, basis_in.shape[-1])
    rows_total = basis.shape[0] * lax.axis_size("gx") * lax.axis_size("sec")
    final, snaps, whole = slab(perm_table, state_init, rock_type, well_cells.reshape(1, -1), well_rate, basis)
    mix, sigma, final = small_algebra(whole.reshape(-1, 128), singular, final, rows_total)
    fresh = rotate(basis, snaps, mix)
    return (final.reshape(state_init.shape), fresh.reshape(basis_in.shape), sigma.reshape(-1))


def solution(mesh):
    return jax.shard_map(
        body,
        mesh=mesh,
        in_specs=(
            P(None, "gx", "sec", None),
            P("gx", "sec"),
            P(),
            P(),
            P(),
            P(("gx", "sec"), None, None, None),
            P(),
        ),
        out_specs=(P(None, "gx", "sec", None), P(("gx", "sec"), None, None, None), P()),
        check_vma=False,
    )
```
